32 devices in a mesh: row: 4 (over y, x), col: 4 (over z), sea: 2 (over core).
Axes of the slice: x: 2, y: 2, z: 4, core: 2. Of those that a mesh axis runs over, the one named last changes fastest.
Arguments:
- kernel: bfloat16 [16, 4, 192, 768], P(None, None, 'col', 'row'), may hold values from -0.0546875 to 0.0546875
- history: bfloat16 [15, 4, 192, 512], P(None, None, 'col', 'sea'), may hold values from -6 to 6
- displacement: float32 [768, 512], P(('row', 'col'), 'sea'), may hold values from -6 to 6
- velocity: float32 [768, 512], P(('row', 'col'), 'sea'), may hold values from -6 to 6
- acceleration: float32 [768, 512], P(('row', 'col'), 'sea'), may hold values from -6 to 6
- excitation: float32 [3, 768, 512], P(None, ('row', 'col'), 'sea'), may hold values from -6 to 6
- solve_inverse: float32 [128, 6, 6], P(('row', 'col')), may hold values from -2.5 to 2.5
- stiffness: float32 [128, 6, 6], P(('row', 'col')), may hold values from -2.5 to 2.5
- owned: int32 [128], replicated, may hold values from 0 to 127, as said below
- links: int32 [128, 16], P(('row', 'col')), may hold values from 0 to 2047, as said below
- arms: float32 [128, 3, 16], P(('row', 'col')), may hold values from -1 to 1
Outputs:
- final_velocity: float32 [768, 512], P(('row', 'col'), 'sea')
- deck_gaps: float32 [128, 16, 3, 512], P(('row', 'col'), None, None, 'sea')
The draws below stay inside these ranges and needn't reach their ends.
Inputs may be any that keep to these rules, and one draw needn't show every extreme that they name: `owned`: A permutation of the 128 modules. Module m has its modes on the grid device m // 8 (row-major over row, col); its owner has the same col. The modules that one device sends to one owner number at most 4, exactly 4 wherever any are sent, and their list positions differ modulo 4. `links`: the partner point lies on another module listed to the same owner.
All inputs are finite; a program needn't handle non-finite values.
Results may differ from the reference program's by a relative error of at most 0.00037.
Values may be sent and summed in bfloat16 or wider, within the bound.
No kernel may reach another device: no remote copies, remote signals or barrier semaphores. Data moves between devices by JAX's collectives and lax.ppermute only.
A program may use at most 128 MiB of HBM per device.

```python
import jax
import jax.numpy as jnp
from jax import lax

MOD_DEV = 8
MODULES = 128
MODES = 768
POINTS = 16
LAGS = 16
STEPS = 3
REALS = 512
BLOCK = 192
CAP = 4
N_ROW = 4
N_COL = 4


def ownership_tables(key):
    base_key = jax.random.fold_in(key, 11)
    col_keys = jax.random.split(base_key, N_COL)

    def one_column(col_key):
        order_key, offset_key = jax.random.split(col_key)
        row_order = jax.random.permutation(order_key, N_ROW)
        row_inverse = jnp.argsort(row_order)
        offsets = jax.random.permutation(offset_key, N_ROW)[:N_ROW // 2]
        slot_range = jnp.arange(MOD_DEV)
        return (row_inverse[:, None] - offsets[slot_range // CAP][None, :]) % N_ROW
    sources = jax.vmap(one_column)(col_keys)
    col_range = jnp.arange(N_COL)
    modules = (sources * N_COL + col_range[:, None, None]) * MOD_DEV + jnp.arange(MOD_DEV)[None, None, :]
    owner_list = jnp.transpose(modules, (1, 0, 2)).reshape(MODULES)
    link_key_a, link_key_b = jax.random.split(jax.random.fold_in(key, 23))
    steps_ahead = jax.random.randint(link_key_a, (MODULES, POINTS), 1, MOD_DEV)
    partner_points = jax.random.randint(link_key_b, (MODULES, POINTS), 0, POINTS)
    positions = jnp.arange(MODULES)[:, None]
    partner_modules = positions // MOD_DEV * MOD_DEV + (positions % MOD_DEV + steps_ahead) % MOD_DEV
    link_table = partner_modules * POINTS + partner_points
    return (owner_list.astype(jnp.int32), link_table.astype(jnp.int32))


def draw_owned(key, part):
    return ownership_tables(key)[0]


def draw_links(key, part):
    return ownership_tables(key)[1]


def block_scale(rng, dims, cuts, smallest, top_value):
    def one(dim, blocks):
        heights = jax.random.uniform(jax.random.fold_in(jax.random.fold_in(rng, 6), dim), (blocks,), jnp.float32, smallest / len(cuts), top_value / len(cuts))
        return jnp.repeat(jnp.exp(heights), dims[dim] // blocks).reshape((-1,) + (1,) * (len(dims) - dim - 1))

    factor_of = one(*cuts[0])
    for cut in cuts[1:]:
        factor_of = factor_of * one(*cut)
    return factor_of


def centred(own_key, shape, spread, most, cuts=(), kind=jnp.bfloat16):
    loudness = block_scale(own_key, shape, cuts, -0.22, 0.18) if cuts else 1.0
    array = jax.random.normal(own_key, shape, jnp.float32) * spread * loudness
    return jnp.minimum(jnp.maximum(array, -most), most).astype(kind)


def setup_inputs(seed: int = 0) -> dict:
    splits = jax.random.split(jax.random.key(seed), 12)
    kernel = centred(splits[0], (LAGS, N_ROW, BLOCK, MODES), (LAGS * MODES) ** -0.5, 0.0546875, ((2, 4), (3, 4)))
    history = centred(splits[1], (LAGS - 1, N_ROW, BLOCK, REALS), 1.0, 6.0, ((2, 4), (3, 2)))
    displacement = centred(splits[2], (MODES, REALS), 1.0, 6.0, ((0, 16), (1, 2)), jnp.float32)
    velocity = centred(splits[3], (MODES, REALS), 1.0, 6.0, ((0, 16), (1, 2)), jnp.float32)
    acceleration = centred(splits[4], (MODES, REALS), 1.0, 6.0, ((0, 16), (1, 2)), jnp.float32)
    excitation = centred(splits[5], (STEPS, MODES, REALS), 1.0, 6.0, ((1, 16), (2, 2)), jnp.float32)
    solve_inverse = centred(splits[6], (MODULES, 6, 6), 6 ** -0.5, 2.5, ((0, 16),), jnp.float32)
    stiffness = centred(splits[7], (MODULES, 6, 6), 6 ** -0.5, 2.5, ((0, 16),), jnp.float32)
    owned = draw_owned(jax.random.fold_in(splits[11], 71), 0)
    links = draw_links(jax.random.fold_in(splits[11], 71), 0)
    arms = jnp.clip(jax.random.uniform(splits[10], (MODULES, 3, POINTS), jnp.float32, -1.0, 1.0) * block_scale(splits[10], (MODULES, 3, POINTS), ((0, 16),), -0.4, 0.0), -1.0, 1.0)
    return dict(kernel=kernel, history=history, displacement=displacement, velocity=velocity, acceleration=acceleration, excitation=excitation, solve_inverse=solve_inverse, stiffness=stiffness, owned=owned, links=links, arms=arms)


DT = 0.5
QUARTER = DT * DT / 4.0


def blocks(matrix, vector):
    return jnp.einsum('mab,mbr->mar', matrix, vector, precision=lax.Precision.HIGHEST)


def newmark(displacement, velocity, acceleration, force_now, excitation_now, solve_inverse, stiffness):
    block_shape = (displacement.shape[0] // 6, 6, displacement.shape[1])
    predicted = displacement + DT * velocity + QUARTER * acceleration
    load_total = excitation_now - force_now - blocks(stiffness, predicted.reshape(block_shape)).reshape(displacement.shape)
    accel_next = blocks(solve_inverse, load_total.reshape(block_shape)).reshape(displacement.shape)
    return predicted + QUARTER * accel_next, velocity + 0.5 * DT * (acceleration + accel_next), accel_next


def deck_motion(motion, levers):
    moving = motion[:, 0:3, None, :]
    turning = motion[:, 3:6, None, :]
    arm_all = levers[:, :, :, None]
    surge_motion = moving[:, 0] + turning[:, 1] * arm_all[:, 2] - turning[:, 2] * arm_all[:, 1]
    sway_motion = moving[:, 1] + turning[:, 2] * arm_all[:, 0] - turning[:, 0] * arm_all[:, 2]
    heave_motion = moving[:, 2] + turning[:, 0] * arm_all[:, 1] - turning[:, 1] * arm_all[:, 0]
    return jnp.stack([surge_motion, sway_motion, heave_motion], axis=2)


def radiation(kernel, window):
    def add_lag(running, lag_pair):
        lag_kernel, lag_window = lag_pair
        flat_kernel = lag_kernel.reshape(MODES, MODES)
        flat_window = lag_window.reshape(MODES, REALS)
        return running + lax.dot_general(flat_kernel, flat_window, (((0,), (0,)), ((), ())), preferred_element_type=jnp.float32), None
    running, unused = lax.scan(add_lag, jnp.zeros((MODES, REALS), jnp.float32), (kernel, window))
    return running


def reference(kernel, history, displacement, velocity, acceleration, excitation, solve_inverse, stiffness, owned, links, arms):
    window = history
    for step_index in range(STEPS):
        newest = velocity.astype(jnp.bfloat16).reshape(1, N_ROW, BLOCK, REALS)
        window = jnp.concatenate([newest, window[:LAGS - 1]], axis=0)
        force_now = radiation(kernel, window)
        displacement, velocity, acceleration = newmark(displacement, velocity, acceleration, force_now, excitation[step_index], solve_inverse, stiffness)
    motion = displacement.reshape(MODULES, 6, REALS)
    owned_motion = jnp.take(motion, owned.astype(jnp.int32), axis=0)
    points = deck_motion(owned_motion, arms).reshape(MODULES * POINTS, 3, REALS)
    partner = jnp.take(points, links.reshape(-1).astype(jnp.int32), axis=0)
    deck_gaps = (points - partner).reshape(MODULES, POINTS, 3, REALS)
    return (velocity, deck_gaps)
```

```python
import functools

import jax
import jax.numpy as jnp
from jax import lax
from jax.experimental import pallas as pl
from jax.experimental.pallas import tpu as pltpu
from jax.sharding import PartitionSpec as P


DT = 0.5
QUARTER = DT * DT / 4.0
F32 = jnp.float32
BF16 = jnp.bfloat16
HIGHEST = lax.Precision.HIGHEST
VMEM = pl.BlockSpec(memory_space=pltpu.VMEM)
SMEM = pl.BlockSpec(memory_space=pltpu.SMEM)


def sends_to(i, d, n):
    return i ^ d if n & (n - 1) == 0 else (i + d) % n


def comes_from(i, d, n):
    return i ^ d if n & (n - 1) == 0 else (i + n - d) % n


def exchange(pieces, axis):
    n = lax.axis_size(axis)
    out = [pieces[0]]
    for d in range(1, n):
        out.append(lax.ppermute(pieces[d], axis, [(i, sends_to(i, d, n)) for i in range(n)]))
    return out


def dot_rows(a, b):
    return lax.dot_general(a, b, (((0,), (0,)), ((), ())), preferred_element_type=F32)


def dot_exact(a, b):
    return jnp.dot(a, b, precision=HIGHEST, preferred_element_type=F32)


def call(body, shapes, in_specs, args, flops, nbytes, scratch=()):
    return pl.pallas_call(
        body,
        out_shape=shapes,
        in_specs=in_specs,
        out_specs=jax.tree.map(lambda _: VMEM, shapes),
        scratch_shapes=scratch,
        cost_estimate=pl.CostEstimate(flops=flops, bytes_accessed=nbytes, transcendentals=0),
    )(*args)


def known_kernel(lag_rows, steps, k_ref, h_ref, *outs):
    total = k_ref.shape[0]
    for s in range(steps):
        first = (s + 1) * lag_rows
        outs[s][...] = dot_rows(k_ref[first:, :], h_ref[: total - first, :])


def known_forces(kernel_flat, history_flat, lag_rows, steps):
    shape = jax.ShapeDtypeStruct((kernel_flat.shape[1], history_flat.shape[1]), F32)
    return call(
        functools.partial(known_kernel, lag_rows, steps),
        (shape,) * steps,
        [VMEM, VMEM],
        (kernel_flat, history_flat),
        2 * steps * kernel_flat.size * history_flat.shape[1],
        2 * (kernel_flat.size + history_flat.size),
    )


def force_kernel(rows, cols, ahead, *refs):
    at, k_ref = refs[0], refs[1]
    arrived = refs[2 : 2 + rows]
    bases = refs[2 + rows : 2 + rows + ahead]
    outs = refs[2 + rows + ahead : -2]
    chunks, later = outs[:cols], outs[cols:]
    whole, total = refs[-2:]
    slab = arrived[0].shape[0]
    for d in range(rows):
        start = pl.multiple_of(comes_from(at[0], d, rows) * slab, 16)
        whole[pl.ds(start, slab), :] = arrived[d][...]
    lag_rows = rows * slab
    total[...] = bases[0][...] + dot_rows(k_ref[:lag_rows, :], whole[...])
    for d in range(cols):
        start = pl.multiple_of(sends_to(at[1], d, cols) * slab, 8)
        chunks[d][...] = total[pl.ds(start, slab), :]
    for n in range(1, ahead):
        later[n - 1][...] = bases[n][...] + dot_rows(
            k_ref[n * lag_rows : (n + 1) * lag_rows, :], whole[...]
        )


def force_pieces(at, kernel_lags, arrived, bases, cols):
    rows, ahead = len(arrived), len(bases)
    slab, reals = arrived[0].shape
    block = kernel_lags.shape[1]
    shapes = (jax.ShapeDtypeStruct((slab, reals), F32),) * cols + (
        jax.ShapeDtypeStruct((block, reals), F32),
    ) * (ahead - 1)
    out = call(
        functools.partial(force_kernel, rows, cols, ahead),
        shapes,
        [SMEM] + [VMEM] * (1 + rows + ahead),
        (at, kernel_lags, *arrived, *bases),
        2 * ahead * rows * slab * block * reals,
        4 * 2 * ahead * block * reals,
        [pltpu.VMEM((rows * slab, reals), BF16), pltpu.VMEM((block, reals), F32)],
    )
    return out[:cols], out[cols:]


def prepare_kernel(x, v, a, e, stiff, predicted, load):
    p = x[...] + DT * v[...] + QUARTER * a[...]
    predicted[...] = p
    load[...] = e[...] - dot_exact(stiff[...], p)


def prepare(x, v, a, e, stiff):
    shape = jax.ShapeDtypeStruct(x.shape, F32)
    return call(
        prepare_kernel, (shape, shape), [VMEM] * 5, (x, v, a, e, stiff),
        12 * x.size * x.shape[0], 24 * x.size,
    )


def advance_kernel(cols, *refs):
    parts = refs[:cols]
    predicted, v, a, load, inverse = refs[cols : cols + 5]
    x_out, v_out, a_out, v_half = refs[cols + 5 :]
    force = parts[0][...]
    for part in parts[1:]:
        force = force + part[...]
    a_next = dot_exact(inverse[...], load[...] - force)
    v_next = v[...] + 0.5 * DT * (a[...] + a_next)
    v_half[...] = v_next.astype(BF16)
    v_out[...] = v_next
    a_out[...] = a_next
    x_out[...] = predicted[...] + QUARTER * a_next


def advance(parts, predicted, v, a, load, inverse):
    shape = jax.ShapeDtypeStruct(v.shape, F32)
    return call(
        functools.partial(advance_kernel, len(parts)),
        (shape, shape, shape, jax.ShapeDtypeStruct(v.shape, BF16)),
        [VMEM] * (len(parts) + 5),
        (*parts, predicted, v, a, load, inverse),
        12 * v.size * v.shape[0], 40 * v.size,
    )


def finish_kernel(cols, rows, *refs):
    parts = refs[:cols]
    predicted, v, a, load, inverse, route = refs[cols : cols + 6]
    v_out, *sends = refs[cols + 6 :]
    force = parts[0][...]
    for part in parts[1:]:
        force = force + part[...]
    a_next = dot_exact(inverse[...], load[...] - force)
    v_out[...] = v[...] + 0.5 * DT * (a[...] + a_next)
    x_next = predicted[...] + QUARTER * a_next
    for d in range(rows):
        sends[d][...] = dot_exact(route[d], x_next)


def finish(parts, predicted, v, a, load, inverse, route):
    rows, slots = route.shape[0], route.shape[1]
    shapes = (jax.ShapeDtypeStruct(v.shape, F32),) + (
        jax.ShapeDtypeStruct((slots, v.shape[1]), F32),
    ) * rows
    out = call(
        functools.partial(finish_kernel, len(parts), rows),
        shapes,
        [VMEM] * (len(parts) + 6),
        (*parts, predicted, v, a, load, inverse, route),
        12 * v.size * v.shape[0], 40 * v.size,
    )
    return out[0], out[1:]


def gaps_kernel(rows, *refs):
    weights, arrived, out = refs[0], refs[1 : 1 + rows], refs[-1]
    total = dot_exact(weights[0], arrived[0][...])
    for d in range(1, rows):
        total = total + dot_exact(weights[d], arrived[d][...])
    out[...] = total


def gaps(weights, arrived):
    points, reals = weights.shape[1], arrived[0].shape[1]
    return call(
        functools.partial(gaps_kernel, len(arrived)),
        jax.ShapeDtypeStruct((points, reals), F32),
        [VMEM] * (1 + len(arrived)),
        (weights, *arrived),
        12 * weights.size * reals, 4 * points * reals,
    )


def block_diagonal(matrix):
    count = matrix.shape[0]
    spread = jnp.eye(count, dtype=F32)[:, None, :, None] * matrix[:, :, None, :]
    return spread.reshape(6 * count, 6 * count)


def routing(owned, grid_index, row, rows, cols, modules):
    capacity = 2 * modules // rows
    six = jnp.arange(6)
    local_ids = grid_index * modules + jnp.arange(modules, dtype=jnp.int32)
    list_range = jnp.arange(owned.shape[0], dtype=jnp.int32)
    positions = jnp.sum(
        jnp.where(owned[None, :] == local_ids[:, None], list_range[None, :], 0), axis=1
    )
    target_row = positions // (cols * modules)
    target_slot = positions % modules % capacity
    order = jnp.arange(rows, dtype=jnp.int32)
    slots = jnp.arange(capacity, dtype=jnp.int32)
    same = (six[:, None] == six[None, :])
    to_row = sends_to(row, order, rows)
    send = (to_row[:, None, None] == target_row[None, None, :]) & (
        slots[None, :, None] == target_slot[None, None, :]
    )
    send = send[:, :, None, :, None] & same[None, None, :, None, :]
    owned_here = lax.dynamic_slice_in_dim(owned, grid_index * modules, modules, 0)
    home_row = owned_here // (cols * modules)
    list_slot = jnp.arange(modules, dtype=jnp.int32) % capacity
    from_row = comes_from(row, order, rows)
    take = (from_row[:, None, None] == home_row[None, :, None]) & (
        slots[None, None, :] == list_slot[None, :, None]
    )
    return (
        send.astype(F32).reshape(rows, capacity * 6, modules * 6),
        take.astype(F32),
    )


def gap_weights(take, links, arms, grid_index):
    rows, modules, capacity = take.shape
    points = arms.shape[2]
    zero, one = jnp.zeros_like(arms[:, 0, :]), jnp.ones_like(arms[:, 0, :])
    e1, e2, e3 = arms[:, 0, :], arms[:, 1, :], arms[:, 2, :]
    lever = jnp.stack(
        [
            jnp.stack([one, zero, zero, zero, e3, -e2], axis=-1),
            jnp.stack([zero, one, zero, -e3, zero, e1], axis=-1),
            jnp.stack([zero, zero, one, e2, -e1, zero], axis=-1),
        ],
        axis=2,
    )
    flat = lever.reshape(modules * points, 18)
    local = (links - grid_index * modules * points).reshape(-1)
    meets = (local[:, None] == jnp.arange(modules * points, dtype=jnp.int32)[None, :]).astype(F32)
    partner = jnp.dot(meets, flat, precision=HIGHEST)
    own_module = jnp.arange(modules * points, dtype=jnp.int32) // points
    partner_module = local // points
    order = jnp.arange(modules, dtype=jnp.int32)
    own_take = jnp.einsum("qm,dms->dqs", (own_module[:, None] == order).astype(F32), take, precision=HIGHEST)
    partner_take = jnp.einsum("qm,dms->dqs", (partner_module[:, None] == order).astype(F32), take, precision=HIGHEST)
    flat = flat.reshape(1, modules, points, 3, 1, 6)
    partner = partner.reshape(1, modules, points, 3, 1, 6)
    own_take = own_take.reshape(rows, modules, points, 1, capacity, 1)
    partner_take = partner_take.reshape(rows, modules, points, 1, capacity, 1)
    weights = own_take * flat - partner_take * partner
    return weights.transpose(0, 1, 3, 2, 4, 5).reshape(rows, modules * 3 * points, capacity * 6)


def body(
    kernel,
    history,
    displacement,
    velocity,
    acceleration,
    excitation,
    solve_inverse,
    stiffness,
    owned,
    links,
    arms,
):
    rows, cols = lax.axis_size("row"), lax.axis_size("col")
    row, col = lax.axis_index("row"), lax.axis_index("col")
    grid_index = row * cols + col
    at = jnp.stack([row, col]).astype(jnp.int32)
    steps = excitation.shape[0]
    slab = velocity.shape[0]
    modules = slab // 6
    points = arms.shape[2]
    reals = velocity.shape[1]
    lag_rows = rows * slab
    kernel_flat = kernel.reshape(-1, kernel.shape[3])
    history_flat = history.reshape(-1, reals)
    x, v, a = displacement, velocity, acceleration
    v_half = v.astype(BF16)
    arrived = exchange([v_half] * rows, "row")
    bases = known_forces(kernel_flat, history_flat, lag_rows, steps)
    inverse, stiff = block_diagonal(solve_inverse), block_diagonal(stiffness)
    send, take = routing(owned, grid_index, row, rows, cols, modules)
    weights = gap_weights(take, links, arms, grid_index)
    kernel_lags = kernel[:steps].reshape(-1, kernel.shape[3])
    for n in range(steps):
        predicted, load = prepare(x, v, a, excitation[n], stiff)
        pieces, bases = force_pieces(at, kernel_lags, arrived, bases, cols)
        parts = exchange(pieces, "col")
        if n < steps - 1:
            x, v, a, v_half = advance(parts, predicted, v, a, load, inverse)
            arrived = exchange([v_half] * rows, "row")
        else:
            v, sends = finish(parts, predicted, v, a, load, inverse, send)
    moved = exchange(sends, "row")
    out = gaps(weights, moved).reshape(modules, 3, points, reals)
    return v, out.transpose(0, 2, 1, 3)


def solution(mesh):
    placed = (
        P(None, None, "col", "row"),
        P(None, None, "col", "sea"),
        P(("row", "col"), "sea"),
        P(("row", "col"), "sea"),
        P(("row", "col"), "sea"),
        P(None, ("row", "col"), "sea"),
        P(("row", "col"), None, None),
        P(("row", "col"), None, None),
        P(),
        P(("row", "col"), None),
        P(("row", "col"), None, None),
    )
    return jax.shard_map(
        body,
        mesh=mesh,
        in_specs=placed,
        out_specs=(P(("row", "col"), "sea"), P(("row", "col"), None, None, "sea")),
        check_vma=False,
    )
```

```python
import functools

import jax
import jax.numpy as jnp
from jax import lax
from jax.experimental import pallas as pl
from jax.experimental.pallas import tpu as pltpu
from jax.sharding import PartitionSpec as P


DT = 0.5
QUARTER = DT * DT / 4.0
F32 = jnp.float32
BF16 = jnp.bfloat16
HIGHEST = lax.Precision.HIGHEST
VMEM = pl.BlockSpec(memory_space=pltpu.VMEM)
SMEM = pl.BlockSpec(memory_space=pltpu.SMEM)


def sends_to(i, d, n):
    return i ^ d if n & (n - 1) == 0 else (i + d) % n


def comes_from(i, d, n):
    return i ^ d if n & (n - 1) == 0 else (i + n - d) % n


def exchange(pieces, axis):
    n = lax.axis_size(axis)
    out = [pieces[0]]
    for d in range(1, n):
        out.append(lax.ppermute(pieces[d], axis, [(i, sends_to(i, d, n)) for i in range(n)]))
    return out


def dot_rows(a, b):
    return lax.dot_general(a, b, (((0,), (0,)), ((), ())), preferred_element_type=F32)


def dot_exact(a, b):
    return jnp.dot(a, b, precision=HIGHEST, preferred_element_type=F32)


def padded_bytes(shape, dtype):
    size = jnp.dtype(dtype).itemsize
    dims = (1, 1, *shape)
    up = lambda n, m: -(-n // m) * m
    major = 1
    for n in dims[:-2]:
        major *= n
    return major * up(dims[-2], 32 // size) * up(dims[-1], 128) * size


def call(body, shapes, in_specs, args, flops, nbytes, scratch=()):
    arrays = list(args) + jax.tree.leaves(shapes)
    held = sum(padded_bytes(t.shape, t.dtype) for t in arrays)
    held += sum(padded_bytes(t.shape, t.dtype) for t in scratch)
    return pl.pallas_call(
        body,
        out_shape=shapes,
        in_specs=in_specs,
        out_specs=jax.tree.map(lambda _: VMEM, shapes),
        scratch_shapes=scratch,
        compiler_params=pltpu.CompilerParams(vmem_limit_bytes=min(2 * held + (2 << 20), 60 << 20)),
        cost_estimate=pl.CostEstimate(flops=flops, bytes_accessed=nbytes, transcendentals=0),
    )(*args)


def known_kernel(lag_rows, steps, k_ref, h_ref, lags_ref, *outs):
    total = k_ref.shape[0]
    lags_ref[...] = k_ref[: steps * lag_rows, :]
    for s in range(steps):
        first = (s + 1) * lag_rows
        outs[s][...] = dot_rows(k_ref[first:, :], h_ref[: total - first, :])


def known_forces(kernel_flat, history_flat, lag_rows, steps):
    block = kernel_flat.shape[1]
    shape = jax.ShapeDtypeStruct((block, history_flat.shape[1]), F32)
    out = call(
        functools.partial(known_kernel, lag_rows, steps),
        (jax.ShapeDtypeStruct((steps * lag_rows, block), BF16),) + (shape,) * steps,
        [VMEM, VMEM],
        (kernel_flat, history_flat),
        2 * steps * kernel_flat.size * history_flat.shape[1],
        2 * (kernel_flat.size + history_flat.size),
    )
    return out[0], out[1:]


def force_kernel(rows, cols, ahead, *refs):
    k_ref = refs[0]
    arrived = refs[1 : 1 + rows]
    bases = refs[1 + rows : 1 + rows + ahead]
    outs = refs[1 + rows + ahead : -2]
    chunks, later = outs[:cols], outs[cols:]
    whole, total = refs[-2:]
    slab = arrived[0].shape[0]
    row, col = lax.axis_index("row"), lax.axis_index("col")
    for d in range(rows):
        start = pl.multiple_of(comes_from(row, d, rows) * slab, 16)
        whole[pl.ds(start, slab), :] = arrived[d][...]
    lag_rows = rows * slab
    total[...] = bases[0][...] + dot_rows(k_ref[:lag_rows, :], whole[...])
    for d in range(cols):
        start = pl.multiple_of(sends_to(col, d, cols) * slab, 8)
        chunks[d][...] = total[pl.ds(start, slab), :]
    for n in range(1, ahead):
        later[n - 1][...] = bases[n][...] + dot_rows(
            k_ref[n * lag_rows : (n + 1) * lag_rows, :], whole[...]
        )


def force_pieces(kernel_lags, arrived, bases, cols):
    rows, ahead = len(arrived), len(bases)
    slab, reals = arrived[0].shape
    block = kernel_lags.shape[1]
    shapes = (jax.ShapeDtypeStruct((slab, reals), F32),) * cols + (
        jax.ShapeDtypeStruct((block, reals), F32),
    ) * (ahead - 1)
    out = call(
        functools.partial(force_kernel, rows, cols, ahead),
        shapes,
        [VMEM] * (1 + rows + ahead),
        (kernel_lags, *arrived, *bases),
        2 * ahead * rows * slab * block * reals,
        4 * 2 * ahead * block * reals,
        [pltpu.VMEM((rows * slab, reals), BF16), pltpu.VMEM((block, reals), F32)],
    )
    return out[:cols], out[cols:]


def prepare_kernel(x, v, a, e, stiff, predicted, load):
    p = x[...] + DT * v[...] + QUARTER * a[...]
    predicted[...] = p
    load[...] = e[...] - dot_exact(stiff[...], p)


def prepare(x, v, a, e, stiff):
    shape = jax.ShapeDtypeStruct(x.shape, F32)
    return call(
        prepare_kernel, (shape, shape), [VMEM] * 5, (x, v, a, e, stiff),
        12 * x.size * x.shape[0], 24 * x.size,
    )


def advance_kernel(cols, *refs):
    parts = refs[:cols]
    predicted, v, a, load, inverse = refs[cols : cols + 5]
    x_out, v_out, a_out, v_half = refs[cols + 5 :]
    force = parts[0][...]
    for part in parts[1:]:
        force = force + part[...]
    a_next = dot_exact(inverse[...], load[...] - force)
    v_next = v[...] + 0.5 * DT * (a[...] + a_next)
    v_half[...] = v_next.astype(BF16)
    v_out[...] = v_next
    a_out[...] = a_next
    x_out[...] = predicted[...] + QUARTER * a_next


def advance(parts, predicted, v, a, load, inverse):
    shape = jax.ShapeDtypeStruct(v.shape, F32)
    return call(
        functools.partial(advance_kernel, len(parts)),
        (shape, shape, shape, jax.ShapeDtypeStruct(v.shape, BF16)),
        [VMEM] * (len(parts) + 5),
        (*parts, predicted, v, a, load, inverse),
        12 * v.size * v.shape[0], 40 * v.size,
    )


def finish_kernel(cols, rows, *refs):
    parts = refs[:cols]
    predicted, v, a, load, inverse, route = refs[cols : cols + 6]
    v_out, *sends = refs[cols + 6 :]
    force = parts[0][...]
    for part in parts[1:]:
        force = force + part[...]
    a_next = dot_exact(inverse[...], load[...] - force)
    v_out[...] = v[...] + 0.5 * DT * (a[...] + a_next)
    x_next = predicted[...] + QUARTER * a_next
    moved = dot_exact(route[...], x_next)
    size = route.shape[0] // rows
    for d in range(rows):
        sends[d][...] = moved[d * size : (d + 1) * size, :]


def finish(parts, predicted, v, a, load, inverse, route, rows):
    shapes = (jax.ShapeDtypeStruct(v.shape, F32),) + (
        jax.ShapeDtypeStruct((route.shape[0] // rows, v.shape[1]), F32),
    ) * rows
    out = call(
        functools.partial(finish_kernel, len(parts), rows),
        shapes,
        [VMEM] * (len(parts) + 6),
        (*parts, predicted, v, a, load, inverse, route),
        12 * v.size * v.shape[0], 40 * v.size,
    )
    return out[0], out[1:]


def gaps_kernel(rows, *refs):
    weights, arrived, out, held = refs[0], refs[1 : 1 + rows], refs[-2], refs[-1]
    size = arrived[0].shape[0]
    for d in range(rows):
        held[d * size : (d + 1) * size, :] = arrived[d][...]
    out[...] = dot_exact(weights[...], held[...])


def gaps(weights, arrived):
    points, reals = weights.shape[0], arrived[0].shape[1]
    return call(
        functools.partial(gaps_kernel, len(arrived)),
        jax.ShapeDtypeStruct((points, reals), F32),
        [VMEM] * (1 + len(arrived)),
        (weights, *arrived),
        12 * weights.size * reals, 4 * points * reals,
        [pltpu.VMEM((weights.shape[1], reals), F32)],
    )


def diagonals_kernel(*refs):
    half = len(refs) // 2
    for blocks, out in zip(refs[:half], refs[half:]):
        modules = blocks.shape[1]
        width = 6 * modules
        lane = lax.broadcasted_iota(jnp.int32, (modules, width), 1) // 6
        module = lax.broadcasted_iota(jnp.int32, (modules, width), 0)
        for i in range(6):
            spread = jnp.concatenate([blocks[i]] * modules, axis=1)
            out[pl.ds(i, modules, stride=6), :] = jnp.where(lane == module, spread, 0.0)


def diagonals(*matrices):
    width = 6 * matrices[0].shape[0]
    shape = jax.ShapeDtypeStruct((width, width), F32)
    return call(
        diagonals_kernel, (shape,) * len(matrices), [VMEM] * len(matrices),
        tuple(m.transpose(1, 0, 2) for m in matrices), 100 * width * width, 16 * width * width,
    )


def plan_kernel(rows, cols, capacity, slot_rows, owned, links, arms, send, weights, table):
    modules = send.shape[1] // 6
    points = links.shape[0] // modules
    row, col = lax.axis_index("row"), lax.axis_index("col")
    grid_index = row * cols + col
    first_module = grid_index * modules
    shape = (slot_rows, modules * 6)
    i = lax.broadcasted_iota(jnp.int32, shape, 0)
    j = lax.broadcasted_iota(jnp.int32, shape, 1)
    for d in range(rows):
        listed = (sends_to(row, d, rows) * cols + col) * modules
        wanted = jnp.full(shape, -1, jnp.int32)
        for k in range(modules):
            local = owned[listed + k] - first_module
            here = (local >= 0) & (local < modules)
            wanted = jnp.where((i // 6 == k % capacity) & here, local, wanted)
        hit = (wanted == j // 6) & (i % 6 == j % 6)
        send[d * slot_rows : (d + 1) * slot_rows, :] = jnp.where(hit, 1.0, 0.0)
    count = modules * points
    table[:, 0:3] = arms[...]
    for q in range(modules):
        home = owned[first_module + q] // (cols * modules)
        home_d = home ^ row if rows & (rows - 1) == 0 else (row + rows - home) % rows
        place = home_d * slot_rows + (q % capacity) * 6
        table[q * points : (q + 1) * points, 3:4] = jnp.full((points, 1), place, jnp.int32).astype(F32)
    own = table[...]
    point = lax.broadcasted_iota(jnp.int32, (count, count), 1)
    meets = jnp.where(links[...] - first_module * points == point, 1.0, 0.0)
    partner = dot_exact(meets, own)
    wide = (count, rows * slot_rows)
    column = lax.broadcasted_iota(jnp.int32, wide, 1)
    total = [None] * 3
    for sign, side in ((1.0, own), (-1.0, partner)):
        mode = column - (side[:, 3:4] + 0.5).astype(jnp.int32)
        e = [jnp.broadcast_to(sign * side[:, c : c + 1], wide) for c in range(3)]
        for c in range(3):
            up, down = (c + 1) % 3, (c + 2) % 3
            value = jnp.where(mode == c, sign, 0.0)
            value = jnp.where(mode == 3 + up, e[down], value)
            value = jnp.where(mode == 3 + down, -e[up], value)
            total[c] = value if total[c] is None else total[c] + value
    for q in range(modules):
        for c in range(3):
            start = (q * 3 + c) * points
            weights[start : start + points, :] = total[c][q * points : (q + 1) * points, :]


def plan(owned, links, arms, rows, cols):
    modules, points = links.shape
    capacity = 2 * modules // rows
    slot_rows = -(-capacity * 6 // 8) * 8
    return call(
        functools.partial(plan_kernel, rows, cols, capacity, slot_rows),
        (
            jax.ShapeDtypeStruct((rows * slot_rows, modules * 6), F32),
            jax.ShapeDtypeStruct((modules * 3 * points, rows * slot_rows), F32),
        ),
        [SMEM, VMEM, VMEM],
        (owned, links.reshape(-1, 1), arms.transpose(0, 2, 1).reshape(-1, 3)),
        12 * (modules * points) ** 2 * 4, 4 * modules * 3 * points * rows * slot_rows,
        [pltpu.VMEM((modules * points, 4), F32)],
    )


def after(value, *others):
    return lax.optimization_barrier((value, *others))[0]


def body(
    kernel,
    history,
    displacement,
    velocity,
    acceleration,
    excitation,
    solve_inverse,
    stiffness,
    owned,
    links,
    arms,
):
    rows, cols = lax.axis_size("row"), lax.axis_size("col")
    steps = excitation.shape[0]
    slab, reals = velocity.shape
    modules, points = links.shape
    x, v, a = displacement, velocity, acceleration
    arrived = exchange([v.astype(BF16)] * rows, "row")
    lags, bases = known_forces(
        kernel.reshape(-1, kernel.shape[3]), history.reshape(-1, reals), rows * slab, steps
    )
    inverse, stiff = diagonals(solve_inverse, stiffness)
    for n in range(steps):
        predicted, load = prepare(x, v, a, excitation[n], stiff)
        pieces, bases = force_pieces(lags, arrived, bases, cols)
        if n == 0:
            send, weights = plan(after(owned, pieces[0]), links, arms, rows, cols)
        parts = exchange(pieces, "col")
        if n < steps - 1:
            x, v, a, v_half = advance(parts, predicted, v, a, load, inverse)
            arrived = exchange([v_half] * rows, "row")
        else:
            v, sends = finish(parts, predicted, v, a, load, inverse, send, rows)
    moved = exchange(sends, "row")
    out = gaps(weights, moved).reshape(modules, 3, points, reals)
    return v, out.transpose(0, 2, 1, 3)


def solution(mesh):
    placed = (
        P(None, None, "col", "row"),
        P(None, None, "col", "sea"),
        P(("row", "col"), "sea"),
        P(("row", "col"), "sea"),
        P(("row", "col"), "sea"),
        P(None, ("row", "col"), "sea"),
        P(("row", "col"), None, None),
        P(("row", "col"), None, None),
        P(),
        P(("row", "col"), None),
        P(("row", "col"), None, None),
    )
    return jax.shard_map(
        body,
        mesh=mesh,
        in_specs=placed,
        out_specs=(P(("row", "col"), "sea"), P(("row", "col"), None, None, "sea")),
        check_vma=False,
    )
```

```python
import functools

import jax
import jax.numpy as jnp
from jax import lax
from jax.experimental import pallas as pl
from jax.experimental.pallas import tpu as pltpu
from jax.sharding import PartitionSpec as P


DT = 0.5
QUARTER = DT * DT / 4.0
F32 = jnp.float32
BF16 = jnp.bfloat16
HIGHEST = lax.Precision.HIGHEST
VMEM = pl.BlockSpec(memory_space=pltpu.VMEM)
SMEM = pl.BlockSpec(memory_space=pltpu.SMEM)


def sends_to(i, d, n):
    return i ^ d if n & (n - 1) == 0 else (i + d) % n


def comes_from(i, d, n):
    return i ^ d if n & (n - 1) == 0 else (i + n - d) % n


def exchange(pieces, axis):
    n = lax.axis_size(axis)
    out = [pieces[0]] + [None] * (n - 1)
    for d in range(n - 1, 0, -1):
        out[d] = lax.ppermute(pieces[d], axis, [(i, sends_to(i, d, n)) for i in range(n)])
    return out


def dot_rows(a, b):
    return lax.dot_general(a, b, (((0,), (0,)), ((), ())), preferred_element_type=F32)


def dot_exact(a, b):
    return jnp.dot(a, b, precision=HIGHEST, preferred_element_type=F32)


def padded_bytes(shape, dtype):
    size = jnp.dtype(dtype).itemsize
    dims = (1, 1, *shape)
    up = lambda n, m: -(-n // m) * m
    major = 1
    for n in dims[:-2]:
        major *= n
    return major * up(dims[-2], 32 // size) * up(dims[-1], 128) * size


def call(body, shapes, in_specs, args, flops, nbytes, scratch=()):
    arrays = list(args) + jax.tree.leaves(shapes)
    held = sum(padded_bytes(t.shape, t.dtype) for t in arrays)
    held += sum(padded_bytes(t.shape, t.dtype) for t in scratch if t.shape[1:])
    return pl.pallas_call(
        body,
        out_shape=shapes,
        in_specs=in_specs,
        out_specs=jax.tree.map(lambda _: VMEM, shapes),
        scratch_shapes=scratch,
        compiler_params=pltpu.CompilerParams(vmem_limit_bytes=min(2 * held + (2 << 20), 60 << 20)),
        cost_estimate=pl.CostEstimate(flops=flops, bytes_accessed=nbytes, transcendentals=0),
    )(*args)


def known_kernel(lag_rows, steps, per, k_hbm, h_hbm, lags_ref, *refs):
    outs, (k_ref, h_ref, k_sem, h_sem) = refs[:steps], refs[steps:]
    total, known = k_ref.shape[0], h_ref.shape[0]
    size = per * lag_rows
    count = -(-total // size)
    copies = []
    for i in range(count):
        k_rows = pl.ds(i * size, min(size, total - i * size))
        h_rows = pl.ds(i * size, min(size, known - i * size))
        pair = (
            pltpu.make_async_copy(k_hbm.at[k_rows], k_ref.at[k_rows], k_sem.at[i]),
            pltpu.make_async_copy(h_hbm.at[h_rows], h_ref.at[h_rows], h_sem.at[i]),
        )
        pair[0].start()
        pair[1].start()
        copies.append(pair)
    for i in range(count):
        copies[i][0].wait()
        copies[i][1].wait()
        for s in range(steps):
            first = max(i * size, (s + 1) * lag_rows)
            last = min((i + 1) * size, total)
            if first >= last:
                continue
            shift = (s + 1) * lag_rows
            term = dot_rows(k_ref[first:last, :], h_ref[first - shift : last - shift, :])
            outs[s][...] = term if i == 0 else outs[s][...] + term
    lags_ref[...] = k_ref[: steps * lag_rows, :]


def known_forces(kernel_flat, history_flat, lag_rows, steps):
    block = kernel_flat.shape[1]
    shape = jax.ShapeDtypeStruct((block, history_flat.shape[1]), F32)
    per = steps + 1
    count = -(-kernel_flat.shape[0] // (per * lag_rows))
    out = call(
        functools.partial(known_kernel, lag_rows, steps, per),
        (jax.ShapeDtypeStruct((steps * lag_rows, block), BF16),) + (shape,) * steps,
        [pl.BlockSpec(memory_space=pltpu.MemorySpace.HBM)] * 2,
        (kernel_flat, history_flat),
        2 * steps * kernel_flat.size * history_flat.shape[1],
        2 * (kernel_flat.size + history_flat.size),
        [
            pltpu.VMEM(kernel_flat.shape, BF16),
            pltpu.VMEM(history_flat.shape, BF16),
            pltpu.SemaphoreType.DMA((count,)),
            pltpu.SemaphoreType.DMA((count,)),
        ],
    )
    return out[0], out[1:]


def force_kernel(rows, cols, ahead, *refs):
    k_ref = refs[0]
    arrived = refs[1 : 1 + rows]
    bases = refs[1 + rows : 1 + rows + ahead]
    outs = refs[1 + rows + ahead : -2]
    chunks, later = outs[:cols], outs[cols:]
    whole, total = refs[-2:]
    slab = arrived[0].shape[0]
    row, col = lax.axis_index("row"), lax.axis_index("col")
    for d in range(rows):
        start = pl.multiple_of(comes_from(row, d, rows) * slab, 16)
        whole[pl.ds(start, slab), :] = arrived[d][...]
    lag_rows = rows * slab
    total[...] = bases[0][...] + dot_rows(k_ref[:lag_rows, :], whole[...])
    for d in range(cols):
        start = pl.multiple_of(sends_to(col, d, cols) * slab, 8)
        chunks[d][...] = total[pl.ds(start, slab), :]
    for n in range(1, ahead):
        later[n - 1][...] = bases[n][...] + dot_rows(
            k_ref[n * lag_rows : (n + 1) * lag_rows, :], whole[...]
        )


def force_pieces(kernel_lags, arrived, bases, cols):
    rows, ahead = len(arrived), len(bases)
    slab, reals = arrived[0].shape
    block = kernel_lags.shape[1]
    shapes = (jax.ShapeDtypeStruct((slab, reals), F32),) * cols + (
        jax.ShapeDtypeStruct((block, reals), F32),
    ) * (ahead - 1)
    out = call(
        functools.partial(force_kernel, rows, cols, ahead),
        shapes,
        [VMEM] * (1 + rows + ahead),
        (kernel_lags, *arrived, *bases),
        2 * ahead * rows * slab * block * reals,
        4 * 2 * ahead * block * reals,
        [pltpu.VMEM((rows * slab, reals), BF16), pltpu.VMEM((block, reals), F32)],
    )
    return out[:cols], out[cols:]


def prepare_kernel(x, v, a, e, stiff, predicted, load):
    p = x[...] + DT * v[...] + QUARTER * a[...]
    predicted[...] = p
    load[...] = e[...] - dot_exact(stiff[...], p)


def prepare(x, v, a, e, stiff):
    shape = jax.ShapeDtypeStruct(x.shape, F32)
    return call(
        prepare_kernel, (shape, shape), [VMEM] * 5, (x, v, a, e, stiff),
        12 * x.size * x.shape[0], 24 * x.size,
    )


def advance_kernel(cols, *refs):
    parts = refs[:cols]
    predicted, v, a, load, inverse = refs[cols : cols + 5]
    x_out, v_out, a_out, v_half = refs[cols + 5 :]
    force = parts[0][...]
    for part in parts[1:]:
        force = force + part[...]
    a_next = dot_exact(inverse[...], load[...] - force)
    v_next = v[...] + 0.5 * DT * (a[...] + a_next)
    v_half[...] = v_next.astype(BF16)
    v_out[...] = v_next
    a_out[...] = a_next
    x_out[...] = predicted[...] + QUARTER * a_next


def advance(parts, predicted, v, a, load, inverse):
    shape = jax.ShapeDtypeStruct(v.shape, F32)
    return call(
        functools.partial(advance_kernel, len(parts)),
        (shape, shape, shape, jax.ShapeDtypeStruct(v.shape, BF16)),
        [VMEM] * (len(parts) + 5),
        (*parts, predicted, v, a, load, inverse),
        12 * v.size * v.shape[0], 40 * v.size,
    )


def finish_kernel(cols, rows, *refs):
    parts = refs[:cols]
    predicted, v, a, load, inverse, route = refs[cols : cols + 6]
    v_out, *sends = refs[cols + 6 :]
    force = parts[0][...]
    for part in parts[1:]:
        force = force + part[...]
    a_next = dot_exact(inverse[...], load[...] - force)
    v_out[...] = v[...] + 0.5 * DT * (a[...] + a_next)
    x_next = predicted[...] + QUARTER * a_next
    moved = dot_exact(route[...], x_next)
    size = route.shape[0] // rows
    for d in range(rows):
        sends[d][...] = moved[d * size : (d + 1) * size, :]


def finish(parts, predicted, v, a, load, inverse, route, rows):
    shapes = (jax.ShapeDtypeStruct(v.shape, F32),) + (
        jax.ShapeDtypeStruct((route.shape[0] // rows, v.shape[1]), F32),
    ) * rows
    out = call(
        functools.partial(finish_kernel, len(parts), rows),
        shapes,
        [VMEM] * (len(parts) + 6),
        (*parts, predicted, v, a, load, inverse, route),
        12 * v.size * v.shape[0], 40 * v.size,
    )
    return out[0], out[1:]


def gaps_kernel(rows, *refs):
    weights, arrived, out, held = refs[0], refs[1 : 1 + rows], refs[-2], refs[-1]
    size = arrived[0].shape[0]
    for d in range(rows):
        held[d * size : (d + 1) * size, :] = arrived[d][...]
    out[...] = dot_exact(weights[...], held[...])


def gaps(weights, arrived):
    points, reals = weights.shape[0], arrived[0].shape[1]
    return call(
        functools.partial(gaps_kernel, len(arrived)),
        jax.ShapeDtypeStruct((points, reals), F32),
        [VMEM] * (1 + len(arrived)),
        (weights, *arrived),
        12 * weights.size * reals, 4 * points * reals,
        [pltpu.VMEM((weights.shape[1], reals), F32)],
    )


def diagonals_kernel(*refs):
    half = len(refs) // 2
    for blocks, out in zip(refs[:half], refs[half:]):
        modules = blocks.shape[1]
        width = 6 * modules
        lane = lax.broadcasted_iota(jnp.int32, (modules, width), 1) // 6
        module = lax.broadcasted_iota(jnp.int32, (modules, width), 0)
        for i in range(6):
            spread = jnp.concatenate([blocks[i]] * modules, axis=1)
            out[pl.ds(i, modules, stride=6), :] = jnp.where(lane == module, spread, 0.0)


def diagonals(*matrices):
    width = 6 * matrices[0].shape[0]
    shape = jax.ShapeDtypeStruct((width, width), F32)
    return call(
        diagonals_kernel, (shape,) * len(matrices), [VMEM] * len(matrices),
        tuple(m.transpose(1, 0, 2) for m in matrices), 100 * width * width, 16 * width * width,
    )


def plan_kernel(rows, cols, capacity, slot_rows, owned, links, arms, send, weights, table):
    modules = send.shape[1] // 6
    points = links.shape[0] // modules
    row, col = lax.axis_index("row"), lax.axis_index("col")
    grid_index = row * cols + col
    first_module = grid_index * modules
    shape = (slot_rows, modules * 6)
    i = lax.broadcasted_iota(jnp.int32, shape, 0)
    j = lax.broadcasted_iota(jnp.int32, shape, 1)
    for d in range(rows):
        listed = (sends_to(row, d, rows) * cols + col) * modules
        wanted = jnp.full(shape, -1, jnp.int32)
        for k in range(modules):
            local = owned[listed + k] - first_module
            here = (local >= 0) & (local < modules)
            wanted = jnp.where((i // 6 == k % capacity) & here, local, wanted)
        hit = (wanted == j // 6) & (i % 6 == j % 6)
        send[d * slot_rows : (d + 1) * slot_rows, :] = jnp.where(hit, 1.0, 0.0)
    count = modules * points
    table[:, 0:3] = arms[...]
    for q in range(modules):
        home = owned[first_module + q] // (cols * modules)
        home_d = home ^ row if rows & (rows - 1) == 0 else (row + rows - home) % rows
        place = home_d * slot_rows + (q % capacity) * 6
        table[q * points : (q + 1) * points, 3:4] = jnp.full((points, 1), place, jnp.int32).astype(F32)
    own = table[...]
    point = lax.broadcasted_iota(jnp.int32, (count, count), 1)
    meets = jnp.where(links[...] - first_module * points == point, 1.0, 0.0)
    partner = dot_exact(meets, own)
    wide = (count, rows * slot_rows)
    column = lax.broadcasted_iota(jnp.int32, wide, 1)
    total = [None] * 3
    for sign, side in ((1.0, own), (-1.0, partner)):
        mode = column - (side[:, 3:4] + 0.5).astype(jnp.int32)
        e = [jnp.broadcast_to(sign * side[:, c : c + 1], wide) for c in range(3)]
        for c in range(3):
            up, down = (c + 1) % 3, (c + 2) % 3
            value = jnp.where(mode == c, sign, 0.0)
            value = jnp.where(mode == 3 + up, e[down], value)
            value = jnp.where(mode == 3 + down, -e[up], value)
            total[c] = value if total[c] is None else total[c] + value
    for q in range(modules):
        for c in range(3):
            start = (q * 3 + c) * points
            weights[start : start + points, :] = total[c][q * points : (q + 1) * points, :]


def plan(owned, links, arms, rows, cols):
    modules, points = links.shape
    capacity = 2 * modules // rows
    slot_rows = -(-capacity * 6 // 8) * 8
    return call(
        functools.partial(plan_kernel, rows, cols, capacity, slot_rows),
        (
            jax.ShapeDtypeStruct((rows * slot_rows, modules * 6), F32),
            jax.ShapeDtypeStruct((modules * 3 * points, rows * slot_rows), F32),
        ),
        [SMEM, VMEM, VMEM],
        (owned, links.reshape(-1, 1), arms.transpose(0, 2, 1).reshape(-1, 3)),
        12 * (modules * points) ** 2 * 4, 4 * modules * 3 * points * rows * slot_rows,
        [pltpu.VMEM((modules * points, 4), F32)],
    )


def after(value, *others):
    return lax.optimization_barrier((value, *others))[0]


def body(
    kernel,
    history,
    displacement,
    velocity,
    acceleration,
    excitation,
    solve_inverse,
    stiffness,
    owned,
    links,
    arms,
):
    rows, cols = lax.axis_size("row"), lax.axis_size("col")
    steps = excitation.shape[0]
    slab, reals = velocity.shape
    modules, points = links.shape
    x, v, a = displacement, velocity, acceleration
    arrived = exchange([v.astype(BF16)] * rows, "row")
    lags, bases = known_forces(
        kernel.reshape(-1, kernel.shape[3]), history.reshape(-1, reals), rows * slab, steps
    )
    inverse, stiff = diagonals(solve_inverse, stiffness)
    for n in range(steps):
        predicted, load = prepare(x, v, a, excitation[n], stiff)
        pieces, bases = force_pieces(lags, arrived, bases, cols)
        if n == 0:
            send, weights = plan(after(owned, pieces[0]), links, arms, rows, cols)
        parts = exchange(pieces, "col")
        if n < steps - 1:
            x, v, a, v_half = advance(parts, predicted, v, a, load, inverse)
            arrived = exchange([v_half] * rows, "row")
        else:
            v, sends = finish(parts, predicted, v, a, load, inverse, send, rows)
    moved = exchange(sends, "row")
    out = gaps(weights, moved).reshape(modules, 3, points, reals)
    return v, out.transpose(0, 2, 1, 3)


def solution(mesh):
    placed = (
        P(None, None, "col", "row"),
        P(None, None, "col", "sea"),
        P(("row", "col"), "sea"),
        P(("row", "col"), "sea"),
        P(("row", "col"), "sea"),
        P(None, ("row", "col"), "sea"),
        P(("row", "col"), None, None),
        P(("row", "col"), None, None),
        P(),
        P(("row", "col"), None),
        P(("row", "col"), None, None),
    )
    return jax.shard_map(
        body,
        mesh=mesh,
        in_specs=placed,
        out_specs=(P(("row", "col"), "sea"), P(("row", "col"), None, None, "sea")),
        check_vma=False,
    )
```

```python
import functools

import jax
import jax.numpy as jnp
from jax import lax
from jax.experimental import pallas as pl
from jax.experimental.pallas import tpu as pltpu
from jax.sharding import PartitionSpec as P


DT = 0.5
QUARTER = DT * DT / 4.0
F32 = jnp.float32
BF16 = jnp.bfloat16
HIGHEST = lax.Precision.HIGHEST
VMEM = pl.BlockSpec(memory_space=pltpu.VMEM)
SMEM = pl.BlockSpec(memory_space=pltpu.SMEM)


def sends_to(i, d, n):
    return i ^ d if n & (n - 1) == 0 else (i + d) % n


def comes_from(i, d, n):
    return i ^ d if n & (n - 1) == 0 else (i + n - d) % n


def exchange(pieces, axis):
    n = lax.axis_size(axis)
    out = [pieces[0]] + [None] * (n - 1)
    for d in range(n - 1, 0, -1):
        out[d] = lax.ppermute(pieces[d], axis, [(i, sends_to(i, d, n)) for i in range(n)])
    return out


def dot_rows(a, b):
    return lax.dot_general(a, b, (((0,), (0,)), ((), ())), preferred_element_type=F32)


def dot_exact(a, b):
    return jnp.dot(a, b, precision=HIGHEST, preferred_element_type=F32)


def padded_bytes(shape, dtype):
    size = jnp.dtype(dtype).itemsize
    dims = (1, 1, *shape)
    up = lambda n, m: -(-n // m) * m
    major = 1
    for n in dims[:-2]:
        major *= n
    return major * up(dims[-2], 32 // size) * up(dims[-1], 128) * size


def call(body, shapes, in_specs, args, flops, nbytes, scratch=()):
    arrays = list(args) + jax.tree.leaves(shapes)
    held = sum(padded_bytes(t.shape, t.dtype) for t in arrays)
    held += sum(padded_bytes(t.shape, t.dtype) for t in scratch if t.shape[1:])
    return pl.pallas_call(
        body,
        out_shape=shapes,
        in_specs=in_specs,
        out_specs=jax.tree.map(lambda _: VMEM, shapes),
        scratch_shapes=scratch,
        compiler_params=pltpu.CompilerParams(vmem_limit_bytes=min(2 * held + (2 << 20), 60 << 20)),
        cost_estimate=pl.CostEstimate(flops=flops, bytes_accessed=nbytes, transcendentals=0),
    )(*args)


def known_kernel(lag_rows, steps, k_ref, h_ref, lags_ref, *outs):
    total = k_ref.shape[0]
    lags_ref[...] = k_ref[: steps * lag_rows, :]
    for s in range(steps):
        first = (s + 1) * lag_rows
        outs[s][...] = dot_rows(k_ref[first:, :], h_ref[: total - first, :])


def known_forces(kernel_flat, history_flat, lag_rows, steps):
    block = kernel_flat.shape[1]
    shape = jax.ShapeDtypeStruct((block, history_flat.shape[1]), F32)
    out = call(
        functools.partial(known_kernel, lag_rows, steps),
        (jax.ShapeDtypeStruct((steps * lag_rows, block), BF16),) + (shape,) * steps,
        [VMEM, VMEM],
        (kernel_flat, history_flat),
        2 * steps * kernel_flat.size * history_flat.shape[1],
        2 * (kernel_flat.size + history_flat.size),
    )
    return out[0], out[1:]


def force_kernel(rows, cols, ahead, *refs):
    k_ref = refs[0]
    arrived = refs[1 : 1 + rows]
    bases = refs[1 + rows : 1 + rows + ahead]
    outs = refs[1 + rows + ahead : -2]
    chunks, later = outs[:cols], outs[cols:]
    whole, total = refs[-2:]
    slab = arrived[0].shape[0]
    row, col = lax.axis_index("row"), lax.axis_index("col")
    for d in range(rows):
        start = pl.multiple_of(comes_from(row, d, rows) * slab, 16)
        whole[pl.ds(start, slab), :] = arrived[d][...]
    lag_rows = rows * slab
    total[...] = bases[0][...] + dot_rows(k_ref[:lag_rows, :], whole[...])
    for d in range(cols):
        start = pl.multiple_of(sends_to(col, d, cols) * slab, 8)
        chunks[d][...] = total[pl.ds(start, slab), :]
    for n in range(1, ahead):
        later[n - 1][...] = bases[n][...] + dot_rows(
            k_ref[n * lag_rows : (n + 1) * lag_rows, :], whole[...]
        )


def force_pieces(kernel_lags, arrived, bases, cols):
    rows, ahead = len(arrived), len(bases)
    slab, reals = arrived[0].shape
    block = kernel_lags.shape[1]
    shapes = (jax.ShapeDtypeStruct((slab, reals), F32),) * cols + (
        jax.ShapeDtypeStruct((block, reals), F32),
    ) * (ahead - 1)
    out = call(
        functools.partial(force_kernel, rows, cols, ahead),
        shapes,
        [VMEM] * (1 + rows + ahead),
        (kernel_lags, *arrived, *bases),
        2 * ahead * rows * slab * block * reals,
        4 * 2 * ahead * block * reals,
        [pltpu.VMEM((rows * slab, reals), BF16), pltpu.VMEM((block, reals), F32)],
    )
    return out[:cols], out[cols:]


def prepare_kernel(x, v, a, e, stiff, predicted, load):
    p = x[...] + DT * v[...] + QUARTER * a[...]
    predicted[...] = p
    load[...] = e[...] - dot_exact(stiff[...], p)


def prepare(x, v, a, e, stiff):
    shape = jax.ShapeDtypeStruct(x.shape, F32)
    return call(
        prepare_kernel, (shape, shape), [VMEM] * 5, (x, v, a, e, stiff),
        12 * x.size * x.shape[0], 24 * x.size,
    )


def split(value, parts):
    out = []
    for _ in range(parts):
        out.append(value.astype(BF16))
        value = value - out[-1].astype(F32)
    return out


def joined(parts):
    total = parts[-1].astype(F32)
    for part in parts[-2::-1]:
        total = total + part.astype(F32)
    return total


def picked(pieces, index):
    out = pieces[0]
    for k in range(1, len(pieces)):
        out = jnp.where(index == k, pieces[k], out)
    return out


def bundle_columns(ahead, block, width):
    return [k * block for k in range(ahead)], [
        [ahead * block + (2 * k + part) * width for part in range(2)] for k in range(ahead)
    ]


def pack_kernel(rows, ahead, *refs):
    lags, bases = refs[0], refs[1 : 1 + ahead]
    e, inverse, stiff = refs[1 + ahead : 4 + ahead]
    outs, coef = refs[4 + ahead : -1], refs[-1]
    block, reals = bases[0].shape
    slab, width = e.shape[1], reals // rows
    lag_rows = lags.shape[0] // (ahead + 1)
    tail = outs[0].shape[0] - slab
    lag_at, base_at = bundle_columns(ahead, block, width)
    modules = inverse.shape[1]
    for i in range(6):
        coef[pl.ds(i, modules, stride=6), :] = jnp.concatenate([inverse[i], stiff[i]], axis=1)
    coefs = split(coef[...], 3)
    row = lax.axis_index("row")

    def cut(value):
        return [value[:, t * width : (t + 1) * width] for t in range(rows)]

    base_cuts = [[cut(part) for part in split(base[...], 2)] for base in bases]
    e_cuts = [[cut(part) for part in split(e[1 + k], 3)] for k in range(ahead)]
    for d in range(rows):
        out, to = outs[d], sends_to(row, d, rows)
        for k in range(ahead):
            out[0:lag_rows, lag_at[k] : lag_at[k] + block] = lags[k * lag_rows : (k + 1) * lag_rows, :]
            for part in range(2):
                out[0:block, base_at[k][part] : base_at[k][part] + width] = picked(
                    base_cuts[k][part], to
                )
            for part in range(3):
                at = (3 * k + part) * width
                out[tail : tail + slab, at : at + width] = picked(e_cuts[k][part], to)
        for part in range(3):
            at = 3 * ahead * width + 12 * part
            out[tail : tail + slab, at : at + 12] = coefs[part]


def pack(lags, bases, e, inverse, stiff, rows):
    ahead = len(bases)
    block, reals = bases[0].shape
    slab, width = e.shape[1], reals // rows
    lag_rows = lags.shape[0] // (ahead + 1)
    lanes = max(ahead * (block + 2 * width), 3 * ahead * width + 36)
    shape = jax.ShapeDtypeStruct((max(lag_rows, block) + slab, lanes), BF16)
    return call(
        functools.partial(pack_kernel, rows, ahead),
        (shape,) * rows,
        [VMEM] * (4 + ahead),
        (lags, *bases, e, inverse.transpose(1, 0, 2), stiff.transpose(1, 0, 2)),
        rows * lags.size, 4 * rows * lags.size,
        [pltpu.VMEM((slab, 12), F32)],
    )


def unpack_kernel(rows, ahead, block, lag_rows, slab, width, *refs):
    arrived = refs[:rows]
    lags = refs[rows : rows + ahead]
    bases = refs[rows + ahead : rows + 2 * ahead]
    es = refs[rows + 2 * ahead : rows + 3 * ahead]
    inverse, stiff = refs[rows + 3 * ahead :]
    tail = arrived[0].shape[0] - slab
    lag_at, base_at = bundle_columns(ahead, block, width)
    modules = slab // 6
    lane = lax.broadcasted_iota(jnp.int32, (slab, slab), 1) // 6
    module = lax.broadcasted_iota(jnp.int32, (slab, slab), 0) // 6
    row = lax.axis_index("row")
    for d in range(rows):
        source = arrived[d]
        g = comes_from(row, d, rows)
        for k in range(ahead):
            lags[k][g] = source[0:lag_rows, lag_at[k] : lag_at[k] + block]
            bases[k][g] = joined(
                [source[0:block, base_at[k][part] : base_at[k][part] + width] for part in range(2)]
            )
            es[k][g] = joined(
                [
                    source[tail : tail + slab, (3 * k + part) * width : (3 * k + part + 1) * width]
                    for part in range(3)
                ]
            )
        first = 3 * ahead * width
        coef = joined(
            [source[tail : tail + slab, first + 12 * part : first + 12 * part + 12] for part in range(3)]
        )
        for at, out in ((0, inverse), (6, stiff)):
            spread = jnp.concatenate([coef[:, at : at + 6]] * modules, axis=1)
            out[g] = jnp.where(lane == module, spread, 0.0)


def unpack(arrived, ahead, block, lag_rows, slab, width):
    rows = len(arrived)
    of = lambda *shape: jax.ShapeDtypeStruct((rows, *shape), F32)
    out = call(
        functools.partial(unpack_kernel, rows, ahead, block, lag_rows, slab, width),
        (jax.ShapeDtypeStruct((rows, lag_rows, block), BF16),) * ahead
        + (of(block, width),) * ahead
        + (of(slab, width),) * ahead
        + (of(slab, slab),) * 2,
        [VMEM] * rows,
        arrived,
        rows * lag_rows * block, 4 * rows * lag_rows * block,
    )
    return out[:ahead], out[ahead : 2 * ahead], out[2 * ahead : 3 * ahead], out[-2], out[-1]


def side_by_side(width, count):
    per = 1
    while 2 * per * width <= 128 and count % (2 * per) == 0:
        per *= 2
    return per


def turn_kernel(cols, rows, *refs):
    parts = refs[:cols]
    predicted, v, a, load, inverse = refs[cols : cols + 5]
    outs = refs[cols + 5 :]
    force = parts[0][...]
    for part in parts[1:]:
        force = force + part[...]
    a_next = dot_exact(inverse[...], load[...] - force)
    v_next = v[...] + 0.5 * DT * (a[...] + a_next)
    x_next = predicted[...] + QUARTER * a_next
    slab, width = v.shape[0], v.shape[1] // rows
    per = side_by_side(width, 4)
    row = lax.axis_index("row")
    for i, value in enumerate((v_next, x_next, a_next)):
        cuts = [value[:, t * width : (t + 1) * width] for t in range(rows)]
        at, lane = i // per * slab, i % per * width
        for d in range(rows):
            outs[d][at : at + slab, lane : lane + width] = picked(cuts, sends_to(row, d, rows))


def turn(parts, predicted, v, a, load, inverse, rows):
    slab, width = v.shape[0], v.shape[1] // rows
    per = side_by_side(width, 4)
    shape = jax.ShapeDtypeStruct((4 // per * slab, per * width), F32)
    return call(
        functools.partial(turn_kernel, len(parts), rows),
        (shape,) * rows,
        [VMEM] * (len(parts) + 5),
        (*parts, predicted, v, a, load, inverse),
        12 * v.size * v.shape[0], 40 * v.size,
    )


def turned_kernel(rows, *refs):
    arrived, (v_half, x, v, a) = refs[:rows], refs[rows:]
    slab, width = v.shape[1:]
    per = side_by_side(width, 4)
    row = lax.axis_index("row")
    for d in range(rows):
        g = comes_from(row, d, rows)
        for i, out in enumerate((v, x, a)):
            at, lane = i // per * slab, i % per * width
            value = arrived[d][at : at + slab, lane : lane + width]
            out[g] = value
            if i == 0:
                v_half[g] = value.astype(BF16)


def turned(arrived, slab, width):
    rows = len(arrived)
    shape = jax.ShapeDtypeStruct((rows, slab, width), F32)
    return call(
        functools.partial(turned_kernel, rows),
        (jax.ShapeDtypeStruct((rows, slab, width), BF16), shape, shape, shape),
        [VMEM] * rows,
        arrived,
        rows * slab * width, 16 * rows * slab * width,
    )


def side_force_kernel(cols, ahead, *refs):
    v_half, lags, bases = refs[0], refs[1 : 1 + ahead], refs[1 + ahead : 1 + 2 * ahead]
    outs = refs[1 + 2 * ahead : -1]
    chunks, later, held = outs[:cols], outs[cols:], refs[-1]
    rows, slab, width = v_half.shape
    per = side_by_side(width, rows)
    deep = rows // per
    newest = v_half[...].reshape(rows * slab, width)
    for g in range(rows):
        force = bases[0][g] + dot_rows(lags[0][g], newest)
        at, lane = g % deep * slab, g // deep * width
        for c in range(cols):
            held[c, at : at + slab, lane : lane + width] = force[c * slab : (c + 1) * slab, :]
    col = lax.axis_index("col")
    for d in range(cols):
        chunks[d][...] = held[sends_to(col, d, cols)]
    for n in range(1, ahead):
        for g in range(rows):
            later[n - 1][g] = bases[n][g] + dot_rows(lags[n][g], newest)


def side_force(v_half, lags, bases, cols):
    ahead = len(bases)
    rows, slab, width = v_half.shape
    block = bases[0].shape[1]
    per = side_by_side(width, rows)
    shape = (rows // per * slab, per * width)
    out = call(
        functools.partial(side_force_kernel, cols, ahead),
        (jax.ShapeDtypeStruct(shape, F32),) * cols
        + (jax.ShapeDtypeStruct((rows, block, width), F32),) * (ahead - 1),
        [VMEM] * (1 + 2 * ahead),
        (v_half, *lags[:ahead], *bases),
        2 * ahead * rows * rows * slab * block * width,
        4 * 2 * ahead * rows * block * width,
        [pltpu.VMEM((cols, *shape), F32)],
    )
    return out[:cols], out[cols:]


def side_prepare_kernel(x, v, a, e, stiff, predicted, load):
    for g in range(x.shape[0]):
        p = x[g] + DT * v[g] + QUARTER * a[g]
        predicted[g] = p
        load[g] = e[g] - dot_exact(stiff[g], p)


def side_prepare(x, v, a, e, stiff):
    shape = jax.ShapeDtypeStruct(x.shape, F32)
    return call(
        side_prepare_kernel, (shape, shape), [VMEM] * 5, (x, v, a, e, stiff),
        12 * x.size * x.shape[1], 24 * x.size,
    )


def side_sum(parts, rows, width, slab):
    force = parts[0][...]
    for part in parts[1:]:
        force = force + part[...]
    deep = rows // side_by_side(width, rows)
    out = []
    for g in range(rows):
        at, lane = g % deep * slab, g // deep * width
        out.append(force[at : at + slab, lane : lane + width])
    return out


def side_advance_kernel(cols, *refs):
    parts = refs[:cols]
    predicted, v, a, load, inverse, x_out, v_out, a_out, v_half = refs[cols:]
    rows, slab, width = v.shape
    for g, force in enumerate(side_sum(parts, rows, width, slab)):
        a_next = dot_exact(inverse[g], load[g] - force)
        v_next = v[g] + 0.5 * DT * (a[g] + a_next)
        v_half[g] = v_next.astype(BF16)
        v_out[g] = v_next
        a_out[g] = a_next
        x_out[g] = predicted[g] + QUARTER * a_next


def side_advance(parts, predicted, v, a, load, inverse):
    shape = jax.ShapeDtypeStruct(v.shape, F32)
    return call(
        functools.partial(side_advance_kernel, len(parts)),
        (shape, shape, shape, jax.ShapeDtypeStruct(v.shape, BF16)),
        [VMEM] * (len(parts) + 5),
        (*parts, predicted, v, a, load, inverse),
        12 * v.size * v.shape[1], 40 * v.size,
    )


def side_finish_kernel(cols, *refs):
    parts = refs[:cols]
    predicted, v, a, load, inverse, route = refs[cols : cols + 6]
    outs, x_held, v_held = refs[cols + 6 : -2], refs[-2], refs[-1]
    rows, slab, width = v.shape
    for g, force in enumerate(side_sum(parts, rows, width, slab)):
        a_next = dot_exact(inverse[g], load[g] - force)
        v_held[g] = v[g] + 0.5 * DT * (a[g] + a_next)
        x_held[g * slab : (g + 1) * slab, :] = predicted[g] + QUARTER * a_next
    moved = dot_exact(route[...], x_held[...])
    row = lax.axis_index("row")
    for d in range(rows):
        outs[d][:, 0:width] = moved[d * slab : (d + 1) * slab, :]
        outs[d][:, width : 2 * width] = v_held[sends_to(row, d, rows)]


def side_finish(parts, predicted, v, a, load, inverse, route):
    rows, slab, width = v.shape
    return call(
        functools.partial(side_finish_kernel, len(parts)),
        (jax.ShapeDtypeStruct((slab, 2 * width), F32),) * rows,
        [VMEM] * (len(parts) + 6),
        (*parts, predicted, v, a, load, inverse, route),
        12 * v.size * rows * slab, 40 * v.size,
        [pltpu.VMEM((rows * slab, width), F32), pltpu.VMEM(v.shape, F32)],
    )


def gaps_kernel(rows, *refs):
    weights, arrived = refs[0], refs[1 : 1 + rows]
    v_out, out, held = refs[1 + rows :]
    width = arrived[0].shape[1] // 2
    row = lax.axis_index("row")
    messages = [ref[...] for ref in arrived]
    for t in range(rows):
        d = t ^ row if rows & (rows - 1) == 0 else (row + rows - t) % rows
        message = picked(messages, d)
        held[:, t * width : (t + 1) * width] = message[:, 0:width]
        v_out[:, t * width : (t + 1) * width] = message[:, width : 2 * width]
    out[...] = dot_exact(weights[...], held[...])


def gaps(weights, arrived):
    rows, points = len(arrived), weights.shape[0]
    slab, reals = arrived[0].shape[0], arrived[0].shape[1] // 2 * rows
    return call(
        functools.partial(gaps_kernel, rows),
        (
            jax.ShapeDtypeStruct((slab, reals), F32),
            jax.ShapeDtypeStruct((points, reals), F32),
        ),
        [VMEM] * (1 + rows),
        (weights, *arrived),
        12 * weights.size * reals, 4 * points * reals,
        [pltpu.VMEM((slab, reals), F32)],
    )


def diagonals_kernel(*refs):
    half = len(refs) // 2
    for blocks, out in zip(refs[:half], refs[half:]):
        modules = blocks.shape[1]
        width = 6 * modules
        lane = lax.broadcasted_iota(jnp.int32, (modules, width), 1) // 6
        module = lax.broadcasted_iota(jnp.int32, (modules, width), 0)
        for i in range(6):
            spread = jnp.concatenate([blocks[i]] * modules, axis=1)
            out[pl.ds(i, modules, stride=6), :] = jnp.where(lane == module, spread, 0.0)


def diagonals(*matrices):
    width = 6 * matrices[0].shape[0]
    shape = jax.ShapeDtypeStruct((width, width), F32)
    return call(
        diagonals_kernel, (shape,) * len(matrices), [VMEM] * len(matrices),
        tuple(m.transpose(1, 0, 2) for m in matrices), 100 * width * width, 16 * width * width,
    )


def plan_kernel(rows, cols, owned, links, arms, send, weights, table):
    modules = weights.shape[1] // 6
    points = links.shape[0] // modules
    row, col = lax.axis_index("row"), lax.axis_index("col")
    slab = modules * 6
    shape = (slab, rows * slab)
    i = lax.broadcasted_iota(jnp.int32, shape, 0)
    j = lax.broadcasted_iota(jnp.int32, shape, 1)
    for d in range(rows):
        listed = (sends_to(row, d, rows) * cols + col) * modules
        wanted = i % 6
        for k in range(modules):
            module = owned[listed + k]
            place = module // (cols * modules) * slab + module % modules * 6
            wanted = wanted + jnp.where(i // 6 == k, place, 0)
        send[d * slab : (d + 1) * slab, :] = jnp.where(wanted == j, 1.0, 0.0)
    count = modules * points
    table[:, 0:3] = arms[...]
    position = lax.broadcasted_iota(jnp.int32, (count, 1), 0)
    table[:, 3:4] = (position // points * 6).astype(F32)
    own = table[...]
    first_point = (row * cols + col) * count
    point = lax.broadcasted_iota(jnp.int32, (count, count), 1)
    meets = jnp.where(links[...] - first_point == point, 1.0, 0.0)
    partner = dot_exact(meets, own)
    wide = (count, slab)
    column = lax.broadcasted_iota(jnp.int32, wide, 1)
    total = [None] * 3
    for sign, side in ((1.0, own), (-1.0, partner)):
        mode = column - (side[:, 3:4] + 0.5).astype(jnp.int32)
        e = [jnp.broadcast_to(sign * side[:, c : c + 1], wide) for c in range(3)]
        for c in range(3):
            up, down = (c + 1) % 3, (c + 2) % 3
            value = jnp.where(mode == c, sign, 0.0)
            value = jnp.where(mode == 3 + up, e[down], value)
            value = jnp.where(mode == 3 + down, -e[up], value)
            total[c] = value if total[c] is None else total[c] + value
    for q in range(modules):
        for c in range(3):
            start = (q * 3 + c) * points
            weights[start : start + points, :] = total[c][q * points : (q + 1) * points, :]


def plan(owned, links, arms, rows, cols):
    modules, points = links.shape
    return call(
        functools.partial(plan_kernel, rows, cols),
        (
            jax.ShapeDtypeStruct((rows * modules * 6, rows * modules * 6), F32),
            jax.ShapeDtypeStruct((modules * 3 * points, modules * 6), F32),
        ),
        [SMEM, VMEM, VMEM],
        (owned, links.reshape(-1, 1), arms.transpose(0, 2, 1).reshape(-1, 3)),
        12 * (modules * points) ** 2 * 4, 4 * modules * 3 * points * rows * modules * 6,
        [pltpu.VMEM((modules * points, 4), F32)],
    )


def after(value, *others):
    return lax.optimization_barrier((value, *others))[0]


def body(
    kernel,
    history,
    displacement,
    velocity,
    acceleration,
    excitation,
    solve_inverse,
    stiffness,
    owned,
    links,
    arms,
):
    rows, cols = lax.axis_size("row"), lax.axis_size("col")
    steps = excitation.shape[0]
    slab, reals = velocity.shape
    modules, points = links.shape
    block, width = kernel.shape[3], reals // rows
    x, v, a = displacement, velocity, acceleration
    arrived = exchange([v.astype(BF16)] * rows, "row")
    lags, bases = known_forces(
        kernel.reshape(-1, block), history.reshape(-1, reals), rows * slab, steps
    )
    inverse, stiff = diagonals(solve_inverse, stiffness)
    predicted, load = prepare(x, v, a, excitation[0], stiff)
    pieces, bases = force_pieces(lags, arrived, bases, cols)
    parts = exchange(pieces, "col")
    bundle = exchange(pack(lags, bases, excitation, solve_inverse, stiffness, rows), "row")
    sends = turn(parts, predicted, v, a, load, inverse, rows)
    messages = exchange(sends, "row")
    lags, bases, excite, inverse, stiff = unpack(
        bundle, steps - 1, block, rows * slab, slab, width
    )
    v_half, x, v, a = turned(messages, slab, width)
    for n in range(1, steps):
        predicted, load = side_prepare(x, v, a, excite[n - 1], stiff)
        pieces, bases = side_force(v_half, lags, bases, cols)
        if n == 1:
            send, weights = plan(after(owned, pieces[0]), links, arms, rows, cols)
        parts = exchange(pieces, "col")
        if n < steps - 1:
            x, v, a, v_half = side_advance(parts, predicted, v, a, load, inverse)
    moved = exchange(side_finish(parts, predicted, v, a, load, inverse, send), "row")
    v, out = gaps(weights, moved)
    return v, out.reshape(modules, 3, points, reals).transpose(0, 2, 1, 3)


def solution(mesh):
    placed = (
        P(None, None, "col", "row"),
        P(None, None, "col", "sea"),
        P(("row", "col"), "sea"),
        P(("row", "col"), "sea"),
        P(("row", "col"), "sea"),
        P(None, ("row", "col"), "sea"),
        P(("row", "col"), None, None),
        P(("row", "col"), None, None),
        P(),
        P(("row", "col"), None),
        P(("row", "col"), None, None),
    )
    return jax.shard_map(
        body,
        mesh=mesh,
        in_specs=placed,
        out_specs=(P(("row", "col"), "sea"), P(("row", "col"), None, None, "sea")),
        check_vma=False,
    )
```

```python
import functools

import jax
import jax.numpy as jnp
from jax import lax
from jax.experimental import pallas as pl
from jax.experimental.pallas import tpu as pltpu
from jax.sharding import PartitionSpec as P


DT = 0.5
QUARTER = DT * DT / 4.0
F32 = jnp.float32
BF16 = jnp.bfloat16
HIGHEST = lax.Precision.HIGHEST
VMEM = pl.BlockSpec(memory_space=pltpu.VMEM)
SMEM = pl.BlockSpec(memory_space=pltpu.SMEM)


def sends_to(i, d, n):
    return i ^ d if n & (n - 1) == 0 else (i + d) % n


def comes_from(i, d, n):
    return i ^ d if n & (n - 1) == 0 else (i + n - d) % n


def exchange(pieces, axis):
    n = lax.axis_size(axis)
    out = [pieces[0]] + [None] * (n - 1)
    for d in range(n - 1, 0, -1):
        out[d] = lax.ppermute(pieces[d], axis, [(i, sends_to(i, d, n)) for i in range(n)])
    return out


def dot_rows(a, b):
    return lax.dot_general(a, b, (((0,), (0,)), ((), ())), preferred_element_type=F32)


def dot_exact(a, b):
    return jnp.dot(a, b, precision=HIGHEST, preferred_element_type=F32)


def padded_bytes(shape, dtype):
    size = jnp.dtype(dtype).itemsize
    dims = (1, 1, *shape)
    up = lambda n, m: -(-n // m) * m
    major = 1
    for n in dims[:-2]:
        major *= n
    return major * up(dims[-2], 32 // size) * up(dims[-1], 128) * size


def call(body, shapes, in_specs, args, flops, nbytes, scratch=()):
    arrays = list(args) + jax.tree.leaves(shapes)
    held = sum(padded_bytes(t.shape, t.dtype) for t in arrays)
    held += sum(padded_bytes(t.shape, t.dtype) for t in scratch if t.shape[1:])
    return pl.pallas_call(
        body,
        out_shape=shapes,
        in_specs=in_specs,
        out_specs=jax.tree.map(lambda _: VMEM, shapes),
        scratch_shapes=scratch,
        compiler_params=pltpu.CompilerParams(
            vmem_limit_bytes=min(2 * held + (2 << 20), 60 << 20)
        ),
        cost_estimate=pl.CostEstimate(flops=flops, bytes_accessed=nbytes, transcendentals=0),
    )(*args)


def known_kernel(lag_rows, steps, per, k_hbm, h_hbm, lags_ref, *refs):
    outs, (k_ref, h_ref, k_sem, h_sem) = refs[:steps], refs[steps:]
    total, known = k_ref.shape[0], h_ref.shape[0]
    size = per * lag_rows
    count = -(-total // size)
    copies = []
    for i in range(count):
        k_rows = pl.ds(i * size, min(size, total - i * size))
        h_rows = pl.ds(i * size, min(size, known - i * size))
        pair = (
            pltpu.make_async_copy(k_hbm.at[k_rows], k_ref.at[k_rows], k_sem.at[i]),
            pltpu.make_async_copy(h_hbm.at[h_rows], h_ref.at[h_rows], h_sem.at[i]),
        )
        pair[0].start()
        pair[1].start()
        copies.append(pair)
    for i in range(count):
        copies[i][0].wait()
        copies[i][1].wait()
        for s in range(steps):
            first = max(i * size, (s + 1) * lag_rows)
            last = min((i + 1) * size, total)
            if first >= last:
                continue
            shift = (s + 1) * lag_rows
            term = dot_rows(k_ref[first:last, :], h_ref[first - shift : last - shift, :])
            outs[s][...] = term if i == 0 else outs[s][...] + term
    lags_ref[...] = k_ref[: steps * lag_rows, :]


def known_forces(kernel_flat, history_flat, lag_rows, steps):
    block = kernel_flat.shape[1]
    shape = jax.ShapeDtypeStruct((block, history_flat.shape[1]), F32)
    per = steps + 1
    count = -(-kernel_flat.shape[0] // (per * lag_rows))
    out = call(
        functools.partial(known_kernel, lag_rows, steps, per),
        (jax.ShapeDtypeStruct((steps * lag_rows, block), BF16),) + (shape,) * steps,
        [pl.BlockSpec(memory_space=pltpu.MemorySpace.HBM)] * 2,
        tuple(
            pltpu.with_memory_space_constraint(t, pltpu.MemorySpace.HBM)
            for t in (kernel_flat, history_flat)
        ),
        2 * steps * kernel_flat.size * history_flat.shape[1],
        2 * (kernel_flat.size + history_flat.size),
        [
            pltpu.VMEM(kernel_flat.shape, BF16),
            pltpu.VMEM(history_flat.shape, BF16),
            pltpu.SemaphoreType.DMA((count,)),
            pltpu.SemaphoreType.DMA((count,)),
        ],
    )
    return out[0], out[1:]


def force_kernel(rows, cols, ahead, *refs):
    k_ref = refs[0]
    arrived = refs[1 : 1 + rows]
    bases = refs[1 + rows : 1 + rows + ahead]
    outs = refs[1 + rows + ahead : -2]
    chunks, later = outs[:cols], outs[cols:]
    whole, total = refs[-2:]
    slab = arrived[0].shape[0]
    row, col = lax.axis_index("row"), lax.axis_index("col")
    for d in range(rows):
        start = pl.multiple_of(comes_from(row, d, rows) * slab, 16)
        whole[pl.ds(start, slab), :] = arrived[d][...]
    lag_rows = rows * slab
    total[...] = bases[0][...] + dot_rows(k_ref[:lag_rows, :], whole[...])
    for d in range(cols):
        start = pl.multiple_of(sends_to(col, d, cols) * slab, 8)
        chunks[d][...] = total[pl.ds(start, slab), :]
    for n in range(1, ahead):
        later[n - 1][...] = bases[n][...] + dot_rows(
            k_ref[n * lag_rows : (n + 1) * lag_rows, :], whole[...]
        )


def force_pieces(kernel_lags, arrived, bases, cols):
    rows, ahead = len(arrived), len(bases)
    slab, reals = arrived[0].shape
    block = kernel_lags.shape[1]
    shapes = (jax.ShapeDtypeStruct((slab, reals), F32),) * cols + (
        jax.ShapeDtypeStruct((block, reals), F32),
    ) * (ahead - 1)
    out = call(
        functools.partial(force_kernel, rows, cols, ahead),
        shapes,
        [VMEM] * (1 + rows + ahead),
        (kernel_lags, *arrived, *bases),
        2 * ahead * rows * slab * block * reals,
        4 * 2 * ahead * block * reals,
        [pltpu.VMEM((rows * slab, reals), BF16), pltpu.VMEM((block, reals), F32)],
    )
    return out[:cols], out[cols:]


def prepare_kernel(x, v, a, e, stiff, predicted, load):
    p = x[...] + DT * v[...] + QUARTER * a[...]
    predicted[...] = p
    load[...] = e[...] - dot_exact(stiff[...], p)


def prepare(x, v, a, e, stiff):
    shape = jax.ShapeDtypeStruct(x.shape, F32)
    return call(
        prepare_kernel, (shape, shape), [VMEM] * 5, (x, v, a, e, stiff),
        12 * x.size * x.shape[0], 24 * x.size,
    )


def advance_kernel(cols, *refs):
    parts = refs[:cols]
    predicted, v, a, load, inverse = refs[cols : cols + 5]
    x_out, v_out, a_out, v_half = refs[cols + 5 :]
    force = parts[0][...]
    for part in parts[1:]:
        force = force + part[...]
    a_next = dot_exact(inverse[...], load[...] - force)
    v_next = v[...] + 0.5 * DT * (a[...] + a_next)
    v_half[...] = v_next.astype(BF16)
    v_out[...] = v_next
    a_out[...] = a_next
    x_out[...] = predicted[...] + QUARTER * a_next


def advance(parts, predicted, v, a, load, inverse):
    shape = jax.ShapeDtypeStruct(v.shape, F32)
    return call(
        functools.partial(advance_kernel, len(parts)),
        (shape, shape, shape, jax.ShapeDtypeStruct(v.shape, BF16)),
        [VMEM] * (len(parts) + 5),
        (*parts, predicted, v, a, load, inverse),
        12 * v.size * v.shape[0], 40 * v.size,
    )


def finish_kernel(cols, rows, *refs):
    parts = refs[:cols]
    predicted, v, a, load, inverse, route = refs[cols : cols + 6]
    v_out, *sends = refs[cols + 6 :]
    force = parts[0][...]
    for part in parts[1:]:
        force = force + part[...]
    a_next = dot_exact(inverse[...], load[...] - force)
    v_out[...] = v[...] + 0.5 * DT * (a[...] + a_next)
    x_next = predicted[...] + QUARTER * a_next
    moved = dot_exact(route[...], x_next)
    size = route.shape[0] // rows
    for d in range(rows):
        sends[d][...] = moved[d * size : (d + 1) * size, :]


def finish(parts, predicted, v, a, load, inverse, route, rows):
    shapes = (jax.ShapeDtypeStruct(v.shape, F32),) + (
        jax.ShapeDtypeStruct((route.shape[0] // rows, v.shape[1]), F32),
    ) * rows
    out = call(
        functools.partial(finish_kernel, len(parts), rows),
        shapes,
        [VMEM] * (len(parts) + 6),
        (*parts, predicted, v, a, load, inverse, route),
        12 * v.size * v.shape[0], 40 * v.size,
    )
    return out[0], out[1:]


def gaps_kernel(rows, *refs):
    weights, arrived, out, held = refs[0], refs[1 : 1 + rows], refs[-2], refs[-1]
    size = arrived[0].shape[0]
    for d in range(rows):
        held[d * size : (d + 1) * size, :] = arrived[d][...]
    out[...] = dot_exact(weights[...], held[...])


def gaps(weights, arrived):
    points, reals = weights.shape[0], arrived[0].shape[1]
    return call(
        functools.partial(gaps_kernel, len(arrived)),
        jax.ShapeDtypeStruct((points, reals), F32),
        [VMEM] * (1 + len(arrived)),
        (weights, *arrived),
        12 * weights.size * reals, 4 * points * reals,
        [pltpu.VMEM((weights.shape[1], reals), F32)],
    )


def diagonals_kernel(*refs):
    half = len(refs) // 2
    for blocks, out in zip(refs[:half], refs[half:]):
        modules = blocks.shape[1]
        width = 6 * modules
        lane = lax.broadcasted_iota(jnp.int32, (modules, width), 1) // 6
        module = lax.broadcasted_iota(jnp.int32, (modules, width), 0)
        for i in range(6):
            spread = jnp.concatenate([blocks[i]] * modules, axis=1)
            out[pl.ds(i, modules, stride=6), :] = jnp.where(lane == module, spread, 0.0)


def diagonals(*matrices):
    width = 6 * matrices[0].shape[0]
    shape = jax.ShapeDtypeStruct((width, width), F32)
    return call(
        diagonals_kernel, (shape,) * len(matrices), [VMEM] * len(matrices),
        tuple(m.transpose(1, 0, 2) for m in matrices), 100 * width * width, 16 * width * width,
    )


def plan_kernel(rows, cols, capacity, slot_rows, owned, links, arms, send, weights, table):
    modules = send.shape[1] // 6
    points = links.shape[0] // modules
    row, col = lax.axis_index("row"), lax.axis_index("col")
    grid_index = row * cols + col
    first_module = grid_index * modules
    shape = (slot_rows, modules * 6)
    i = lax.broadcasted_iota(jnp.int32, shape, 0)
    j = lax.broadcasted_iota(jnp.int32, shape, 1)
    for d in range(rows):
        listed = (sends_to(row, d, rows) * cols + col) * modules
        wanted = jnp.full(shape, -1, jnp.int32)
        for k in range(modules):
            local = owned[listed + k] - first_module
            here = (local >= 0) & (local < modules)
            wanted = jnp.where((i // 6 == k % capacity) & here, local, wanted)
        hit = (wanted == j // 6) & (i % 6 == j % 6)
        send[d * slot_rows : (d + 1) * slot_rows, :] = jnp.where(hit, 1.0, 0.0)
    count = modules * points
    table[:, 0:3] = arms[...]
    for q in range(modules):
        home = owned[first_module + q] // (cols * modules)
        home_d = home ^ row if rows & (rows - 1) == 0 else (row + rows - home) % rows
        place = home_d * slot_rows + (q % capacity) * 6
        table[q * points : (q + 1) * points, 3:4] = jnp.full((points, 1), place, jnp.int32).astype(F32)
    own = table[...]
    point = lax.broadcasted_iota(jnp.int32, (count, count), 1)
    meets = jnp.where(links[...] - first_module * points == point, 1.0, 0.0)
    partner = dot_exact(meets, own)
    wide = (count, rows * slot_rows)
    column = lax.broadcasted_iota(jnp.int32, wide, 1)
    total = [None] * 3
    for sign, side in ((1.0, own), (-1.0, partner)):
        mode = column - (side[:, 3:4] + 0.5).astype(jnp.int32)
        e = [jnp.broadcast_to(sign * side[:, c : c + 1], wide) for c in range(3)]
        for c in range(3):
            up, down = (c + 1) % 3, (c + 2) % 3
            value = jnp.where(mode == c, sign, 0.0)
            value = jnp.where(mode == 3 + up, e[down], value)
            value = jnp.where(mode == 3 + down, -e[up], value)
            total[c] = value if total[c] is None else total[c] + value
    for q in range(modules):
        for c in range(3):
            start = (q * 3 + c) * points
            weights[start : start + points, :] = total[c][q * points : (q + 1) * points, :]


def plan(owned, links, arms, rows, cols):
    modules, points = links.shape
    capacity = 2 * modules // rows
    slot_rows = -(-capacity * 6 // 8) * 8
    return call(
        functools.partial(plan_kernel, rows, cols, capacity, slot_rows),
        (
            jax.ShapeDtypeStruct((rows * slot_rows, modules * 6), F32),
            jax.ShapeDtypeStruct((modules * 3 * points, rows * slot_rows), F32),
        ),
        [SMEM, VMEM, VMEM],
        (owned, links.reshape(-1, 1), arms.transpose(0, 2, 1).reshape(-1, 3)),
        12 * (modules * points) ** 2 * 4, 4 * modules * 3 * points * rows * slot_rows,
        [pltpu.VMEM((modules * points, 4), F32)],
    )


def after(value, *others):
    return lax.optimization_barrier((value, *others))[0]


def body(
    kernel,
    history,
    displacement,
    velocity,
    acceleration,
    excitation,
    solve_inverse,
    stiffness,
    owned,
    links,
    arms,
):
    rows, cols = lax.axis_size("row"), lax.axis_size("col")
    steps = excitation.shape[0]
    slab, reals = velocity.shape
    modules, points = links.shape
    x, v, a = displacement, velocity, acceleration
    arrived = exchange([v.astype(BF16)] * rows, "row")
    lags, bases = known_forces(
        kernel.reshape(-1, kernel.shape[3]), history.reshape(-1, reals), rows * slab, steps
    )
    inverse, stiff = diagonals(solve_inverse, stiffness)
    for n in range(steps):
        predicted, load = prepare(x, v, a, excitation[n], stiff)
        pieces, bases = force_pieces(lags, arrived, bases, cols)
        if n == 0:
            send, weights = plan(after(owned, pieces[0]), links, arms, rows, cols)
        parts = exchange(pieces, "col")
        if n < steps - 1:
            x, v, a, v_half = advance(parts, predicted, v, a, load, inverse)
            arrived = exchange([v_half] * rows, "row")
        else:
            v, sends = finish(parts, predicted, v, a, load, inverse, send, rows)
    moved = exchange(sends, "row")
    out = gaps(weights, moved).reshape(modules, 3, points, reals)
    return v, out.transpose(0, 2, 1, 3)


def solution(mesh):
    placed = (
        P(None, None, "col", "row"),
        P(None, None, "col", "sea"),
        P(("row", "col"), "sea"),
        P(("row", "col"), "sea"),
        P(("row", "col"), "sea"),
        P(None, ("row", "col"), "sea"),
        P(("row", "col"), None, None),
        P(("row", "col"), None, None),
        P(),
        P(("row", "col"), None),
        P(("row", "col"), None, None),
    )
    return jax.shard_map(
        body,
        mesh=mesh,
        in_specs=placed,
        out_specs=(P(("row", "col"), "sea"), P(("row", "col"), None, None, "sea")),
        check_vma=False,
    )
```

```python
import functools

import jax
import jax.numpy as jnp
from jax import lax
from jax.experimental import pallas as pl
from jax.experimental.pallas import tpu as pltpu
from jax.sharding import PartitionSpec as P


DT = 0.5
QUARTER = DT * DT / 4.0
F32 = jnp.float32
BF16 = jnp.bfloat16
HIGHEST = lax.Precision.HIGHEST
VMEM = pl.BlockSpec(memory_space=pltpu.VMEM)
SMEM = pl.BlockSpec(memory_space=pltpu.SMEM)


def sends_to(i, d, n):
    return i ^ d if n & (n - 1) == 0 else (i + d) % n


def comes_from(i, d, n):
    return i ^ d if n & (n - 1) == 0 else (i + n - d) % n


def exchange(pieces, axis):
    n = lax.axis_size(axis)
    out = [pieces[0]] + [None] * (n - 1)
    for d in range(n - 1, 0, -1):
        out[d] = lax.ppermute(pieces[d], axis, [(i, sends_to(i, d, n)) for i in range(n)])
    return out


def dot_rows(a, b):
    return lax.dot_general(a, b, (((0,), (0,)), ((), ())), preferred_element_type=F32)


def dot_exact(a, b):
    return jnp.dot(a, b, precision=HIGHEST, preferred_element_type=F32)


def padded_bytes(shape, dtype):
    size = jnp.dtype(dtype).itemsize
    dims = (1, 1, *shape)
    up = lambda n, m: -(-n // m) * m
    major = 1
    for n in dims[:-2]:
        major *= n
    return major * up(dims[-2], 32 // size) * up(dims[-1], 128) * size


def call(body, shapes, in_specs, args, flops, nbytes, scratch=()):
    arrays = list(args) + jax.tree.leaves(shapes)
    held = sum(padded_bytes(t.shape, t.dtype) for t in arrays)
    held += sum(padded_bytes(t.shape, t.dtype) for t in scratch if t.shape[1:])
    return pl.pallas_call(
        body,
        out_shape=shapes,
        in_specs=in_specs,
        out_specs=jax.tree.map(lambda _: VMEM, shapes),
        scratch_shapes=scratch,
        compiler_params=pltpu.CompilerParams(
            vmem_limit_bytes=min(2 * held + (2 << 20), 60 << 20)
        ),
        cost_estimate=pl.CostEstimate(flops=flops, bytes_accessed=nbytes, transcendentals=0),
    )(*args)


def known_kernel(lag_rows, steps, per, k_hbm, h_hbm, lags_ref, *refs):
    outs, (k_ref, h_ref, k_sem, h_sem) = refs[:steps], refs[steps:]
    total, known = k_ref.shape[0], h_ref.shape[0]
    size = per * lag_rows
    count = -(-total // size)
    copies = []
    for i in range(count):
        k_rows = pl.ds(i * size, min(size, total - i * size))
        h_rows = pl.ds(i * size, min(size, known - i * size))
        pair = (
            pltpu.make_async_copy(k_hbm.at[k_rows], k_ref.at[k_rows], k_sem.at[i]),
            pltpu.make_async_copy(h_hbm.at[h_rows], h_ref.at[h_rows], h_sem.at[i]),
        )
        pair[0].start()
        pair[1].start()
        copies.append(pair)
    for i in range(count):
        copies[i][0].wait()
        copies[i][1].wait()
        for s in range(steps):
            first = max(i * size, (s + 1) * lag_rows)
            last = min((i + 1) * size, total)
            if first >= last:
                continue
            shift = (s + 1) * lag_rows
            term = dot_rows(k_ref[first:last, :], h_ref[first - shift : last - shift, :])
            outs[s][...] = term if i == 0 else outs[s][...] + term
    lags_ref[...] = k_ref[: steps * lag_rows, :]


def known_forces(kernel_flat, history_flat, lag_rows, steps):
    block = kernel_flat.shape[1]
    shape = jax.ShapeDtypeStruct((block, history_flat.shape[1]), F32)
    per = steps + 1
    count = -(-kernel_flat.shape[0] // (per * lag_rows))
    out = call(
        functools.partial(known_kernel, lag_rows, steps, per),
        (jax.ShapeDtypeStruct((steps * lag_rows, block), BF16),) + (shape,) * steps,
        [pl.BlockSpec(memory_space=pltpu.MemorySpace.HBM)] * 2,
        tuple(
            pltpu.with_memory_space_constraint(t, pltpu.MemorySpace.HBM)
            for t in (kernel_flat, history_flat)
        ),
        2 * steps * kernel_flat.size * history_flat.shape[1],
        2 * (kernel_flat.size + history_flat.size),
        [
            pltpu.VMEM(kernel_flat.shape, BF16),
            pltpu.VMEM(history_flat.shape, BF16),
            pltpu.SemaphoreType.DMA((count,)),
            pltpu.SemaphoreType.DMA((count,)),
        ],
    )
    return out[0], out[1:]


def force_kernel(rows, cols, ahead, *refs):
    k_ref = refs[0]
    arrived = refs[1 : 1 + rows]
    bases = refs[1 + rows : 1 + rows + ahead]
    outs = refs[1 + rows + ahead : -2]
    chunks, later = outs[:cols], outs[cols:]
    whole, total = refs[-2:]
    slab = arrived[0].shape[0]
    row, col = lax.axis_index("row"), lax.axis_index("col")
    for d in range(rows):
        start = pl.multiple_of(comes_from(row, d, rows) * slab, 16)
        whole[pl.ds(start, slab), :] = arrived[d][...].astype(BF16)
    lag_rows = rows * slab
    total[...] = bases[0][...] + dot_rows(k_ref[:lag_rows, :], whole[...])
    for d in range(cols):
        start = pl.multiple_of(sends_to(col, d, cols) * slab, 8)
        chunks[d][...] = total[pl.ds(start, slab), :]
    for n in range(1, ahead):
        later[n - 1][...] = bases[n][...] + dot_rows(
            k_ref[n * lag_rows : (n + 1) * lag_rows, :], whole[...]
        )


def force_pieces(kernel_lags, arrived, bases, cols):
    rows, ahead = len(arrived), len(bases)
    slab, reals = arrived[0].shape
    block = kernel_lags.shape[1]
    shapes = (jax.ShapeDtypeStruct((slab, reals), F32),) * cols + (
        jax.ShapeDtypeStruct((block, reals), F32),
    ) * (ahead - 1)
    out = call(
        functools.partial(force_kernel, rows, cols, ahead),
        shapes,
        [VMEM] * (1 + rows + ahead),
        (kernel_lags, *arrived, *bases),
        2 * ahead * rows * slab * block * reals,
        4 * 2 * ahead * block * reals,
        [pltpu.VMEM((rows * slab, reals), BF16), pltpu.VMEM((block, reals), F32)],
    )
    return out[:cols], out[cols:]


def prepare_kernel(x, v, a, e, stiff, predicted, load):
    p = x[...] + DT * v[...] + QUARTER * a[...]
    predicted[...] = p
    load[...] = e[...] - dot_exact(stiff[...], p)


def prepare(x, v, a, e, stiff):
    shape = jax.ShapeDtypeStruct(x.shape, F32)
    return call(
        prepare_kernel, (shape, shape), [VMEM] * 5, (x, v, a, e, stiff),
        12 * x.size * x.shape[0], 24 * x.size,
    )


def advance_kernel(cols, *refs):
    parts = refs[:cols]
    predicted, v, a, load, inverse = refs[cols : cols + 5]
    x_out, v_out, a_out, v_half = refs[cols + 5 :]
    force = parts[0][...]
    for part in parts[1:]:
        force = force + part[...]
    a_next = dot_exact(inverse[...], load[...] - force)
    v_next = v[...] + 0.5 * DT * (a[...] + a_next)
    v_half[...] = v_next.astype(BF16)
    v_out[...] = v_next
    a_out[...] = a_next
    x_out[...] = predicted[...] + QUARTER * a_next


def advance(parts, predicted, v, a, load, inverse):
    shape = jax.ShapeDtypeStruct(v.shape, F32)
    return call(
        functools.partial(advance_kernel, len(parts)),
        (shape, shape, shape, jax.ShapeDtypeStruct(v.shape, BF16)),
        [VMEM] * (len(parts) + 5),
        (*parts, predicted, v, a, load, inverse),
        12 * v.size * v.shape[0], 40 * v.size,
    )


def finish_kernel(cols, rows, *refs):
    parts = refs[:cols]
    predicted, v, a, load, inverse, route = refs[cols : cols + 6]
    v_out, *sends = refs[cols + 6 :]
    force = parts[0][...]
    for part in parts[1:]:
        force = force + part[...]
    a_next = dot_exact(inverse[...], load[...] - force)
    v_out[...] = v[...] + 0.5 * DT * (a[...] + a_next)
    x_next = predicted[...] + QUARTER * a_next
    moved = dot_exact(route[...], x_next)
    size = route.shape[0] // rows
    for d in range(rows):
        sends[d][...] = moved[d * size : (d + 1) * size, :]


def finish(parts, predicted, v, a, load, inverse, route, rows):
    shapes = (jax.ShapeDtypeStruct(v.shape, F32),) + (
        jax.ShapeDtypeStruct((route.shape[0] // rows, v.shape[1]), F32),
    ) * rows
    out = call(
        functools.partial(finish_kernel, len(parts), rows),
        shapes,
        [VMEM] * (len(parts) + 6),
        (*parts, predicted, v, a, load, inverse, route),
        12 * v.size * v.shape[0], 40 * v.size,
    )
    return out[0], out[1:]


def settle_kernel(v, out):
    out[...] = v[...]


def settle(v):
    return call(settle_kernel, jax.ShapeDtypeStruct(v.shape, F32), [VMEM], (v,), v.size, 8 * v.size)


def gaps_kernel(rows, modules, *refs):
    weights, arrived, out, held, done, sems = refs[0], refs[1 : 1 + rows], *refs[1 + rows :]
    size = arrived[0].shape[0]
    for d in range(rows):
        held[d * size : (d + 1) * size, :] = arrived[d][...]
    pieces = 4 if modules % 4 == 0 else 1
    lines = weights.shape[0] // pieces
    copies = []
    for i in range(pieces):
        at = pl.ds(i * lines, lines)
        done[at, :] = dot_exact(weights[at, :], held[...])
        copies.append(pltpu.make_async_copy(done.at[at], out.at[at], sems.at[i]))
        copies[-1].start()
    for copy in copies:
        copy.wait()


def gaps(weights, arrived, modules):
    points, reals = weights.shape[0], arrived[0].shape[1]
    shape = jax.ShapeDtypeStruct((points, reals), F32)
    return pl.pallas_call(
        functools.partial(gaps_kernel, len(arrived), modules),
        out_shape=shape,
        in_specs=[VMEM] * (1 + len(arrived)),
        out_specs=pl.BlockSpec(memory_space=pltpu.MemorySpace.HBM),
        scratch_shapes=[
            pltpu.VMEM((weights.shape[1], reals), F32),
            pltpu.VMEM((points, reals), F32),
            pltpu.SemaphoreType.DMA((4,)),
        ],
        compiler_params=pltpu.CompilerParams(vmem_limit_bytes=16 << 20),
        cost_estimate=pl.CostEstimate(
            flops=12 * weights.size * reals, bytes_accessed=4 * points * reals, transcendentals=0
        ),
    )(weights, *arrived)


def diagonals_kernel(*refs):
    half = len(refs) // 2
    for blocks, out in zip(refs[:half], refs[half:]):
        modules = blocks.shape[1]
        width = 6 * modules
        lane = lax.broadcasted_iota(jnp.int32, (modules, width), 1) // 6
        module = lax.broadcasted_iota(jnp.int32, (modules, width), 0)
        for i in range(6):
            spread = jnp.concatenate([blocks[i]] * modules, axis=1)
            out[pl.ds(i, modules, stride=6), :] = jnp.where(lane == module, spread, 0.0)


def diagonals(*matrices):
    width = 6 * matrices[0].shape[0]
    shape = jax.ShapeDtypeStruct((width, width), F32)
    return call(
        diagonals_kernel, (shape,) * len(matrices), [VMEM] * len(matrices),
        tuple(m.transpose(1, 0, 2) for m in matrices), 100 * width * width, 16 * width * width,
    )


def plan_kernel(rows, cols, capacity, slot_rows, owned, links, arms, send, weights, table):
    modules = send.shape[1] // 6
    points = links.shape[0] // modules
    row, col = lax.axis_index("row"), lax.axis_index("col")
    grid_index = row * cols + col
    first_module = grid_index * modules
    shape = (slot_rows, modules * 6)
    i = lax.broadcasted_iota(jnp.int32, shape, 0)
    j = lax.broadcasted_iota(jnp.int32, shape, 1)
    for d in range(rows):
        listed = (sends_to(row, d, rows) * cols + col) * modules
        wanted = jnp.full(shape, -1, jnp.int32)
        for k in range(modules):
            local = owned[listed + k] - first_module
            here = (local >= 0) & (local < modules)
            wanted = jnp.where((i // 6 == k % capacity) & here, local, wanted)
        hit = (wanted == j // 6) & (i % 6 == j % 6)
        send[d * slot_rows : (d + 1) * slot_rows, :] = jnp.where(hit, 1.0, 0.0)
    count = modules * points
    table[:, 0:3] = arms[...]
    for q in range(modules):
        home = owned[first_module + q] // (cols * modules)
        home_d = home ^ row if rows & (rows - 1) == 0 else (row + rows - home) % rows
        place = home_d * slot_rows + (q % capacity) * 6
        table[q * points : (q + 1) * points, 3:4] = jnp.full((points, 1), place, jnp.int32).astype(F32)
    own = table[...]
    point = lax.broadcasted_iota(jnp.int32, (count, count), 1)
    meets = jnp.where(links[...] - first_module * points == point, 1.0, 0.0)
    partner = dot_exact(meets, own)
    wide = (count, rows * slot_rows)
    column = lax.broadcasted_iota(jnp.int32, wide, 1)
    total = [None] * 3
    for sign, side in ((1.0, own), (-1.0, partner)):
        mode = column - (side[:, 3:4] + 0.5).astype(jnp.int32)
        e = [jnp.broadcast_to(sign * side[:, c : c + 1], wide) for c in range(3)]
        for c in range(3):
            up, down = (c + 1) % 3, (c + 2) % 3
            value = jnp.where(mode == c, sign, 0.0)
            value = jnp.where(mode == 3 + up, e[down], value)
            value = jnp.where(mode == 3 + down, -e[up], value)
            total[c] = value if total[c] is None else total[c] + value
    for q in range(modules):
        for c in range(3):
            start = (q * 3 + c) * points
            weights[start : start + points, :] = total[c][q * points : (q + 1) * points, :]


def plan(owned, links, arms, rows, cols):
    modules, points = links.shape
    capacity = 2 * modules // rows
    slot_rows = -(-capacity * 6 // 8) * 8
    return call(
        functools.partial(plan_kernel, rows, cols, capacity, slot_rows),
        (
            jax.ShapeDtypeStruct((rows * slot_rows, modules * 6), F32),
            jax.ShapeDtypeStruct((modules * 3 * points, rows * slot_rows), F32),
        ),
        [SMEM, VMEM, VMEM],
        (owned, links.reshape(-1, 1), arms.transpose(0, 2, 1).reshape(-1, 3)),
        12 * (modules * points) ** 2 * 4, 4 * modules * 3 * points * rows * slot_rows,
        [pltpu.VMEM((modules * points, 4), F32)],
    )


def after(value, *others):
    return lax.optimization_barrier((value, *others))[0]


def body(
    kernel,
    history,
    displacement,
    velocity,
    acceleration,
    excitation,
    solve_inverse,
    stiffness,
    owned,
    links,
    arms,
):
    rows, cols = lax.axis_size("row"), lax.axis_size("col")
    steps = excitation.shape[0]
    slab, reals = velocity.shape
    modules, points = links.shape
    x, v, a = displacement, velocity, acceleration
    arrived = exchange([v] * rows, "row")
    lags, bases = known_forces(
        kernel.reshape(-1, kernel.shape[3]), history.reshape(-1, reals), rows * slab, steps
    )
    inverse, stiff = diagonals(solve_inverse, stiffness)
    for n in range(steps):
        predicted, load = prepare(x, v, a, excitation[n], stiff)
        pieces, bases = force_pieces(lags, arrived, bases, cols)
        if n == 0:
            send, weights = plan(after(owned, pieces[0]), links, arms, rows, cols)
        parts = exchange(pieces, "col")
        if n < steps - 1:
            x, v, a, v_half = advance(parts, predicted, v, a, load, inverse)
            arrived = exchange([v_half] * rows, "row")
        else:
            v, sends = finish(parts, predicted, v, a, load, inverse, send, rows)
    moved = exchange(sends, "row")
    v = settle(v)
    out = gaps(weights, moved, modules).reshape(modules, 3, points, reals)
    return v, out.transpose(0, 2, 1, 3)


def solution(mesh):
    placed = (
        P(None, None, "col", "row"),
        P(None, None, "col", "sea"),
        P(("row", "col"), "sea"),
        P(("row", "col"), "sea"),
        P(("row", "col"), "sea"),
        P(None, ("row", "col"), "sea"),
        P(("row", "col"), None, None),
        P(("row", "col"), None, None),
        P(),
        P(("row", "col"), None),
        P(("row", "col"), None, None),
    )
    return jax.shard_map(
        body,
        mesh=mesh,
        in_specs=placed,
        out_specs=(P(("row", "col"), "sea"), P(("row", "col"), None, None, "sea")),
        check_vma=False,
    )
```

```python
import functools

import jax
import jax.numpy as jnp
from jax import lax
from jax.experimental import pallas as pl
from jax.experimental.pallas import tpu as pltpu
from jax.sharding import PartitionSpec as P


DT = 0.5
QUARTER = DT * DT / 4.0
F32 = jnp.float32
BF16 = jnp.bfloat16
HIGHEST = lax.Precision.HIGHEST
VMEM = pl.BlockSpec(memory_space=pltpu.VMEM)
SMEM = pl.BlockSpec(memory_space=pltpu.SMEM)


def sends_to(i, d, n):
    return i ^ d if n & (n - 1) == 0 else (i + d) % n


def comes_from(i, d, n):
    return i ^ d if n & (n - 1) == 0 else (i + n - d) % n


def exchange(pieces, axis):
    n = lax.axis_size(axis)
    out = [pieces[0]] + [None] * (n - 1)
    for d in range(n - 1, 0, -1):
        out[d] = lax.ppermute(pieces[d], axis, [(i, sends_to(i, d, n)) for i in range(n)])
    return out


def dot_rows(a, b):
    return lax.dot_general(a, b, (((0,), (0,)), ((), ())), preferred_element_type=F32)


def dot_exact(a, b):
    return jnp.dot(a, b, precision=HIGHEST, preferred_element_type=F32)


def padded_bytes(shape, dtype):
    size = jnp.dtype(dtype).itemsize
    dims = (1, 1, *shape)
    up = lambda n, m: -(-n // m) * m
    major = 1
    for n in dims[:-2]:
        major *= n
    return major * up(dims[-2], 32 // size) * up(dims[-1], 128) * size


def call(body, shapes, in_specs, args, flops, nbytes, scratch=()):
    arrays = list(args) + jax.tree.leaves(shapes)
    held = sum(padded_bytes(t.shape, t.dtype) for t in arrays)
    held += sum(padded_bytes(t.shape, t.dtype) for t in scratch if t.shape[1:])
    return pl.pallas_call(
        body,
        out_shape=shapes,
        in_specs=in_specs,
        out_specs=jax.tree.map(lambda _: VMEM, shapes),
        scratch_shapes=scratch,
        compiler_params=pltpu.CompilerParams(
            vmem_limit_bytes=min(2 * held + (2 << 20), 60 << 20)
        ),
        cost_estimate=pl.CostEstimate(flops=flops, bytes_accessed=nbytes, transcendentals=0),
    )(*args)


def known_kernel(lag_rows, steps, per, k_hbm, h_hbm, lags_ref, *refs):
    outs, (k_ref, h_ref, k_sem, h_sem) = refs[:steps], refs[steps:]
    total, known = k_ref.shape[0], h_ref.shape[0]
    size = per * lag_rows
    count = -(-total // size)
    copies = []
    for i in range(count):
        k_rows = pl.ds(i * size, min(size, total - i * size))
        h_rows = pl.ds(i * size, min(size, known - i * size))
        pair = (
            pltpu.make_async_copy(k_hbm.at[k_rows], k_ref.at[k_rows], k_sem.at[i]),
            pltpu.make_async_copy(h_hbm.at[h_rows], h_ref.at[h_rows], h_sem.at[i]),
        )
        pair[0].start()
        pair[1].start()
        copies.append(pair)
    for i in range(count):
        copies[i][0].wait()
        copies[i][1].wait()
        last = min((i + 1) * size, total)
        turned = k_ref[i * size : last, :].T if i else None
        for s in range(steps):
            shift = (s + 1) * lag_rows
            if i == 0:
                outs[s][...] = dot_rows(k_ref[shift:last, :], h_ref[: last - shift, :])
            else:
                known = h_ref[i * size - shift : last - shift, :]
                outs[s][...] += jnp.dot(turned, known, preferred_element_type=F32)
    lags_ref[...] = k_ref[: steps * lag_rows, :]


def known_forces(kernel_flat, history_flat, lag_rows, steps):
    block = kernel_flat.shape[1]
    shape = jax.ShapeDtypeStruct((block, history_flat.shape[1]), F32)
    per = steps + 1
    count = -(-kernel_flat.shape[0] // (per * lag_rows))
    out = call(
        functools.partial(known_kernel, lag_rows, steps, per),
        (jax.ShapeDtypeStruct((steps * lag_rows, block), BF16),) + (shape,) * steps,
        [pl.BlockSpec(memory_space=pltpu.MemorySpace.HBM)] * 2,
        tuple(
            pltpu.with_memory_space_constraint(t, pltpu.MemorySpace.HBM)
            for t in (kernel_flat, history_flat)
        ),
        2 * steps * kernel_flat.size * history_flat.shape[1],
        2 * (kernel_flat.size + history_flat.size),
        [
            pltpu.VMEM(kernel_flat.shape, BF16),
            pltpu.VMEM(history_flat.shape, BF16),
            pltpu.SemaphoreType.DMA((count,)),
            pltpu.SemaphoreType.DMA((count,)),
        ],
    )
    return out[0], out[1:]


def force_kernel(cols, ahead, keep, *refs):
    lags = refs[0]
    arrived, refs = refs[1 : 1 + keep], refs[1 + keep :]
    bases, outs = refs[:ahead], refs[ahead:-2]
    chunks, later = outs[:cols], outs[cols:]
    whole, total = refs[-2:]
    rows = keep
    slab, reals = chunks[0].shape[0] // (2 if ahead == 2 else 1), chunks[0].shape[1]
    row, col = lax.axis_index("row"), lax.axis_index("col")
    for d in range(rows):
        start = pl.multiple_of(comes_from(row, d, rows) * slab, 16)
        whole[pl.ds(start, slab), :] = arrived[d][0:slab, 0:reals].astype(BF16)
    lag_rows = rows * slab
    for n in range(ahead):
        value = bases[n][...] + dot_rows(lags[n * lag_rows : (n + 1) * lag_rows, :], whole[...])
        if n == 0 or ahead == 2:
            total[...] = value
            for d in range(cols):
                start = pl.multiple_of(sends_to(col, d, cols) * slab, 8)
                chunks[d][n * slab : (n + 1) * slab, :] = total[pl.ds(start, slab), :]
        else:
            later[n - 1][...] = value


def force_pieces(lags, arrived, bases, slab, cols):
    rows, ahead = len(arrived), len(bases)
    block, reals = bases[0].shape
    both = ahead == 2
    shapes = (jax.ShapeDtypeStruct((slab * (2 if both else 1), reals), F32),) * cols
    if not both:
        shapes += (jax.ShapeDtypeStruct((block, reals), F32),) * (ahead - 1)
    out = call(
        functools.partial(force_kernel, cols, ahead, rows),
        shapes,
        [VMEM] * (1 + rows + ahead),
        (lags, *arrived, *bases),
        2 * ahead * rows * slab * block * reals,
        4 * 2 * ahead * block * reals,
        [pltpu.VMEM((rows * slab, reals), BF16), pltpu.VMEM((block, reals), F32)],
    )
    return out[:cols], out[cols:]


def prepare_kernel(x, v, a, e, stiff, predicted, load):
    p = x[...] + DT * v[...] + QUARTER * a[...]
    predicted[...] = p
    load[...] = e[...] - dot_exact(stiff[...], p)


def prepare(x, v, a, e, stiff):
    shape = jax.ShapeDtypeStruct(x.shape, F32)
    return call(
        prepare_kernel, (shape, shape), [VMEM] * 5, (x, v, a, e, stiff),
        12 * x.size * x.shape[0], 24 * x.size,
    )


def summed(parts, first, count):
    total = parts[0][first : first + count, :]
    for part in parts[1:]:
        total = total + part[first : first + count, :]
    return total


def split(value):
    out = []
    for _ in range(3):
        out.append(value.astype(BF16).astype(F32))
        value = value - out[-1]
    return out


def first_advance_kernel(cols, rows, *refs):
    parts = refs[:cols]
    predicted, v, a, load, inverse = refs[cols : cols + 5]
    riders = refs[cols + 5 : cols + 5 + rows]
    x_out, v_out, a_out, *messages = refs[cols + 5 + rows :]
    slab, reals = v.shape
    a_next = dot_exact(inverse[...], load[...] - summed(parts, 0, slab))
    v_next = v[...] + 0.5 * DT * (a[...] + a_next)
    v_half = v_next.astype(BF16)
    for message, rider in zip(messages, riders):
        message[0:slab, 0:reals] = v_half
        message[slab:, :] = rider[...]
    v_out[...] = v_next
    a_out[...] = a_next
    x_out[...] = predicted[...] + QUARTER * a_next


def first_advance(parts, predicted, v, a, load, inverse, riders):
    shape = jax.ShapeDtypeStruct(v.shape, F32)
    lines, lanes = riders[0].shape
    message = jax.ShapeDtypeStruct((v.shape[0] + lines, lanes), BF16)
    out = call(
        functools.partial(first_advance_kernel, len(parts), len(riders)),
        (shape,) * 3 + (message,) * len(riders),
        [VMEM] * (len(parts) + 5 + len(riders)),
        (*parts, predicted, v, a, load, inverse, *riders),
        12 * v.size * v.shape[0], 40 * v.size,
    )
    return out[0], out[1], out[2], out[3:]


def last_advance_kernel(cols, rows, *refs):
    parts = refs[:cols]
    predicted, v, a, load, e, inverse, stiff, send = refs[cols : cols + 8]
    settled, *messages = refs[cols + 8 : -1]
    held = refs[-1]
    slab, _ = v.shape
    size = send.shape[0] // rows
    a_next = dot_exact(inverse[...], load[...] - summed(parts, 0, slab))
    v_next = v[...] + 0.5 * DT * (a[...] + a_next)
    x_next = predicted[...] + QUARTER * a_next
    ahead = x_next + DT * v_next + QUARTER * a_next
    known = e[...] - summed(parts, slab, slab) - dot_exact(stiff[...], ahead)
    push = dot_exact(inverse[...], known)
    settled[...] = v_next + 0.5 * DT * (a_next + push)
    moved = dot_exact(send[...], ahead + QUARTER * push)
    v_half = v_next.astype(BF16)
    cuts = split(moved)
    for d in range(rows):
        for k in range(3):
            held[k * size : (k + 1) * size, :] = cuts[k][d * size : (d + 1) * size, :]
        messages[d][0:slab, :] = v_half
        messages[d][slab:, :] = held[...].astype(BF16)


def last_advance(parts, predicted, v, a, load, e, inverse, stiff, send, rows):
    slab, reals = v.shape
    size = send.shape[0] // rows
    out = call(
        functools.partial(last_advance_kernel, len(parts), rows),
        (jax.ShapeDtypeStruct(v.shape, F32),)
        + (jax.ShapeDtypeStruct((slab + 3 * size, reals), BF16),) * rows,
        [VMEM] * (len(parts) + 8),
        (*parts, predicted, v, a, load, e, inverse, stiff, send),
        48 * v.size * slab, 40 * v.size,
        [pltpu.VMEM((3 * size, reals), F32)],
    )
    return out[0], out[1:]


def last_force_kernel(cols, rows, *refs):
    lags, listed = refs[0], refs[1]
    arrived = refs[2 : 2 + rows]
    chunks, (whole, total) = refs[2 + rows : -2], refs[-2:]
    slab = chunks[0].shape[0] // 2
    row, col = lax.axis_index("row"), lax.axis_index("col")
    for d in range(rows):
        start = pl.multiple_of(comes_from(row, d, rows) * slab, 16)
        whole[pl.ds(start, slab), :] = arrived[d][0:slab, :]
    newest = whole[...]
    total[0] = dot_rows(lags[0 : rows * slab, :], newest)
    total[1] = jnp.dot(listed[...], newest, preferred_element_type=F32)
    for d in range(cols):
        start = pl.multiple_of(sends_to(col, d, cols) * slab, 8)
        for k in range(2):
            chunks[d][k * slab : (k + 1) * slab, :] = total[k, pl.ds(start, slab), :]


def last_force(lags, listed, arrived, slab, cols):
    rows, block, reals = len(arrived), lags.shape[1], arrived[0].shape[1]
    return call(
        functools.partial(last_force_kernel, cols, rows),
        (jax.ShapeDtypeStruct((2 * slab, reals), F32),) * cols,
        [VMEM] * (2 + rows),
        (lags, listed, *arrived),
        4 * rows * slab * block * reals, 8 * block * reals,
        [pltpu.VMEM((rows * slab, reals), BF16), pltpu.VMEM((2, block, reals), F32)],
    )


def listed_kernel(rows, cols, slab, lag_rows, *refs):
    arrived, (take, own_take, weights) = refs[:rows], refs[rows : rows + 3]
    listed, pull, held, stack, blocks = refs[rows + 3 :]
    size = own_take.shape[1] // rows
    modules = slab // 6
    for d in range(rows):
        held[...] = arrived[d][slab:, :].astype(F32)
        for c in range(cols):
            stack[c, d * size : (d + 1) * size, :] = held[c * size : (c + 1) * size, 0:lag_rows]
        cuts = [held[0:size, lag_rows + 6 * k : lag_rows + 6 * k + 6] for k in range(3)]
        blocks[d * size : (d + 1) * size, :] = (cuts[2] + cuts[1]) + cuts[0]
    for c in range(cols):
        found = jnp.dot(take[c].astype(BF16), stack[c].astype(BF16), preferred_element_type=F32)
        listed[c * slab : (c + 1) * slab, :] = found.astype(BF16)
    block = dot_exact(own_take[...], blocks[...])
    lane = lax.broadcasted_iota(jnp.int32, (slab, slab), 1) // 6
    module = lax.broadcasted_iota(jnp.int32, (slab, slab), 0) // 6
    inverse = jnp.where(lane == module, jnp.concatenate([block] * modules, axis=1), 0.0)
    pull[...] = QUARTER * dot_exact(weights[...], inverse)


def listed_parts(arrived, take, own_take, weights, slab, lag_rows):
    rows, cols = len(arrived), take.shape[0]
    lines, lanes = arrived[0].shape
    return call(
        functools.partial(listed_kernel, rows, cols, slab, lag_rows),
        (
            jax.ShapeDtypeStruct((cols * slab, lag_rows), BF16),
            jax.ShapeDtypeStruct(weights.shape, F32),
        ),
        [VMEM] * (rows + 3),
        (*arrived, take, own_take, weights),
        4 * take.size * lag_rows, 4 * take.size,
        [
            pltpu.VMEM((lines - slab, lanes), F32),
            pltpu.VMEM((cols, own_take.shape[1], lag_rows), F32),
            pltpu.VMEM((own_take.shape[1], 6), F32),
        ],
    )


def settled_gaps_kernel(rows, *refs):
    arrived, (own_take, weights, out, held) = refs[:rows], refs[rows:]
    size = own_take.shape[1] // rows
    slab = own_take.shape[0]
    for d in range(rows):
        cuts = arrived[d][slab:, :].astype(F32)
        held[d * size : (d + 1) * size, :] = (
            cuts[2 * size : 3 * size, :] + cuts[size : 2 * size, :]
        ) + cuts[0:size, :]
    out[...] = dot_exact(weights[...], dot_exact(own_take[...], held[...]))


def settled_gaps(arrived, own_take, weights):
    rows, reals = len(arrived), arrived[0].shape[1]
    return call(
        functools.partial(settled_gaps_kernel, rows),
        jax.ShapeDtypeStruct((weights.shape[0], reals), F32),
        [VMEM] * (rows + 2),
        (*arrived, own_take, weights),
        12 * weights.size * reals, 4 * weights.shape[0] * reals,
        [pltpu.VMEM((own_take.shape[1], reals), F32)],
    )


def end_kernel(cols, pieces, *refs):
    parts = refs[:cols]
    settled, inverse, known, pull, v_out, out, v_done, done, sems = refs[cols:]
    slab = settled.shape[0]
    lines = known.shape[0] // pieces
    force = summed(parts, slab, slab)
    copies = []
    for i in range(pieces):
        at = pl.ds(i * lines, lines)
        done[at, :] = known[at, :] - dot_exact(pull[at, :], force)
        copies.append(pltpu.make_async_copy(done.at[at], out.at[at], sems.at[i]))
        copies[-1].start()
        if i == 0:
            push = dot_exact(inverse[...], summed(parts, 0, slab))
            v_done[...] = settled[...] - 0.5 * DT * push
            copies.append(pltpu.make_async_copy(v_done, v_out, sems.at[pieces]))
            copies[-1].start()
    for copy in copies:
        copy.wait()


def end(parts, settled, inverse, known, pull, pieces):
    hbm = pl.BlockSpec(memory_space=pltpu.MemorySpace.HBM)
    v_shape = jax.ShapeDtypeStruct(settled.shape, F32)
    shape = jax.ShapeDtypeStruct(known.shape, F32)
    return pl.pallas_call(
        functools.partial(end_kernel, len(parts), pieces),
        out_shape=(v_shape, shape),
        in_specs=[VMEM] * (len(parts) + 4),
        out_specs=(hbm, hbm),
        scratch_shapes=[
            pltpu.VMEM(settled.shape, F32),
            pltpu.VMEM(known.shape, F32),
            pltpu.SemaphoreType.DMA((pieces + 1,)),
        ],
        compiler_params=pltpu.CompilerParams(vmem_limit_bytes=16 << 20),
        cost_estimate=pl.CostEstimate(
            flops=12 * pull.size * settled.shape[1], bytes_accessed=8 * known.size, transcendentals=0
        ),
    )(*parts, settled, inverse, known, pull)


def diagonals_kernel(*refs):
    half = len(refs) // 2
    for blocks, out in zip(refs[:half], refs[half:]):
        modules = blocks.shape[1]
        width = 6 * modules
        lane = lax.broadcasted_iota(jnp.int32, (modules, width), 1) // 6
        module = lax.broadcasted_iota(jnp.int32, (modules, width), 0)
        for i in range(6):
            spread = jnp.concatenate([blocks[i]] * modules, axis=1)
            out[pl.ds(i, modules, stride=6), :] = jnp.where(lane == module, spread, 0.0)


def diagonals(*matrices):
    width = 6 * matrices[0].shape[0]
    shape = jax.ShapeDtypeStruct((width, width), F32)
    return call(
        diagonals_kernel, (shape,) * len(matrices), [VMEM] * len(matrices),
        tuple(m.transpose(1, 0, 2) for m in matrices), 100 * width * width, 16 * width * width,
    )


def plan_kernel(rows, cols, capacity, size, *refs):
    owned, links, arms, lags, blocks = refs[:5]
    riders = refs[5 : 5 + rows]
    send, take, own_take, weights, table, sends, coef, turned, held = refs[5 + rows :]
    modules = weights.shape[1] // 6
    points = links.shape[0] // modules
    row, col = lax.axis_index("row"), lax.axis_index("col")
    slab, lag_rows = modules * 6, turned.shape[1]
    turned[...] = lags[0:lag_rows, :].T
    shape = (size, slab)
    i = lax.broadcasted_iota(jnp.int32, shape, 0)
    j = lax.broadcasted_iota(jnp.int32, shape, 1)
    wide = (slab, rows * size)
    p = lax.broadcasted_iota(jnp.int32, wide, 0)
    q = lax.broadcasted_iota(jnp.int32, wide, 1)
    for c in range(cols):
        home = (row * cols + c) * modules
        for d in range(rows):
            first = (sends_to(row, d, rows) * cols + c) * modules
            wanted = jnp.full(shape, -1, jnp.int32)
            for k in range(modules):
                local = owned[first + k] - home
                here = (local >= 0) & (local < modules)
                wanted = jnp.where((i // 6 == k % capacity) & here, local, wanted)
            hit = (wanted == j // 6) & (i % 6 == j % 6)
            sends[c, d * size : (d + 1) * size, :] = jnp.where(hit, 1.0, 0.0)
        place = p % 6
        for k in range(modules):
            source = owned[home + k] // (cols * modules)
            d = source ^ row if rows & (rows - 1) == 0 else (row + rows - source) % rows
            place = place + jnp.where(p // 6 == k, d * size + k % capacity * 6, 0)
        take[c] = jnp.where(place == q, 1.0, 0.0)
        picked = jnp.dot(
            sends[c].astype(BF16), turned[c * slab : (c + 1) * slab, :], preferred_element_type=F32
        )
        for d in range(rows):
            held[d, c * size : (c + 1) * size, 0:lag_rows] = picked[d * size : (d + 1) * size, :]
    send[...] = sends[col]
    own_take[...] = take[col]
    for k in range(6):
        coef[pl.ds(k, modules, stride=6), :] = blocks[k]
    cuts = jnp.concatenate(split(dot_exact(send[...], coef[...])), axis=1)
    for d in range(rows):
        held[d, 0:size, lag_rows : lag_rows + 18] = cuts[d * size : (d + 1) * size, :]
        riders[d][...] = held[d].astype(BF16)
    count = modules * points
    table[:, 0:3] = arms[...]
    position = lax.broadcasted_iota(jnp.int32, (count, 1), 0)
    table[:, 3:4] = (position // points * 6).astype(F32)
    own = table[...]
    first_point = (row * cols + col) * count
    point = lax.broadcasted_iota(jnp.int32, (count, count), 1)
    meets = jnp.where(links[...] - first_point == point, 1.0, 0.0)
    partner = dot_exact(meets, own)
    deep = (count, slab)
    column = lax.broadcasted_iota(jnp.int32, deep, 1)
    total = [None] * 3
    for sign, side in ((1.0, own), (-1.0, partner)):
        mode = column - (side[:, 3:4] + 0.5).astype(jnp.int32)
        e = [jnp.broadcast_to(sign * side[:, c : c + 1], deep) for c in range(3)]
        for c in range(3):
            up, down = (c + 1) % 3, (c + 2) % 3
            value = jnp.where(mode == c, sign, 0.0)
            value = jnp.where(mode == 3 + up, e[down], value)
            value = jnp.where(mode == 3 + down, -e[up], value)
            total[c] = value if total[c] is None else total[c] + value
    for m in range(modules):
        for c in range(3):
            start = (m * 3 + c) * points
            weights[start : start + points, :] = total[c][m * points : (m + 1) * points, :]


def plan(owned, links, arms, lags, solve_inverse, rows, cols, lag_rows, reals):
    modules, points = links.shape
    slab, block = modules * 6, lags.shape[1]
    capacity = 2 * modules // rows
    size = -(-capacity * 6 // 8) * 8
    lines, lanes = cols * size, max(reals, lag_rows + 18)
    out = call(
        functools.partial(plan_kernel, rows, cols, capacity, size),
        (jax.ShapeDtypeStruct((lines, lanes), BF16),) * rows
        + (
            jax.ShapeDtypeStruct((rows * size, slab), F32),
            jax.ShapeDtypeStruct((cols, slab, rows * size), F32),
            jax.ShapeDtypeStruct((slab, rows * size), F32),
            jax.ShapeDtypeStruct((modules * 3 * points, slab), F32),
        ),
        [SMEM] + [VMEM] * 4,
        (
            owned,
            links.reshape(-1, 1),
            arms.transpose(0, 2, 1).reshape(-1, 3),
            lags,
            solve_inverse.transpose(1, 0, 2),
        ),
        12 * (modules * points) ** 2 * 4, 4 * modules * 3 * points * rows * modules * 6,
        [
            pltpu.VMEM((modules * points, 4), F32),
            pltpu.VMEM((cols, rows * size, slab), F32),
            pltpu.VMEM((slab, 6), F32),
            pltpu.VMEM((block, lag_rows), BF16),
            pltpu.VMEM((rows, lines, lanes), F32),
        ],
    )
    return out[:rows], *out[rows:]


def after(value, *others):
    return lax.optimization_barrier((value, *others))[0]


def body(
    kernel,
    history,
    displacement,
    velocity,
    acceleration,
    excitation,
    solve_inverse,
    stiffness,
    owned,
    links,
    arms,
):
    rows, cols = lax.axis_size("row"), lax.axis_size("col")
    steps = excitation.shape[0]
    slab, reals = velocity.shape
    modules, points = links.shape
    x, v, a = displacement, velocity, acceleration
    arrived = exchange([v] * rows, "row")
    lags, bases = known_forces(
        kernel.reshape(-1, kernel.shape[3]), history.reshape(-1, reals), rows * slab, steps
    )
    inverse, stiff = diagonals(solve_inverse, stiffness)
    predicted, load = prepare(x, v, a, excitation[0], stiff)
    pieces, bases = force_pieces(lags, arrived, bases, slab, cols)
    riders, send, take, own_take, weights = plan(
        after(owned, pieces[0]), links, arms, lags, solve_inverse, rows, cols, rows * slab, reals
    )
    parts = exchange(pieces, "col")
    x, v, a, messages = first_advance(parts, predicted, v, a, load, inverse, riders)
    arrived = exchange(messages, "row")
    predicted, load = prepare(x, v, a, excitation[1], stiff)
    pieces, _ = force_pieces(lags, arrived, bases, slab, cols)
    parts = exchange(pieces, "col")
    listed, pull = listed_parts(arrived, take, own_take, weights, slab, rows * slab)
    settled, messages = last_advance(
        parts, predicted, v, a, load, excitation[2], inverse, stiff, send, rows
    )
    arrived = exchange(messages, "row")
    pieces = last_force(lags, listed, arrived, slab, cols)
    parts = exchange(pieces, "col")
    known = settled_gaps(arrived, own_take, weights)
    v, out = end(parts, settled, inverse, known, pull, 4 if modules % 4 == 0 else 1)
    return v, out.reshape(modules, 3, points, reals).transpose(0, 2, 1, 3)


def solution(mesh):
    placed = (
        P(None, None, "col", "row"),
        P(None, None, "col", "sea"),
        P(("row", "col"), "sea"),
        P(("row", "col"), "sea"),
        P(("row", "col"), "sea"),
        P(None, ("row", "col"), "sea"),
        P(("row", "col"), None, None),
        P(("row", "col"), None, None),
        P(),
        P(("row", "col"), None),
        P(("row", "col"), None, None),
    )
    return jax.shard_map(
        body,
        mesh=mesh,
        in_specs=placed,
        out_specs=(P(("row", "col"), "sea"), P(("row", "col"), None, None, "sea")),
        check_vma=False,
    )
```

```python
import functools

import jax
import jax.numpy as jnp
from jax import lax
from jax.experimental import pallas as pl
from jax.experimental.pallas import tpu as pltpu
from jax.sharding import PartitionSpec as P


DT = 0.5
QUARTER = DT * DT / 4.0
F32 = jnp.float32
BF16 = jnp.bfloat16
HIGHEST = lax.Precision.HIGHEST
VMEM = pl.BlockSpec(memory_space=pltpu.VMEM)
SMEM = pl.BlockSpec(memory_space=pltpu.SMEM)


def sends_to(i, d, n):
    return i ^ d if n & (n - 1) == 0 else (i + d) % n


def comes_from(i, d, n):
    return i ^ d if n & (n - 1) == 0 else (i + n - d) % n


def exchange(pieces, axis):
    n = lax.axis_size(axis)
    out = [pieces[0]] + [None] * (n - 1)
    for d in range(n - 1, 0, -1):
        out[d] = lax.ppermute(pieces[d], axis, [(i, sends_to(i, d, n)) for i in range(n)])
    return out


def dot_rows(a, b):
    return lax.dot_general(a, b, (((0,), (0,)), ((), ())), preferred_element_type=F32)


def dot_exact(a, b):
    return jnp.dot(a, b, precision=HIGHEST, preferred_element_type=F32)


def padded_bytes(shape, dtype):
    size = jnp.dtype(dtype).itemsize
    dims = (1, 1, *shape)
    up = lambda n, m: -(-n // m) * m
    major = 1
    for n in dims[:-2]:
        major *= n
    return major * up(dims[-2], 32 // size) * up(dims[-1], 128) * size


def call(body, shapes, in_specs, args, flops, nbytes, scratch=()):
    arrays = list(args) + jax.tree.leaves(shapes)
    held = sum(padded_bytes(t.shape, t.dtype) for t in arrays)
    held += sum(padded_bytes(t.shape, t.dtype) for t in scratch if t.shape[1:])
    return pl.pallas_call(
        body,
        out_shape=shapes,
        in_specs=in_specs,
        out_specs=jax.tree.map(lambda _: VMEM, shapes),
        scratch_shapes=scratch,
        compiler_params=pltpu.CompilerParams(
            vmem_limit_bytes=min(2 * held + (2 << 20), 60 << 20)
        ),
        cost_estimate=pl.CostEstimate(flops=flops, bytes_accessed=nbytes, transcendentals=0),
    )(*args)


def known_kernel(lag_rows, steps, per, k_hbm, h_hbm, lags_ref, *refs):
    outs, (k_ref, h_ref, k_sem, h_sem) = refs[:steps], refs[steps:]
    total, known = k_ref.shape[0], h_ref.shape[0]
    size = per * lag_rows
    count = -(-total // size)
    copies = []
    for i in range(count):
        k_rows = pl.ds(i * size, min(size, total - i * size))
        pair = [pltpu.make_async_copy(k_hbm.at[k_rows], k_ref.at[k_rows], k_sem.at[i])]
        if i * size < known:
            h_rows = pl.ds(i * size, min(size, known - i * size))
            pair.append(pltpu.make_async_copy(h_hbm.at[h_rows], h_ref.at[h_rows], h_sem.at[i]))
        copies.append(pair)
    for i in range(min(2, count)):
        for copy in copies[i]:
            copy.start()
    for i in range(count):
        for copy in copies[i]:
            copy.wait()
        if i + 2 < count:
            for copy in copies[i + 2]:
                copy.start()
        last = min((i + 1) * size, total)
        turned = k_ref[i * size : last, :].T if i * size >= steps * lag_rows else None
        for s in range(steps):
            shift = (s + 1) * lag_rows
            first = max(i * size, shift)
            if first >= last:
                outs[s][...] = jnp.zeros_like(outs[s])
                continue
            rows = h_ref[first - shift : last - shift, :]
            if turned is None:
                term = dot_rows(k_ref[first:last, :], rows)
            else:
                term = jnp.dot(turned, rows, preferred_element_type=F32)
            outs[s][...] = term if i == 0 else outs[s][...] + term
    lags_ref[...] = k_ref[: steps * lag_rows, :]


def known_forces(kernel_flat, history_flat, lag_rows, steps):
    block = kernel_flat.shape[1]
    shape = jax.ShapeDtypeStruct((block, history_flat.shape[1]), F32)
    per = 2
    count = -(-kernel_flat.shape[0] // (per * lag_rows))
    out = call(
        functools.partial(known_kernel, lag_rows, steps, per),
        (jax.ShapeDtypeStruct((steps * lag_rows, block), BF16),) + (shape,) * steps,
        [pl.BlockSpec(memory_space=pltpu.MemorySpace.HBM)] * 2,
        tuple(
            pltpu.with_memory_space_constraint(t, pltpu.MemorySpace.HBM)
            for t in (kernel_flat, history_flat)
        ),
        2 * steps * kernel_flat.size * history_flat.shape[1],
        2 * (kernel_flat.size + history_flat.size),
        [
            pltpu.VMEM(kernel_flat.shape, BF16),
            pltpu.VMEM(history_flat.shape, BF16),
            pltpu.SemaphoreType.DMA((count,)),
            pltpu.SemaphoreType.DMA((count,)),
        ],
    )
    return out[0], out[1:]


def force_kernel(cols, ahead, keep, *refs):
    lags = refs[0]
    arrived, refs = refs[1 : 1 + keep], refs[1 + keep :]
    bases, outs = refs[:ahead], refs[ahead:-2]
    chunks, later = outs[:cols], outs[cols:]
    whole, total = refs[-2:]
    rows = keep
    slab, reals = chunks[0].shape[0] // (2 if ahead == 2 else 1), chunks[0].shape[1]
    row, col = lax.axis_index("row"), lax.axis_index("col")
    for d in range(rows):
        start = pl.multiple_of(comes_from(row, d, rows) * slab, 16)
        whole[pl.ds(start, slab), :] = arrived[d][0:slab, 0:reals].astype(BF16)
    lag_rows = rows * slab
    for n in range(ahead):
        value = bases[n][...] + dot_rows(lags[n * lag_rows : (n + 1) * lag_rows, :], whole[...])
        if n == 0 or ahead == 2:
            total[...] = value
            for d in range(cols):
                start = pl.multiple_of(sends_to(col, d, cols) * slab, 8)
                chunks[d][n * slab : (n + 1) * slab, :] = total[pl.ds(start, slab), :]
        else:
            later[n - 1][...] = value


def force_pieces(lags, arrived, bases, slab, cols):
    rows, ahead = len(arrived), len(bases)
    block, reals = bases[0].shape
    both = ahead == 2
    shapes = (jax.ShapeDtypeStruct((slab * (2 if both else 1), reals), F32),) * cols
    if not both:
        shapes += (jax.ShapeDtypeStruct((block, reals), F32),) * (ahead - 1)
    out = call(
        functools.partial(force_kernel, cols, ahead, rows),
        shapes,
        [VMEM] * (1 + rows + ahead),
        (lags, *arrived, *bases),
        2 * ahead * rows * slab * block * reals,
        4 * 2 * ahead * block * reals,
        [pltpu.VMEM((rows * slab, reals), BF16), pltpu.VMEM((block, reals), F32)],
    )
    return out[:cols], out[cols:]


def prepare_kernel(x, v, a, e, stiff, predicted, load):
    p = x[...] + DT * v[...] + QUARTER * a[...]
    predicted[...] = p
    load[...] = e[...] - dot_exact(stiff[...], p)


def prepare(x, v, a, e, stiff):
    shape = jax.ShapeDtypeStruct(x.shape, F32)
    return call(
        prepare_kernel, (shape, shape), [VMEM] * 5, (x, v, a, e, stiff),
        12 * x.size * x.shape[0], 24 * x.size,
    )


def summed(parts, first, count):
    total = parts[0][first : first + count, :]
    for part in parts[1:]:
        total = total + part[first : first + count, :]
    return total


def split(value):
    out = []
    for _ in range(3):
        out.append(value.astype(BF16).astype(F32))
        value = value - out[-1]
    return out


def first_advance_kernel(cols, rows, *refs):
    parts = refs[:cols]
    predicted, v, a, load, inverse = refs[cols : cols + 5]
    riders = refs[cols + 5 : cols + 5 + rows]
    x_out, v_out, a_out, *messages = refs[cols + 5 + rows :]
    slab, reals = v.shape
    a_next = dot_exact(inverse[...], load[...] - summed(parts, 0, slab))
    v_next = v[...] + 0.5 * DT * (a[...] + a_next)
    v_half = v_next.astype(BF16)
    for message, rider in zip(messages, riders):
        message[0:slab, 0:reals] = v_half
        message[slab:, :] = rider[...]
    v_out[...] = v_next
    a_out[...] = a_next
    x_out[...] = predicted[...] + QUARTER * a_next


def first_advance(parts, predicted, v, a, load, inverse, riders):
    shape = jax.ShapeDtypeStruct(v.shape, F32)
    lines, lanes = riders[0].shape
    message = jax.ShapeDtypeStruct((v.shape[0] + lines, lanes), BF16)
    out = call(
        functools.partial(first_advance_kernel, len(parts), len(riders)),
        (shape,) * 3 + (message,) * len(riders),
        [VMEM] * (len(parts) + 5 + len(riders)),
        (*parts, predicted, v, a, load, inverse, *riders),
        12 * v.size * v.shape[0], 40 * v.size,
    )
    return out[0], out[1], out[2], out[3:]


def drift_kernel(predicted, v, a, e, early, moved, both):
    slab = v.shape[0]
    both[0:slab, :] = predicted[...] + DT * v[...] + 0.5 * DT * DT * a[...]
    both[slab:, :] = e[...]
    moved[...] = dot_exact(early[...], both[...])


def drift(predicted, v, a, e, early):
    lines, reals = early.shape[0], v.shape[1]
    return call(
        drift_kernel,
        jax.ShapeDtypeStruct((lines, reals), F32),
        [VMEM] * 5,
        (predicted, v, a, e, early),
        12 * early.size * reals, 24 * v.size,
        [pltpu.VMEM((2 * v.shape[0], reals), F32)],
    )


def last_advance_kernel(cols, rows, *refs):
    parts = refs[:cols]
    v, a, load, inverse, drifted, late = refs[cols : cols + 6]
    v_out, a_out, rest, *messages = refs[cols + 6 : -2]
    held, both = refs[-2:]
    slab, _ = v.shape
    size = late.shape[0] // rows
    turning = load[...] - summed(parts, 0, slab)
    known = summed(parts, slab, slab)
    both[0:slab, :] = turning
    both[slab:, :] = known
    moved = drifted[...] + dot_exact(late[...], both[...])
    a_next = dot_exact(inverse[...], turning)
    v_next = v[...] + 0.5 * DT * (a[...] + a_next)
    v_half = v_next.astype(BF16)
    cuts = split(moved)
    for d in range(rows):
        for k in range(3):
            held[k * size : (k + 1) * size, :] = cuts[k][d * size : (d + 1) * size, :]
        messages[d][0:slab, :] = v_half
        messages[d][slab:, :] = held[...].astype(BF16)
    v_out[...] = v_next
    a_out[...] = a_next
    rest[...] = known


def last_advance(parts, v, a, load, inverse, drifted, late, rows):
    slab, reals = v.shape
    size = late.shape[0] // rows
    shape = jax.ShapeDtypeStruct(v.shape, F32)
    out = call(
        functools.partial(last_advance_kernel, len(parts), rows),
        (shape,) * 3 + (jax.ShapeDtypeStruct((slab + 3 * size, reals), BF16),) * rows,
        [VMEM] * (len(parts) + 6),
        (*parts, v, a, load, inverse, drifted, late),
        48 * v.size * slab, 40 * v.size,
        [pltpu.VMEM((3 * size, reals), F32), pltpu.VMEM((2 * slab, reals), F32)],
    )
    return out[0], out[1], out[2], out[3:]


def settled_kernel(predicted, v, a, e, rest, inverse, stiff, out):
    ahead = predicted[...] + DT * v[...] + 2 * QUARTER * a[...]
    push = dot_exact(inverse[...], e[...] - rest[...] - dot_exact(stiff[...], ahead))
    out[...] = v[...] + 0.5 * DT * (a[...] + push)


def settled_velocity(predicted, v, a, e, rest, inverse, stiff):
    return call(
        settled_kernel,
        jax.ShapeDtypeStruct(v.shape, F32),
        [VMEM] * 7,
        (predicted, v, a, e, rest, inverse, stiff),
        24 * v.size * v.shape[0], 32 * v.size,
    )


def last_force_kernel(cols, rows, *refs):
    lags, listed = refs[0], refs[1]
    arrived = refs[2 : 2 + rows]
    chunks, (whole, total) = refs[2 + rows : -2], refs[-2:]
    slab = chunks[0].shape[0] // 2
    row, col = lax.axis_index("row"), lax.axis_index("col")
    for d in range(rows):
        start = pl.multiple_of(comes_from(row, d, rows) * slab, 16)
        whole[pl.ds(start, slab), :] = arrived[d][0:slab, :]
    newest = whole[...]
    total[0] = dot_rows(lags[0 : rows * slab, :], newest)
    total[1] = jnp.dot(listed[...], newest, preferred_element_type=F32)
    for d in range(cols):
        start = pl.multiple_of(sends_to(col, d, cols) * slab, 8)
        for k in range(2):
            chunks[d][k * slab : (k + 1) * slab, :] = total[k, pl.ds(start, slab), :]


def last_force(lags, listed, arrived, slab, cols):
    rows, block, reals = len(arrived), lags.shape[1], arrived[0].shape[1]
    return call(
        functools.partial(last_force_kernel, cols, rows),
        (jax.ShapeDtypeStruct((2 * slab, reals), F32),) * cols,
        [VMEM] * (2 + rows),
        (lags, listed, *arrived),
        4 * rows * slab * block * reals, 8 * block * reals,
        [pltpu.VMEM((rows * slab, reals), BF16), pltpu.VMEM((2, block, reals), F32)],
    )


def listed_kernel(rows, cols, slab, lag_rows, *refs):
    arrived, (take, own_take, weights) = refs[:rows], refs[rows : rows + 3]
    listed, pull, held, stack, blocks = refs[rows + 3 :]
    size = own_take.shape[1] // rows
    modules = slab // 6
    for d in range(rows):
        held[...] = arrived[d][slab:, :].astype(F32)
        for c in range(cols):
            stack[c, d * size : (d + 1) * size, :] = held[c * size : (c + 1) * size, 0:lag_rows]
        cuts = [held[0:size, lag_rows + 6 * k : lag_rows + 6 * k + 6] for k in range(3)]
        blocks[d * size : (d + 1) * size, :] = (cuts[2] + cuts[1]) + cuts[0]
    for c in range(cols):
        found = jnp.dot(take[c].astype(BF16), stack[c].astype(BF16), preferred_element_type=F32)
        listed[c * slab : (c + 1) * slab, :] = found.astype(BF16)
    block = dot_exact(own_take[...], blocks[...])
    lane = lax.broadcasted_iota(jnp.int32, (slab, slab), 1) // 6
    module = lax.broadcasted_iota(jnp.int32, (slab, slab), 0) // 6
    inverse = jnp.where(lane == module, jnp.concatenate([block] * modules, axis=1), 0.0)
    pull[...] = QUARTER * dot_exact(weights[...], inverse)


def listed_parts(arrived, take, own_take, weights, slab, lag_rows):
    rows, cols = len(arrived), take.shape[0]
    lines, lanes = arrived[0].shape
    return call(
        functools.partial(listed_kernel, rows, cols, slab, lag_rows),
        (
            jax.ShapeDtypeStruct((cols * slab, lag_rows), BF16),
            jax.ShapeDtypeStruct(weights.shape, F32),
        ),
        [VMEM] * (rows + 3),
        (*arrived, take, own_take, weights),
        4 * take.size * lag_rows, 4 * take.size,
        [
            pltpu.VMEM((lines - slab, lanes), F32),
            pltpu.VMEM((cols, own_take.shape[1], lag_rows), F32),
            pltpu.VMEM((own_take.shape[1], 6), F32),
        ],
    )


def settled_gaps_kernel(rows, *refs):
    arrived, (own_take, weights, out, held) = refs[:rows], refs[rows:]
    size = own_take.shape[1] // rows
    slab = own_take.shape[0]
    for d in range(rows):
        cuts = arrived[d][slab:, :].astype(F32)
        held[d * size : (d + 1) * size, :] = (
            cuts[2 * size : 3 * size, :] + cuts[size : 2 * size, :]
        ) + cuts[0:size, :]
    out[...] = dot_exact(weights[...], dot_exact(own_take[...], held[...]))


def settled_gaps(arrived, own_take, weights):
    rows, reals = len(arrived), arrived[0].shape[1]
    return call(
        functools.partial(settled_gaps_kernel, rows),
        jax.ShapeDtypeStruct((weights.shape[0], reals), F32),
        [VMEM] * (rows + 2),
        (*arrived, own_take, weights),
        12 * weights.size * reals, 4 * weights.shape[0] * reals,
        [pltpu.VMEM((own_take.shape[1], reals), F32)],
    )


def end_kernel(cols, pieces, *refs):
    parts = refs[:cols]
    settled, inverse, known, pull, v_out, out, v_done, done, sems = refs[cols:]
    slab = settled.shape[0]
    lines = known.shape[0] // pieces
    force = summed(parts, slab, slab)
    copies = []
    for i in range(pieces):
        at = pl.ds(i * lines, lines)
        done[at, :] = known[at, :] - dot_exact(pull[at, :], force)
        copies.append(pltpu.make_async_copy(done.at[at], out.at[at], sems.at[i]))
        copies[-1].start()
        if i == 0:
            push = dot_exact(inverse[...], summed(parts, 0, slab))
            v_done[...] = settled[...] - 0.5 * DT * push
            copies.append(pltpu.make_async_copy(v_done, v_out, sems.at[pieces]))
            copies[-1].start()
    for copy in copies:
        copy.wait()


def end(parts, settled, inverse, known, pull, pieces):
    hbm = pl.BlockSpec(memory_space=pltpu.MemorySpace.HBM)
    v_shape = jax.ShapeDtypeStruct(settled.shape, F32)
    shape = jax.ShapeDtypeStruct(known.shape, F32)
    return pl.pallas_call(
        functools.partial(end_kernel, len(parts), pieces),
        out_shape=(v_shape, shape),
        in_specs=[VMEM] * (len(parts) + 4),
        out_specs=(hbm, hbm),
        scratch_shapes=[
            pltpu.VMEM(settled.shape, F32),
            pltpu.VMEM(known.shape, F32),
            pltpu.SemaphoreType.DMA((pieces + 1,)),
        ],
        compiler_params=pltpu.CompilerParams(vmem_limit_bytes=16 << 20),
        cost_estimate=pl.CostEstimate(
            flops=12 * pull.size * settled.shape[1], bytes_accessed=8 * known.size, transcendentals=0
        ),
    )(*parts, settled, inverse, known, pull)


def diagonals_kernel(*refs):
    half = len(refs) // 2
    for blocks, out in zip(refs[:half], refs[half:]):
        modules = blocks.shape[1]
        width = 6 * modules
        lane = lax.broadcasted_iota(jnp.int32, (modules, width), 1) // 6
        module = lax.broadcasted_iota(jnp.int32, (modules, width), 0)
        for i in range(6):
            spread = jnp.concatenate([blocks[i]] * modules, axis=1)
            out[pl.ds(i, modules, stride=6), :] = jnp.where(lane == module, spread, 0.0)


def diagonals(*matrices):
    width = 6 * matrices[0].shape[0]
    shape = jax.ShapeDtypeStruct((width, width), F32)
    return call(
        diagonals_kernel, (shape,) * len(matrices), [VMEM] * len(matrices),
        tuple(m.transpose(1, 0, 2) for m in matrices), 100 * width * width, 16 * width * width,
    )


def plan_kernel(rows, cols, capacity, size, *refs):
    owned, lags, blocks = refs[:3]
    riders = refs[3 : 3 + rows]
    send, take, own_take, sends, coef, turned, held = refs[3 + rows :]
    modules = send.shape[1] // 6
    row, col = lax.axis_index("row"), lax.axis_index("col")
    slab, lag_rows = modules * 6, turned.shape[1]
    turned[...] = lags[0:lag_rows, :].T
    shape = (size, slab)
    i = lax.broadcasted_iota(jnp.int32, shape, 0)
    j = lax.broadcasted_iota(jnp.int32, shape, 1)
    wide = (slab, rows * size)
    p = lax.broadcasted_iota(jnp.int32, wide, 0)
    q = lax.broadcasted_iota(jnp.int32, wide, 1)
    for c in range(cols):
        home = (row * cols + c) * modules
        for d in range(rows):
            first = (sends_to(row, d, rows) * cols + c) * modules
            wanted = jnp.full(shape, -1, jnp.int32)
            for k in range(modules):
                local = owned[first + k] - home
                here = (local >= 0) & (local < modules)
                wanted = jnp.where((i // 6 == k % capacity) & here, local, wanted)
            hit = (wanted == j // 6) & (i % 6 == j % 6)
            sends[c, d * size : (d + 1) * size, :] = jnp.where(hit, 1.0, 0.0)
        place = p % 6
        for k in range(modules):
            source = owned[home + k] // (cols * modules)
            d = source ^ row if rows & (rows - 1) == 0 else (row + rows - source) % rows
            place = place + jnp.where(p // 6 == k, d * size + k % capacity * 6, 0)
        take[c] = jnp.where(place == q, 1.0, 0.0)
        picked = jnp.dot(
            sends[c].astype(BF16), turned[c * slab : (c + 1) * slab, :], preferred_element_type=F32
        )
        for d in range(rows):
            held[d, c * size : (c + 1) * size, 0:lag_rows] = picked[d * size : (d + 1) * size, :]
    send[...] = sends[col]
    own_take[...] = take[col]
    for k in range(6):
        coef[pl.ds(k, modules, stride=6), :] = blocks[k]
    cuts = jnp.concatenate(split(dot_exact(send[...], coef[...])), axis=1)
    for d in range(rows):
        held[d, 0:size, lag_rows : lag_rows + 18] = cuts[d * size : (d + 1) * size, :]
        riders[d][...] = held[d].astype(BF16)


def gap_map_kernel(links, arms, inverse, stiff, send, weights, early, late, table):
    modules = weights.shape[1] // 6
    points = links.shape[0] // modules
    row, col = lax.axis_index("row"), lax.axis_index("col")
    cols = lax.axis_size("col")
    slab = modules * 6
    count = modules * points
    table[:, 0:3] = arms[...]
    position = lax.broadcasted_iota(jnp.int32, (count, 1), 0)
    table[:, 3:4] = (position // points * 6).astype(F32)
    own = table[...]
    first_point = (row * cols + col) * count
    point = lax.broadcasted_iota(jnp.int32, (count, count), 1)
    meets = jnp.where(links[...] - first_point == point, 1.0, 0.0)
    partner = dot_exact(meets, own)
    deep = (count, slab)
    column = lax.broadcasted_iota(jnp.int32, deep, 1)
    total = [None] * 3
    for sign, side in ((1.0, own), (-1.0, partner)):
        mode = column - (side[:, 3:4] + 0.5).astype(jnp.int32)
        e = [jnp.broadcast_to(sign * side[:, c : c + 1], deep) for c in range(3)]
        for c in range(3):
            up, down = (c + 1) % 3, (c + 2) % 3
            value = jnp.where(mode == c, sign, 0.0)
            value = jnp.where(mode == 3 + up, e[down], value)
            value = jnp.where(mode == 3 + down, -e[up], value)
            total[c] = value if total[c] is None else total[c] + value
    for m in range(modules):
        for c in range(3):
            start = (m * 3 + c) * points
            weights[start : start + points, :] = total[c][m * points : (m + 1) * points, :]
    press = dot_exact(send[...], QUARTER * inverse[...])
    drift = send[...] - dot_exact(press, stiff[...])
    early[:, 0:slab] = drift
    early[:, slab:] = press
    late[:, 0:slab] = dot_exact((2 * QUARTER + 0.25 * DT) * drift, inverse[...])
    late[:, slab:] = -press


def gap_map(links, arms, inverse, stiff, send):
    modules, points = links.shape
    slab = 6 * modules
    wide = jax.ShapeDtypeStruct((send.shape[0], 2 * slab), F32)
    return call(
        gap_map_kernel,
        (jax.ShapeDtypeStruct((modules * 3 * points, slab), F32), wide, wide),
        [VMEM] * 5,
        (links.reshape(-1, 1), arms.transpose(0, 2, 1).reshape(-1, 3), inverse, stiff, send),
        12 * (modules * points) ** 2 * 4, 16 * modules * 3 * points * slab,
        [pltpu.VMEM((modules * points, 4), F32)],
    )


def plan(owned, lags, solve_inverse, rows, cols, lag_rows, reals):
    modules = solve_inverse.shape[0]
    slab, block = modules * 6, lags.shape[1]
    capacity = 2 * modules // rows
    size = -(-capacity * 6 // 8) * 8
    lines, lanes = cols * size, max(reals, lag_rows + 18)
    out = call(
        functools.partial(plan_kernel, rows, cols, capacity, size),
        (jax.ShapeDtypeStruct((lines, lanes), BF16),) * rows
        + (
            jax.ShapeDtypeStruct((rows * size, slab), F32),
            jax.ShapeDtypeStruct((cols, slab, rows * size), F32),
            jax.ShapeDtypeStruct((slab, rows * size), F32),
        ),
        [SMEM, VMEM, VMEM],
        (owned, lags, solve_inverse.transpose(1, 0, 2)),
        4 * rows * cols * size * slab * lag_rows, 16 * rows * lines * lanes,
        [
            pltpu.VMEM((cols, rows * size, slab), F32),
            pltpu.VMEM((slab, 6), F32),
            pltpu.VMEM((block, lag_rows), BF16),
            pltpu.VMEM((rows, lines, lanes), F32),
        ],
    )
    return out[:rows], *out[rows:]


def after(value, *others):
    return lax.optimization_barrier((value, *others))[0]


def body(
    kernel,
    history,
    displacement,
    velocity,
    acceleration,
    excitation,
    solve_inverse,
    stiffness,
    owned,
    links,
    arms,
):
    rows, cols = lax.axis_size("row"), lax.axis_size("col")
    steps = excitation.shape[0]
    slab, reals = velocity.shape
    modules, points = links.shape
    x, v, a = displacement, velocity, acceleration
    arrived = exchange([v] * rows, "row")
    lags, bases = known_forces(
        kernel.reshape(-1, kernel.shape[3]), history.reshape(-1, reals), rows * slab, steps
    )
    inverse, stiff = diagonals(solve_inverse, stiffness)
    predicted, load = prepare(x, v, a, excitation[0], stiff)
    pieces, bases = force_pieces(lags, arrived, bases, slab, cols)
    riders, send, take, own_take = plan(
        after(owned, pieces[0]), lags, solve_inverse, rows, cols, rows * slab, reals
    )
    parts = exchange(pieces, "col")
    x, v, a, messages = first_advance(parts, predicted, v, a, load, inverse, riders)
    arrived = exchange(messages, "row")
    predicted, load = prepare(x, v, a, excitation[1], stiff)
    weights, early, late = gap_map(after(links, v), arms, inverse, stiff, send)
    drifted = drift(predicted, v, a, excitation[2], early)
    pieces, _ = force_pieces(lags, arrived, bases, slab, cols)
    parts = exchange(pieces, "col")
    listed, pull = listed_parts(arrived, take, own_take, weights, slab, rows * slab)
    v, a, rest, messages = last_advance(parts, v, a, load, inverse, drifted, late, rows)
    arrived = exchange(messages, "row")
    settled = settled_velocity(predicted, v, a, excitation[2], rest, inverse, stiff)
    pieces = last_force(lags, listed, arrived, slab, cols)
    parts = exchange(pieces, "col")
    known = settled_gaps(arrived, own_take, weights)
    v, out = end(parts, settled, inverse, known, pull, 4 if modules % 4 == 0 else 1)
    return v, out.reshape(modules, 3, points, reals).transpose(0, 2, 1, 3)


def solution(mesh):
    placed = (
        P(None, None, "col", "row"),
        P(None, None, "col", "sea"),
        P(("row", "col"), "sea"),
        P(("row", "col"), "sea"),
        P(("row", "col"), "sea"),
        P(None, ("row", "col"), "sea"),
        P(("row", "col"), None, None),
        P(("row", "col"), None, None),
        P(),
        P(("row", "col"), None),
        P(("row", "col"), None, None),
    )
    return jax.shard_map(
        body,
        mesh=mesh,
        in_specs=placed,
        out_specs=(P(("row", "col"), "sea"), P(("row", "col"), None, None, "sea")),
        check_vma=False,
    )
```

```python
import functools

import jax
import jax.numpy as jnp
from jax import lax
from jax.experimental import pallas as pl
from jax.experimental.pallas import tpu as pltpu
from jax.sharding import PartitionSpec as P


DT = 0.5
QUARTER = DT * DT / 4.0
F32 = jnp.float32
BF16 = jnp.bfloat16
HIGHEST = lax.Precision.HIGHEST
VMEM = pl.BlockSpec(memory_space=pltpu.VMEM)
SMEM = pl.BlockSpec(memory_space=pltpu.SMEM)


def sends_to(i, d, n):
    return i ^ d if n & (n - 1) == 0 else (i + d) % n


def comes_from(i, d, n):
    return i ^ d if n & (n - 1) == 0 else (i + n - d) % n


def exchange(pieces, axis):
    n = lax.axis_size(axis)
    out = [pieces[0]] + [None] * (n - 1)
    for d in range(n - 1, 0, -1):
        out[d] = lax.ppermute(pieces[d], axis, [(i, sends_to(i, d, n)) for i in range(n)])
    return out


def dot_rows(a, b):
    return lax.dot_general(a, b, (((0,), (0,)), ((), ())), preferred_element_type=F32)


def dot_exact(a, b):
    return jnp.dot(a, b, precision=HIGHEST, preferred_element_type=F32)


def padded_bytes(shape, dtype):
    size = jnp.dtype(dtype).itemsize
    dims = (1, 1, *shape)
    up = lambda n, m: -(-n // m) * m
    major = 1
    for n in dims[:-2]:
        major *= n
    return major * up(dims[-2], 32 // size) * up(dims[-1], 128) * size


def call(body, shapes, in_specs, args, flops, nbytes, scratch=()):
    arrays = list(args) + jax.tree.leaves(shapes)
    held = sum(padded_bytes(t.shape, t.dtype) for t in arrays)
    held += sum(padded_bytes(t.shape, t.dtype) for t in scratch if t.shape[1:])
    return pl.pallas_call(
        body,
        out_shape=shapes,
        in_specs=in_specs,
        out_specs=jax.tree.map(lambda _: VMEM, shapes),
        scratch_shapes=scratch,
        compiler_params=pltpu.CompilerParams(
            vmem_limit_bytes=min(2 * held + (2 << 20), 60 << 20)
        ),
        cost_estimate=pl.CostEstimate(flops=flops, bytes_accessed=nbytes, transcendentals=0),
    )(*args)


def known_kernel(lag_rows, pieces, k_hbm, h_hbm, k_ref, h_ref, out, k_sem, h_sem):
    copies = []
    for far, near, sems in ((k_hbm, k_ref, k_sem), (h_hbm, h_ref, h_sem)):
        size = far.shape[0] // pieces
        for i in range(pieces):
            at = pl.ds(i * size, size)
            copies.append(pltpu.make_async_copy(far.at[at], near.at[at], sems.at[i]))
            copies[-1].start()
    for copy in copies:
        copy.wait()
    total = k_ref.shape[0]
    out[...] = dot_rows(k_ref[lag_rows:, :], h_ref[: total - lag_rows, :])


def known_force(kernel_flat, history_flat, lag_rows):
    shapes = (
        jax.ShapeDtypeStruct(kernel_flat.shape, BF16),
        jax.ShapeDtypeStruct(history_flat.shape, BF16),
        jax.ShapeDtypeStruct((kernel_flat.shape[1], history_flat.shape[1]), F32),
    )
    pieces = 2 if kernel_flat.shape[0] % 32 == 0 and history_flat.shape[0] % 32 == 0 else 1
    return call(
        functools.partial(known_kernel, lag_rows, pieces),
        shapes,
        [pl.BlockSpec(memory_space=pltpu.MemorySpace.HBM)] * 2,
        tuple(
            pltpu.with_memory_space_constraint(t, pltpu.MemorySpace.HBM)
            for t in (kernel_flat, history_flat)
        ),
        2 * kernel_flat.size * history_flat.shape[1],
        2 * (kernel_flat.size + history_flat.size),
        [pltpu.SemaphoreType.DMA((pieces,)), pltpu.SemaphoreType.DMA((pieces,))],
    )


def later_kernel(k_ref, h_ref, newest, *outs):
    total, lag_rows = k_ref.shape[0], newest.shape[0]
    for n, out in enumerate(outs):
        first = (n + 1) * lag_rows
        out[...] = dot_rows(k_ref[first : first + lag_rows, :], newest[...]) + dot_rows(
            k_ref[first + lag_rows :, :], h_ref[: total - first - lag_rows, :]
        )


def later_forces(k, h, newest, count):
    shape = jax.ShapeDtypeStruct((k.shape[1], h.shape[1]), F32)
    return call(
        later_kernel, (shape,) * count, [VMEM] * 3, (k, h, newest),
        2 * count * k.size * h.shape[1], 2 * (k.size + h.size),
    )


def gather_newest(arrived, whole, slab, reals):
    row, rows = lax.axis_index("row"), len(arrived)
    for d in range(rows):
        start = pl.multiple_of(comes_from(row, d, rows) * slab, 16)
        whole[pl.ds(start, slab), :] = arrived[d][0:slab, 0:reals].astype(BF16)


def first_force_kernel(cols, rows, *refs):
    k_ref, arrived, base = refs[0], refs[1 : 1 + rows], refs[1 + rows]
    chunks, (whole, total) = refs[2 + rows : -2], refs[-2:]
    slab, reals = chunks[0].shape
    gather_newest(arrived, whole, slab, reals)
    total[...] = base[...] + dot_rows(k_ref[0 : rows * slab, :], whole[...])
    col = lax.axis_index("col")
    for d in range(cols):
        start = pl.multiple_of(sends_to(col, d, cols) * slab, 8)
        chunks[d][...] = total[pl.ds(start, slab), :]


def first_force(k, arrived, base, slab, cols):
    rows, (block, reals) = len(arrived), base.shape
    out = call(
        functools.partial(first_force_kernel, cols, rows),
        (jax.ShapeDtypeStruct((slab, reals), F32),) * cols
        + (jax.ShapeDtypeStruct((rows * slab, reals), BF16),),
        [VMEM] * (2 + rows),
        (k, *arrived, base),
        2 * rows * slab * block * reals, 8 * block * reals,
        [pltpu.VMEM((block, reals), F32)],
    )
    return out[:cols], out[cols]


def force_kernel(cols, rows, *refs):
    lags, arrived, bases = refs[0], refs[1 : 1 + rows], refs[1 + rows : 3 + rows]
    chunks, (whole, total) = refs[3 + rows : -2], refs[-2:]
    slab, reals = chunks[0].shape[0] // 2, chunks[0].shape[1]
    gather_newest(arrived, whole, slab, reals)
    lag_rows = rows * slab
    col = lax.axis_index("col")
    for n in range(2):
        total[n] = bases[n][...] + dot_rows(
            lags[n * lag_rows : (n + 1) * lag_rows, :], whole[...]
        )
        for d in range(cols):
            start = pl.multiple_of(sends_to(col, d, cols) * slab, 8)
            chunks[d][n * slab : (n + 1) * slab, :] = total[n, pl.ds(start, slab), :]


def force_pieces(lags, arrived, bases, slab, cols):
    rows, (block, reals) = len(arrived), bases[0].shape
    return call(
        functools.partial(force_kernel, cols, rows),
        (jax.ShapeDtypeStruct((2 * slab, reals), F32),) * cols,
        [VMEM] * (3 + rows),
        (lags, *arrived, *bases),
        4 * rows * slab * block * reals, 16 * block * reals,
        [pltpu.VMEM((rows * slab, reals), BF16), pltpu.VMEM((2, block, reals), F32)],
    )


def prepare_kernel(x, v, a, e, stiff, predicted, load):
    p = x[...] + DT * v[...] + QUARTER * a[...]
    predicted[...] = p
    load[...] = e[...] - dot_exact(stiff[...], p)


def prepare(x, v, a, e, stiff):
    shape = jax.ShapeDtypeStruct(x.shape, F32)
    return call(
        prepare_kernel, (shape, shape), [VMEM] * 5, (x, v, a, e, stiff),
        12 * x.size * x.shape[0], 24 * x.size,
    )


def summed(parts, first, count):
    total = parts[0][first : first + count, :]
    for part in parts[1:]:
        total = total + part[first : first + count, :]
    return total


def split(value):
    out = []
    for _ in range(3):
        out.append(value.astype(BF16).astype(F32))
        value = value - out[-1]
    return out


def first_advance_kernel(cols, rows, *refs):
    parts = refs[:cols]
    predicted, v, a, load, inverse = refs[cols : cols + 5]
    riders = refs[cols + 5 : cols + 5 + rows]
    x_out, v_out, a_out, *messages = refs[cols + 5 + rows :]
    slab, reals = v.shape
    a_next = dot_exact(inverse[...], load[...] - summed(parts, 0, slab))
    v_next = v[...] + 0.5 * DT * (a[...] + a_next)
    v_half = v_next.astype(BF16)
    for message, rider in zip(messages, riders):
        message[0:slab, 0:reals] = v_half
        message[slab:, :] = rider[...]
    v_out[...] = v_next
    a_out[...] = a_next
    x_out[...] = predicted[...] + QUARTER * a_next


def first_advance(parts, predicted, v, a, load, inverse, riders):
    shape = jax.ShapeDtypeStruct(v.shape, F32)
    lines, lanes = riders[0].shape
    message = jax.ShapeDtypeStruct((v.shape[0] + lines, lanes), BF16)
    out = call(
        functools.partial(first_advance_kernel, len(parts), len(riders)),
        (shape,) * 3 + (message,) * len(riders),
        [VMEM] * (len(parts) + 5 + len(riders)),
        (*parts, predicted, v, a, load, inverse, *riders),
        12 * v.size * v.shape[0], 40 * v.size,
    )
    return out[0], out[1], out[2], out[3:]


def drift_kernel(predicted, v, a, e, early, moved, both):
    slab = v.shape[0]
    both[0:slab, :] = predicted[...] + DT * v[...] + 0.5 * DT * DT * a[...]
    both[slab:, :] = e[...]
    moved[...] = dot_exact(early[...], both[...])


def drift(predicted, v, a, e, early):
    lines, reals = early.shape[0], v.shape[1]
    return call(
        drift_kernel,
        jax.ShapeDtypeStruct((lines, reals), F32),
        [VMEM] * 5,
        (predicted, v, a, e, early),
        12 * early.size * reals, 24 * v.size,
        [pltpu.VMEM((2 * v.shape[0], reals), F32)],
    )


def last_advance_kernel(cols, rows, *refs):
    parts = refs[:cols]
    v, a, load, inverse, drifted, late = refs[cols : cols + 6]
    v_out, a_out, rest, *messages = refs[cols + 6 : -2]
    held, both = refs[-2:]
    slab, _ = v.shape
    size = late.shape[0] // rows
    turning = load[...] - summed(parts, 0, slab)
    known = summed(parts, slab, slab)
    both[0:slab, :] = turning
    both[slab:, :] = known
    moved = drifted[...] + dot_exact(late[...], both[...])
    a_next = dot_exact(inverse[...], turning)
    v_next = v[...] + 0.5 * DT * (a[...] + a_next)
    v_half = v_next.astype(BF16)
    cuts = split(moved)
    for d in range(rows):
        for k in range(3):
            held[k * size : (k + 1) * size, :] = cuts[k][d * size : (d + 1) * size, :]
        messages[d][0:slab, :] = v_half
        messages[d][slab:, :] = held[...].astype(BF16)
    v_out[...] = v_next
    a_out[...] = a_next
    rest[...] = known


def last_advance(parts, v, a, load, inverse, drifted, late, rows):
    slab, reals = v.shape
    size = late.shape[0] // rows
    shape = jax.ShapeDtypeStruct(v.shape, F32)
    out = call(
        functools.partial(last_advance_kernel, len(parts), rows),
        (shape,) * 3 + (jax.ShapeDtypeStruct((slab + 3 * size, reals), BF16),) * rows,
        [VMEM] * (len(parts) + 6),
        (*parts, v, a, load, inverse, drifted, late),
        48 * v.size * slab, 40 * v.size,
        [pltpu.VMEM((3 * size, reals), F32), pltpu.VMEM((2 * slab, reals), F32)],
    )
    return out[0], out[1], out[2], out[3:]


def settled_kernel(predicted, v, a, e, rest, inverse, stiff, out):
    ahead = predicted[...] + DT * v[...] + 2 * QUARTER * a[...]
    push = dot_exact(inverse[...], e[...] - rest[...] - dot_exact(stiff[...], ahead))
    out[...] = v[...] + 0.5 * DT * (a[...] + push)


def settled_velocity(predicted, v, a, e, rest, inverse, stiff):
    return call(
        settled_kernel,
        jax.ShapeDtypeStruct(v.shape, F32),
        [VMEM] * 7,
        (predicted, v, a, e, rest, inverse, stiff),
        24 * v.size * v.shape[0], 32 * v.size,
    )


def last_force_kernel(cols, rows, *refs):
    lags, listed = refs[0], refs[1]
    arrived = refs[2 : 2 + rows]
    chunks, (whole, total) = refs[2 + rows : -2], refs[-2:]
    slab = chunks[0].shape[0] // 2
    row, col = lax.axis_index("row"), lax.axis_index("col")
    for d in range(rows):
        start = pl.multiple_of(comes_from(row, d, rows) * slab, 16)
        whole[pl.ds(start, slab), :] = arrived[d][0:slab, :]
    newest = whole[...]
    total[0] = dot_rows(lags[0 : rows * slab, :], newest)
    total[1] = jnp.dot(listed[...], newest, preferred_element_type=F32)
    for d in range(cols):
        start = pl.multiple_of(sends_to(col, d, cols) * slab, 8)
        for k in range(2):
            chunks[d][k * slab : (k + 1) * slab, :] = total[k, pl.ds(start, slab), :]


def last_force(lags, listed, arrived, slab, cols):
    rows, block, reals = len(arrived), lags.shape[1], arrived[0].shape[1]
    return call(
        functools.partial(last_force_kernel, cols, rows),
        (jax.ShapeDtypeStruct((2 * slab, reals), F32),) * cols,
        [VMEM] * (2 + rows),
        (lags, listed, *arrived),
        4 * rows * slab * block * reals, 8 * block * reals,
        [pltpu.VMEM((rows * slab, reals), BF16), pltpu.VMEM((2, block, reals), F32)],
    )


def listed_kernel(rows, cols, slab, lag_rows, *refs):
    arrived, (take, own_take, weights) = refs[:rows], refs[rows : rows + 3]
    listed, pull, held, stack, blocks = refs[rows + 3 :]
    size = own_take.shape[1] // rows
    modules = slab // 6
    for d in range(rows):
        held[...] = arrived[d][slab:, :].astype(F32)
        for c in range(cols):
            stack[c, d * size : (d + 1) * size, :] = held[c * size : (c + 1) * size, 0:lag_rows]
        cuts = [held[0:size, lag_rows + 6 * k : lag_rows + 6 * k + 6] for k in range(3)]
        blocks[d * size : (d + 1) * size, :] = (cuts[2] + cuts[1]) + cuts[0]
    for c in range(cols):
        found = jnp.dot(take[c].astype(BF16), stack[c].astype(BF16), preferred_element_type=F32)
        listed[c * slab : (c + 1) * slab, :] = found.astype(BF16)
    block = dot_exact(own_take[...], blocks[...])
    lane = lax.broadcasted_iota(jnp.int32, (slab, slab), 1) // 6
    module = lax.broadcasted_iota(jnp.int32, (slab, slab), 0) // 6
    inverse = jnp.where(lane == module, jnp.concatenate([block] * modules, axis=1), 0.0)
    pull[...] = QUARTER * dot_exact(weights[...], inverse)


def listed_parts(arrived, take, own_take, weights, slab, lag_rows):
    rows, cols = len(arrived), take.shape[0]
    lines, lanes = arrived[0].shape
    return call(
        functools.partial(listed_kernel, rows, cols, slab, lag_rows),
        (
            jax.ShapeDtypeStruct((cols * slab, lag_rows), BF16),
            jax.ShapeDtypeStruct(weights.shape, F32),
        ),
        [VMEM] * (rows + 3),
        (*arrived, take, own_take, weights),
        4 * take.size * lag_rows, 4 * take.size,
        [
            pltpu.VMEM((lines - slab, lanes), F32),
            pltpu.VMEM((cols, own_take.shape[1], lag_rows), F32),
            pltpu.VMEM((own_take.shape[1], 6), F32),
        ],
    )


def settled_gaps_kernel(rows, *refs):
    arrived, (own_take, weights, out, held) = refs[:rows], refs[rows:]
    size = own_take.shape[1] // rows
    slab = own_take.shape[0]
    for d in range(rows):
        cuts = arrived[d][slab:, :].astype(F32)
        held[d * size : (d + 1) * size, :] = (
            cuts[2 * size : 3 * size, :] + cuts[size : 2 * size, :]
        ) + cuts[0:size, :]
    out[...] = dot_exact(weights[...], dot_exact(own_take[...], held[...]))


def settled_gaps(arrived, own_take, weights):
    rows, reals = len(arrived), arrived[0].shape[1]
    return call(
        functools.partial(settled_gaps_kernel, rows),
        jax.ShapeDtypeStruct((weights.shape[0], reals), F32),
        [VMEM] * (rows + 2),
        (*arrived, own_take, weights),
        12 * weights.size * reals, 4 * weights.shape[0] * reals,
        [pltpu.VMEM((own_take.shape[1], reals), F32)],
    )


def end_kernel(cols, pieces, *refs):
    parts = refs[:cols]
    settled, inverse, known, pull, v_out, out, v_done, done, sems = refs[cols:]
    slab = settled.shape[0]
    lines = known.shape[0] // pieces
    force = summed(parts, slab, slab)
    copies = []
    for i in range(pieces):
        at = pl.ds(i * lines, lines)
        done[at, :] = known[at, :] - dot_exact(pull[at, :], force)
        copies.append(pltpu.make_async_copy(done.at[at], out.at[at], sems.at[i]))
        copies[-1].start()
        if i == 0:
            push = dot_exact(inverse[...], summed(parts, 0, slab))
            v_done[...] = settled[...] - 0.5 * DT * push
            copies.append(pltpu.make_async_copy(v_done, v_out, sems.at[pieces]))
            copies[-1].start()
    for copy in copies:
        copy.wait()


def end(parts, settled, inverse, known, pull, pieces):
    hbm = pl.BlockSpec(memory_space=pltpu.MemorySpace.HBM)
    v_shape = jax.ShapeDtypeStruct(settled.shape, F32)
    shape = jax.ShapeDtypeStruct(known.shape, F32)
    return pl.pallas_call(
        functools.partial(end_kernel, len(parts), pieces),
        out_shape=(v_shape, shape),
        in_specs=[VMEM] * (len(parts) + 4),
        out_specs=(hbm, hbm),
        scratch_shapes=[
            pltpu.VMEM(settled.shape, F32),
            pltpu.VMEM(known.shape, F32),
            pltpu.SemaphoreType.DMA((pieces + 1,)),
        ],
        compiler_params=pltpu.CompilerParams(vmem_limit_bytes=16 << 20),
        cost_estimate=pl.CostEstimate(
            flops=12 * pull.size * settled.shape[1], bytes_accessed=8 * known.size, transcendentals=0
        ),
    )(*parts, settled, inverse, known, pull)


def diagonals_kernel(*refs):
    half = len(refs) // 2
    for blocks, out in zip(refs[:half], refs[half:]):
        modules = blocks.shape[1]
        width = 6 * modules
        lane = lax.broadcasted_iota(jnp.int32, (modules, width), 1) // 6
        module = lax.broadcasted_iota(jnp.int32, (modules, width), 0)
        for i in range(6):
            spread = jnp.concatenate([blocks[i]] * modules, axis=1)
            out[pl.ds(i, modules, stride=6), :] = jnp.where(lane == module, spread, 0.0)


def diagonals(*matrices):
    width = 6 * matrices[0].shape[0]
    shape = jax.ShapeDtypeStruct((width, width), F32)
    return call(
        diagonals_kernel, (shape,) * len(matrices), [VMEM] * len(matrices),
        tuple(m.transpose(1, 0, 2) for m in matrices), 100 * width * width, 16 * width * width,
    )


def plan_kernel(rows, cols, capacity, size, *refs):
    owned, lags, blocks = refs[:3]
    riders = refs[3 : 3 + rows]
    send, take, own_take, sends, coef, turned, held = refs[3 + rows :]
    modules = send.shape[1] // 6
    row, col = lax.axis_index("row"), lax.axis_index("col")
    slab, lag_rows = modules * 6, turned.shape[1]
    turned[...] = lags[0:lag_rows, :].T
    shape = (size, slab)
    i = lax.broadcasted_iota(jnp.int32, shape, 0)
    j = lax.broadcasted_iota(jnp.int32, shape, 1)
    wide = (slab, rows * size)
    p = lax.broadcasted_iota(jnp.int32, wide, 0)
    q = lax.broadcasted_iota(jnp.int32, wide, 1)
    for c in range(cols):
        home = (row * cols + c) * modules
        for d in range(rows):
            first = (sends_to(row, d, rows) * cols + c) * modules
            wanted = jnp.full(shape, -1, jnp.int32)
            for k in range(modules):
                local = owned[first + k] - home
                here = (local >= 0) & (local < modules)
                wanted = jnp.where((i // 6 == k % capacity) & here, local, wanted)
            hit = (wanted == j // 6) & (i % 6 == j % 6)
            sends[c, d * size : (d + 1) * size, :] = jnp.where(hit, 1.0, 0.0)
        place = p % 6
        for k in range(modules):
            source = owned[home + k] // (cols * modules)
            d = source ^ row if rows & (rows - 1) == 0 else (row + rows - source) % rows
            place = place + jnp.where(p // 6 == k, d * size + k % capacity * 6, 0)
        take[c] = jnp.where(place == q, 1.0, 0.0)
        picked = jnp.dot(
            sends[c].astype(BF16), turned[c * slab : (c + 1) * slab, :], preferred_element_type=F32
        )
        for d in range(rows):
            held[d, c * size : (c + 1) * size, 0:lag_rows] = picked[d * size : (d + 1) * size, :]
    send[...] = sends[col]
    own_take[...] = take[col]
    for k in range(6):
        coef[pl.ds(k, modules, stride=6), :] = blocks[k]
    cuts = jnp.concatenate(split(dot_exact(send[...], coef[...])), axis=1)
    for d in range(rows):
        held[d, 0:size, lag_rows : lag_rows + 18] = cuts[d * size : (d + 1) * size, :]
        riders[d][...] = held[d].astype(BF16)


def gap_map_kernel(links, arms, inverse, stiff, send, weights, early, late, table):
    modules = weights.shape[1] // 6
    points = links.shape[0] // modules
    row, col = lax.axis_index("row"), lax.axis_index("col")
    cols = lax.axis_size("col")
    slab = modules * 6
    count = modules * points
    table[:, 0:3] = arms[...]
    position = lax.broadcasted_iota(jnp.int32, (count, 1), 0)
    table[:, 3:4] = (position // points * 6).astype(F32)
    own = table[...]
    first_point = (row * cols + col) * count
    point = lax.broadcasted_iota(jnp.int32, (count, count), 1)
    meets = jnp.where(links[...] - first_point == point, 1.0, 0.0)
    partner = dot_exact(meets, own)
    deep = (count, slab)
    column = lax.broadcasted_iota(jnp.int32, deep, 1)
    total = [None] * 3
    for sign, side in ((1.0, own), (-1.0, partner)):
        mode = column - (side[:, 3:4] + 0.5).astype(jnp.int32)
        e = [jnp.broadcast_to(sign * side[:, c : c + 1], deep) for c in range(3)]
        for c in range(3):
            up, down = (c + 1) % 3, (c + 2) % 3
            value = jnp.where(mode == c, sign, 0.0)
            value = jnp.where(mode == 3 + up, e[down], value)
            value = jnp.where(mode == 3 + down, -e[up], value)
            total[c] = value if total[c] is None else total[c] + value
    for m in range(modules):
        for c in range(3):
            start = (m * 3 + c) * points
            weights[start : start + points, :] = total[c][m * points : (m + 1) * points, :]
    press = dot_exact(send[...], QUARTER * inverse[...])
    drift = send[...] - dot_exact(press, stiff[...])
    early[:, 0:slab] = drift
    early[:, slab:] = press
    late[:, 0:slab] = dot_exact((2 * QUARTER + 0.25 * DT) * drift, inverse[...])
    late[:, slab:] = -press


def gap_map(links, arms, inverse, stiff, send):
    modules, points = links.shape
    slab = 6 * modules
    wide = jax.ShapeDtypeStruct((send.shape[0], 2 * slab), F32)
    return call(
        gap_map_kernel,
        (jax.ShapeDtypeStruct((modules * 3 * points, slab), F32), wide, wide),
        [VMEM] * 5,
        (links.reshape(-1, 1), arms.transpose(0, 2, 1).reshape(-1, 3), inverse, stiff, send),
        12 * (modules * points) ** 2 * 4, 16 * modules * 3 * points * slab,
        [pltpu.VMEM((modules * points, 4), F32)],
    )


def plan(owned, lags, solve_inverse, rows, cols, lag_rows, reals):
    modules = solve_inverse.shape[0]
    slab, block = modules * 6, lags.shape[1]
    capacity = 2 * modules // rows
    size = -(-capacity * 6 // 8) * 8
    lines, lanes = cols * size, max(reals, lag_rows + 18)
    out = call(
        functools.partial(plan_kernel, rows, cols, capacity, size),
        (jax.ShapeDtypeStruct((lines, lanes), BF16),) * rows
        + (
            jax.ShapeDtypeStruct((rows * size, slab), F32),
            jax.ShapeDtypeStruct((cols, slab, rows * size), F32),
            jax.ShapeDtypeStruct((slab, rows * size), F32),
        ),
        [SMEM, VMEM, VMEM],
        (owned, lags, solve_inverse.transpose(1, 0, 2)),
        4 * rows * cols * size * slab * lag_rows, 16 * rows * lines * lanes,
        [
            pltpu.VMEM((cols, rows * size, slab), F32),
            pltpu.VMEM((slab, 6), F32),
            pltpu.VMEM((block, lag_rows), BF16),
            pltpu.VMEM((rows, lines, lanes), F32),
        ],
    )
    return out[:rows], *out[rows:]


def after(value, *others):
    return lax.optimization_barrier((value, *others))[0]


def body(
    kernel,
    history,
    displacement,
    velocity,
    acceleration,
    excitation,
    solve_inverse,
    stiffness,
    owned,
    links,
    arms,
):
    rows, cols = lax.axis_size("row"), lax.axis_size("col")
    steps = excitation.shape[0]
    slab, reals = velocity.shape
    modules, points = links.shape
    x, v, a = displacement, velocity, acceleration
    arrived = exchange([v] * rows, "row")
    lags, past, base = known_force(
        kernel.reshape(-1, kernel.shape[3]), history.reshape(-1, reals), rows * slab
    )
    inverse, stiff = diagonals(solve_inverse, stiffness)
    predicted, load = prepare(x, v, a, excitation[0], stiff)
    pieces, newest = first_force(lags, arrived, base, slab, cols)
    riders, send, take, own_take = plan(
        after(owned, pieces[0]), lags, solve_inverse, rows, cols, rows * slab, reals
    )
    parts = exchange(pieces, "col")
    x, v, a, messages = first_advance(parts, predicted, v, a, load, inverse, riders)
    arrived = exchange(messages, "row")
    predicted, load = prepare(x, v, a, excitation[1], stiff)
    weights, early, late = gap_map(after(links, v), arms, inverse, stiff, send)
    drifted = drift(predicted, v, a, excitation[2], early)
    bases = later_forces(lags, past, after(newest, v), steps - 1)
    pieces = force_pieces(lags, arrived, bases, slab, cols)
    parts = exchange(pieces, "col")
    listed, pull = listed_parts(arrived, take, own_take, weights, slab, rows * slab)
    v, a, rest, messages = last_advance(parts, v, a, load, inverse, drifted, late, rows)
    arrived = exchange(messages, "row")
    settled = settled_velocity(predicted, v, a, excitation[2], rest, inverse, stiff)
    pieces = last_force(lags, listed, arrived, slab, cols)
    parts = exchange(pieces, "col")
    known = settled_gaps(arrived, own_take, weights)
    v, out = end(parts, settled, inverse, known, pull, 4 if modules % 4 == 0 else 1)
    return v, out.reshape(modules, 3, points, reals).transpose(0, 2, 1, 3)


def solution(mesh):
    placed = (
        P(None, None, "col", "row"),
        P(None, None, "col", "sea"),
        P(("row", "col"), "sea"),
        P(("row", "col"), "sea"),
        P(("row", "col"), "sea"),
        P(None, ("row", "col"), "sea"),
        P(("row", "col"), None, None),
        P(("row", "col"), None, None),
        P(),
        P(("row", "col"), None),
        P(("row", "col"), None, None),
    )
    return jax.shard_map(
        body,
        mesh=mesh,
        in_specs=placed,
        out_specs=(P(("row", "col"), "sea"), P(("row", "col"), None, None, "sea")),
        check_vma=False,
    )
```

```python
import functools

import jax
import jax.numpy as jnp
from jax import lax
from jax.experimental import pallas as pl
from jax.experimental.pallas import tpu as pltpu
from jax.sharding import PartitionSpec as P


DT = 0.5
QUARTER = DT * DT / 4.0
F32 = jnp.float32
BF16 = jnp.bfloat16
HIGHEST = lax.Precision.HIGHEST
PAIRS = ((0, 0), (0, 1), (0, 2), (1, 0), (1, 1), (2, 0))
VMEM = pl.BlockSpec(memory_space=pltpu.VMEM)
SMEM = pl.BlockSpec(memory_space=pltpu.SMEM)


def sends_to(i, d, n):
    return i ^ d if n & (n - 1) == 0 else (i + d) % n


def comes_from(i, d, n):
    return i ^ d if n & (n - 1) == 0 else (i + n - d) % n


def exchange(pieces, axis):
    n = lax.axis_size(axis)
    out = [pieces[0]] + [None] * (n - 1)
    for d in range(n - 1, 0, -1):
        out[d] = lax.ppermute(pieces[d], axis, [(i, sends_to(i, d, n)) for i in range(n)])
    return out


def dot_rows(a, b):
    return lax.dot_general(a, b, (((0,), (0,)), ((), ())), preferred_element_type=F32)


def dot_exact(a, b):
    return jnp.dot(a, b, precision=HIGHEST, preferred_element_type=F32)


def padded_bytes(shape, dtype):
    size = jnp.dtype(dtype).itemsize
    dims = (1, 1, *shape)
    up = lambda n, m: -(-n // m) * m
    major = 1
    for n in dims[:-2]:
        major *= n
    return major * up(dims[-2], 32 // size) * up(dims[-1], 128) * size


def call(body, shapes, in_specs, args, flops, nbytes, scratch=()):
    arrays = list(args) + jax.tree.leaves(shapes)
    held = sum(padded_bytes(t.shape, t.dtype) for t in arrays)
    held += sum(padded_bytes(t.shape, t.dtype) for t in scratch if t.shape[1:])
    return pl.pallas_call(
        body,
        out_shape=shapes,
        in_specs=in_specs,
        out_specs=jax.tree.map(lambda _: VMEM, shapes),
        scratch_shapes=scratch,
        compiler_params=pltpu.CompilerParams(
            vmem_limit_bytes=min(2 * held + (2 << 20), 60 << 20)
        ),
        cost_estimate=pl.CostEstimate(flops=flops, bytes_accessed=nbytes, transcendentals=0),
    )(*args)


def known_kernel(lag_rows, pieces, k_hbm, h_hbm, k_ref, h_ref, out, k_sem, h_sem):
    copies = []
    for far, near, sems in ((k_hbm, k_ref, k_sem), (h_hbm, h_ref, h_sem)):
        size = far.shape[0] // pieces
        for i in range(pieces):
            at = pl.ds(i * size, size)
            copies.append(pltpu.make_async_copy(far.at[at], near.at[at], sems.at[i]))
            copies[-1].start()
    for copy in copies:
        copy.wait()
    total = k_ref.shape[0]
    out[...] = dot_rows(k_ref[lag_rows:, :], h_ref[: total - lag_rows, :])


def known_force(kernel_flat, history_flat, lag_rows):
    shapes = (
        jax.ShapeDtypeStruct(kernel_flat.shape, BF16),
        jax.ShapeDtypeStruct(history_flat.shape, BF16),
        jax.ShapeDtypeStruct((kernel_flat.shape[1], history_flat.shape[1]), F32),
    )
    pieces = 2 if kernel_flat.shape[0] % 32 == 0 and history_flat.shape[0] % 32 == 0 else 1
    return call(
        functools.partial(known_kernel, lag_rows, pieces),
        shapes,
        [pl.BlockSpec(memory_space=pltpu.MemorySpace.HBM)] * 2,
        tuple(
            pltpu.with_memory_space_constraint(t, pltpu.MemorySpace.HBM)
            for t in (kernel_flat, history_flat)
        ),
        2 * kernel_flat.size * history_flat.shape[1],
        2 * (kernel_flat.size + history_flat.size),
        [pltpu.SemaphoreType.DMA((pieces,)), pltpu.SemaphoreType.DMA((pieces,))],
    )


def later_kernel(k_ref, h_ref, newest, *outs):
    total, lag_rows = k_ref.shape[0], newest.shape[0]
    for n, out in enumerate(outs):
        first = (n + 1) * lag_rows
        out[...] = dot_rows(k_ref[first : first + lag_rows, :], newest[...]) + dot_rows(
            k_ref[first + lag_rows :, :], h_ref[: total - first - lag_rows, :]
        )


def later_forces(k, h, newest, count):
    shape = jax.ShapeDtypeStruct((k.shape[1], h.shape[1]), F32)
    return call(
        later_kernel, (shape,) * count, [VMEM] * 3, (k, h, newest),
        2 * count * k.size * h.shape[1], 2 * (k.size + h.size),
    )


def gather_newest(arrived, whole, slab, reals):
    row, rows = lax.axis_index("row"), len(arrived)
    for d in range(rows):
        start = pl.multiple_of(comes_from(row, d, rows) * slab, 16)
        whole[pl.ds(start, slab), :] = arrived[d][0:slab, 0:reals].astype(BF16)


def first_force_kernel(cols, rows, *refs):
    k_ref, arrived, base = refs[0], refs[1 : 1 + rows], refs[1 + rows]
    chunks, (whole, total) = refs[2 + rows : -2], refs[-2:]
    slab, reals = chunks[0].shape
    gather_newest(arrived, whole, slab, reals)
    total[...] = base[...] + dot_rows(k_ref[0 : rows * slab, :], whole[...])
    col = lax.axis_index("col")
    for d in range(cols):
        start = pl.multiple_of(sends_to(col, d, cols) * slab, 8)
        chunks[d][...] = total[pl.ds(start, slab), :]


def first_force(k, arrived, base, slab, cols):
    rows, (block, reals) = len(arrived), base.shape
    out = call(
        functools.partial(first_force_kernel, cols, rows),
        (jax.ShapeDtypeStruct((slab, reals), F32),) * cols
        + (jax.ShapeDtypeStruct((rows * slab, reals), BF16),),
        [VMEM] * (2 + rows),
        (k, *arrived, base),
        2 * rows * slab * block * reals, 8 * block * reals,
        [pltpu.VMEM((block, reals), F32)],
    )
    return out[:cols], out[cols]


def force_kernel(cols, rows, *refs):
    lags, arrived, bases = refs[0], refs[1 : 1 + rows], refs[1 + rows : 3 + rows]
    chunks, (whole, total) = refs[3 + rows : -2], refs[-2:]
    slab, reals = chunks[0].shape[0] // 2, chunks[0].shape[1]
    gather_newest(arrived, whole, slab, reals)
    lag_rows = rows * slab
    col = lax.axis_index("col")
    for n in range(2):
        total[n] = bases[n][...] + dot_rows(
            lags[n * lag_rows : (n + 1) * lag_rows, :], whole[...]
        )
        for d in range(cols):
            start = pl.multiple_of(sends_to(col, d, cols) * slab, 8)
            chunks[d][n * slab : (n + 1) * slab, :] = total[n, pl.ds(start, slab), :]


def force_pieces(lags, arrived, bases, slab, cols):
    rows, (block, reals) = len(arrived), bases[0].shape
    return call(
        functools.partial(force_kernel, cols, rows),
        (jax.ShapeDtypeStruct((2 * slab, reals), F32),) * cols,
        [VMEM] * (3 + rows),
        (lags, *arrived, *bases),
        4 * rows * slab * block * reals, 16 * block * reals,
        [pltpu.VMEM((rows * slab, reals), BF16), pltpu.VMEM((2, block, reals), F32)],
    )


def prepare_kernel(x, v, a, e, stiff, predicted, load):
    p = x[...] + DT * v[...] + QUARTER * a[...]
    predicted[...] = p
    load[...] = e[...] - dot_exact(stiff[...], p)


def prepare(x, v, a, e, stiff):
    shape = jax.ShapeDtypeStruct(x.shape, F32)
    return call(
        prepare_kernel, (shape, shape), [VMEM] * 5, (x, v, a, e, stiff),
        12 * x.size * x.shape[0], 24 * x.size,
    )


def summed(parts, first, count):
    total = parts[0][first : first + count, :]
    for part in parts[1:]:
        total = total + part[first : first + count, :]
    return total


def split(value, count):
    out = []
    for _ in range(count):
        out.append(value.astype(BF16).astype(F32))
        value = value - out[-1]
    return out


def first_advance_kernel(cols, rows, *refs):
    parts = refs[:cols]
    predicted, v, a, load, inverse = refs[cols : cols + 5]
    riders = refs[cols + 5 : cols + 5 + rows]
    x_out, v_out, a_out, *messages = refs[cols + 5 + rows :]
    slab, reals = v.shape
    a_next = dot_exact(inverse[...], load[...] - summed(parts, 0, slab))
    v_next = v[...] + 0.5 * DT * (a[...] + a_next)
    v_half = v_next.astype(BF16)
    for message, rider in zip(messages, riders):
        message[0:slab, 0:reals] = v_half
        message[slab:, :] = rider[...]
    v_out[...] = v_next
    a_out[...] = a_next
    x_out[...] = predicted[...] + QUARTER * a_next


def first_advance(parts, predicted, v, a, load, inverse, riders):
    shape = jax.ShapeDtypeStruct(v.shape, F32)
    lines, lanes = riders[0].shape
    message = jax.ShapeDtypeStruct((v.shape[0] + lines, lanes), BF16)
    out = call(
        functools.partial(first_advance_kernel, len(parts), len(riders)),
        (shape,) * 3 + (message,) * len(riders),
        [VMEM] * (len(parts) + 5 + len(riders)),
        (*parts, predicted, v, a, load, inverse, *riders),
        12 * v.size * v.shape[0], 40 * v.size,
    )
    return out[0], out[1], out[2], out[3:]


def drift_kernel(predicted, v, a, e, early, moved, both):
    slab = v.shape[0]
    both[0:slab, :] = predicted[...] + DT * v[...] + 0.5 * DT * DT * a[...]
    both[slab:, :] = e[...]
    moved[...] = dot_exact(early[...], both[...])


def drift(predicted, v, a, e, early):
    lines, reals = early.shape[0], v.shape[1]
    return call(
        drift_kernel,
        jax.ShapeDtypeStruct((lines, reals), F32),
        [VMEM] * 5,
        (predicted, v, a, e, early),
        12 * early.size * reals, 24 * v.size,
        [pltpu.VMEM((2 * v.shape[0], reals), F32)],
    )


def last_advance_kernel(cols, rows, *refs):
    parts = refs[:cols]
    v, a, load, inverse, drifted, late = refs[cols : cols + 6]
    v_out, a_out, rest, *messages = refs[cols + 6 : -2]
    held, both = refs[-2:]
    slab, _ = v.shape
    size = late.shape[0] // rows
    turning = load[...] - summed(parts, 0, slab)
    known = summed(parts, slab, slab)
    both[0:slab, :] = turning
    both[slab:, :] = known
    moved = drifted[...] + dot_exact(late[...], both[...])
    a_next = dot_exact(inverse[...], turning)
    v_next = v[...] + 0.5 * DT * (a[...] + a_next)
    v_half = v_next.astype(BF16)
    cuts = split(moved, 2)
    for d in range(rows):
        for k in range(2):
            held[k * size : (k + 1) * size, :] = cuts[k][d * size : (d + 1) * size, :]
        messages[d][0:slab, :] = v_half
        messages[d][slab:, :] = held[...].astype(BF16)
    v_out[...] = v_next
    a_out[...] = a_next
    rest[...] = known


def last_advance(parts, v, a, load, inverse, drifted, late, rows):
    slab, reals = v.shape
    size = late.shape[0] // rows
    shape = jax.ShapeDtypeStruct(v.shape, F32)
    out = call(
        functools.partial(last_advance_kernel, len(parts), rows),
        (shape,) * 3 + (jax.ShapeDtypeStruct((slab + 2 * size, reals), BF16),) * rows,
        [VMEM] * (len(parts) + 6),
        (*parts, v, a, load, inverse, drifted, late),
        48 * v.size * slab, 40 * v.size,
        [pltpu.VMEM((2 * size, reals), F32), pltpu.VMEM((2 * slab, reals), F32)],
    )
    return out[0], out[1], out[2], out[3:]


def settled_kernel(predicted, v, a, e, rest, inverse, stiff, out):
    ahead = predicted[...] + DT * v[...] + 2 * QUARTER * a[...]
    push = dot_exact(inverse[...], e[...] - rest[...] - dot_exact(stiff[...], ahead))
    out[...] = v[...] + 0.5 * DT * (a[...] + push)


def settled_velocity(predicted, v, a, e, rest, inverse, stiff):
    return call(
        settled_kernel,
        jax.ShapeDtypeStruct(v.shape, F32),
        [VMEM] * 7,
        (predicted, v, a, e, rest, inverse, stiff),
        24 * v.size * v.shape[0], 32 * v.size,
    )


def last_force_kernel(cols, rows, *refs):
    lags, listed = refs[0], refs[1]
    arrived = refs[2 : 2 + rows]
    chunks, (whole, total) = refs[2 + rows : -2], refs[-2:]
    slab = chunks[0].shape[0] // 2
    row, col = lax.axis_index("row"), lax.axis_index("col")
    for d in range(rows):
        start = pl.multiple_of(comes_from(row, d, rows) * slab, 16)
        whole[pl.ds(start, slab), :] = arrived[d][0:slab, :]
    newest = whole[...]
    total[0] = dot_rows(lags[0 : rows * slab, :], newest)
    total[1] = jnp.dot(listed[...], newest, preferred_element_type=F32)
    for d in range(cols):
        start = pl.multiple_of(sends_to(col, d, cols) * slab, 8)
        for k in range(2):
            chunks[d][k * slab : (k + 1) * slab, :] = total[k, pl.ds(start, slab), :]


def last_force(lags, listed, arrived, slab, cols):
    rows, block, reals = len(arrived), lags.shape[1], arrived[0].shape[1]
    return call(
        functools.partial(last_force_kernel, cols, rows),
        (jax.ShapeDtypeStruct((2 * slab, reals), F32),) * cols,
        [VMEM] * (2 + rows),
        (lags, listed, *arrived),
        4 * rows * slab * block * reals, 8 * block * reals,
        [pltpu.VMEM((rows * slab, reals), BF16), pltpu.VMEM((2, block, reals), F32)],
    )


def listed_kernel(rows, cols, slab, lag_rows, *refs):
    arrived, (take, own_take, weights) = refs[:rows], refs[rows : rows + 3]
    listed, pull, held, stack, blocks = refs[rows + 3 :]
    size = own_take.shape[1] // rows
    modules = slab // 6
    for d in range(rows):
        held[...] = arrived[d][slab:, :].astype(F32)
        for c in range(cols):
            stack[c, d * size : (d + 1) * size, :] = held[c * size : (c + 1) * size, 0:lag_rows]
        cuts = [held[0:size, lag_rows + 6 * k : lag_rows + 6 * k + 6] for k in range(3)]
        blocks[d * size : (d + 1) * size, :] = (cuts[2] + cuts[1]) + cuts[0]
    for c in range(cols):
        found = jnp.dot(take[c].astype(BF16), stack[c].astype(BF16), preferred_element_type=F32)
        listed[c * slab : (c + 1) * slab, :] = found.astype(BF16)
    block = dot_exact(own_take[...], blocks[...])
    lane = lax.broadcasted_iota(jnp.int32, (slab, slab), 1) // 6
    module = lax.broadcasted_iota(jnp.int32, (slab, slab), 0) // 6
    inverse = jnp.where(lane == module, jnp.concatenate([block] * modules, axis=1), 0.0)
    cuts = split(QUARTER * dot_exact(weights[...], inverse), 3)
    for k, (part, _) in enumerate(PAIRS):
        pull[:, k * slab : (k + 1) * slab] = cuts[part].astype(BF16)


def listed_parts(arrived, take, own_take, weights, slab, lag_rows):
    rows, cols = len(arrived), take.shape[0]
    lines, lanes = arrived[0].shape
    return call(
        functools.partial(listed_kernel, rows, cols, slab, lag_rows),
        (
            jax.ShapeDtypeStruct((cols * slab, lag_rows), BF16),
            jax.ShapeDtypeStruct((weights.shape[0], len(PAIRS) * slab), BF16),
        ),
        [VMEM] * (rows + 3),
        (*arrived, take, own_take, weights),
        4 * take.size * lag_rows, 4 * take.size,
        [
            pltpu.VMEM((lines - slab, lanes), F32),
            pltpu.VMEM((cols, own_take.shape[1], lag_rows), F32),
            pltpu.VMEM((own_take.shape[1], 6), F32),
        ],
    )


def settled_gaps_kernel(rows, *refs):
    arrived, (own_take, weights, out, held) = refs[:rows], refs[rows:]
    size = own_take.shape[1] // rows
    slab = own_take.shape[0]
    for d in range(rows):
        cuts = arrived[d][slab:, :].astype(F32)
        held[d * size : (d + 1) * size, :] = cuts[size : 2 * size, :] + cuts[0:size, :]
    out[...] = dot_exact(weights[...], dot_exact(own_take[...], held[...]))


def settled_gaps(arrived, own_take, weights):
    rows, reals = len(arrived), arrived[0].shape[1]
    return call(
        functools.partial(settled_gaps_kernel, rows),
        jax.ShapeDtypeStruct((weights.shape[0], reals), F32),
        [VMEM] * (rows + 2),
        (*arrived, own_take, weights),
        12 * weights.size * reals, 4 * weights.shape[0] * reals,
        [pltpu.VMEM((own_take.shape[1], reals), F32)],
    )


def end_kernel(cols, pieces, *refs):
    parts = refs[:cols]
    settled, inverse, known, pull, v_out, out, v_done, done, stack, sems = refs[cols:]
    slab = settled.shape[0]
    lines = known.shape[0] // pieces
    cuts = split(summed(parts, slab, slab), 3)
    for k, (_, part) in enumerate(PAIRS):
        stack[k * slab : (k + 1) * slab, :] = cuts[part].astype(BF16)
    copies = []
    for i in range(pieces):
        at = pl.ds(i * lines, lines)
        done[at, :] = known[at, :] - jnp.dot(
            pull[at, :], stack[...], preferred_element_type=F32
        )
        copies.append(pltpu.make_async_copy(done.at[at], out.at[at], sems.at[i]))
        copies[-1].start()
        if i == 0:
            push = dot_exact(inverse[...], summed(parts, 0, slab))
            v_done[...] = settled[...] - 0.5 * DT * push
            copies.append(pltpu.make_async_copy(v_done, v_out, sems.at[pieces]))
            copies[-1].start()
    for copy in copies:
        copy.wait()


def end(parts, settled, inverse, known, pull, pieces):
    hbm = pl.BlockSpec(memory_space=pltpu.MemorySpace.HBM)
    v_shape = jax.ShapeDtypeStruct(settled.shape, F32)
    shape = jax.ShapeDtypeStruct(known.shape, F32)
    return pl.pallas_call(
        functools.partial(end_kernel, len(parts), pieces),
        out_shape=(v_shape, shape),
        in_specs=[VMEM] * (len(parts) + 4),
        out_specs=(hbm, hbm),
        scratch_shapes=[
            pltpu.VMEM(settled.shape, F32),
            pltpu.VMEM(known.shape, F32),
            pltpu.VMEM((len(PAIRS) * settled.shape[0], settled.shape[1]), BF16),
            pltpu.SemaphoreType.DMA((pieces + 1,)),
        ],
        compiler_params=pltpu.CompilerParams(vmem_limit_bytes=16 << 20),
        cost_estimate=pl.CostEstimate(
            flops=12 * pull.size * settled.shape[1], bytes_accessed=8 * known.size, transcendentals=0
        ),
    )(*parts, settled, inverse, known, pull)


def diagonals_kernel(*refs):
    half = len(refs) // 2
    for blocks, out in zip(refs[:half], refs[half:]):
        modules = blocks.shape[1]
        width = 6 * modules
        lane = lax.broadcasted_iota(jnp.int32, (modules, width), 1) // 6
        module = lax.broadcasted_iota(jnp.int32, (modules, width), 0)
        for i in range(6):
            spread = jnp.concatenate([blocks[i]] * modules, axis=1)
            out[pl.ds(i, modules, stride=6), :] = jnp.where(lane == module, spread, 0.0)


def diagonals(*matrices):
    width = 6 * matrices[0].shape[0]
    shape = jax.ShapeDtypeStruct((width, width), F32)
    return call(
        diagonals_kernel, (shape,) * len(matrices), [VMEM] * len(matrices),
        tuple(m.transpose(1, 0, 2) for m in matrices), 100 * width * width, 16 * width * width,
    )


def plan_kernel(rows, cols, capacity, size, *refs):
    owned, lags, blocks = refs[:3]
    riders = refs[3 : 3 + rows]
    send, take, own_take, sends, coef, turned, held = refs[3 + rows :]
    modules = send.shape[1] // 6
    row, col = lax.axis_index("row"), lax.axis_index("col")
    slab, lag_rows = modules * 6, turned.shape[1]
    turned[...] = lags[0:lag_rows, :].T
    shape = (size, slab)
    i = lax.broadcasted_iota(jnp.int32, shape, 0)
    j = lax.broadcasted_iota(jnp.int32, shape, 1)
    wide = (slab, rows * size)
    p = lax.broadcasted_iota(jnp.int32, wide, 0)
    q = lax.broadcasted_iota(jnp.int32, wide, 1)
    for c in range(cols):
        home = (row * cols + c) * modules
        for d in range(rows):
            first = (sends_to(row, d, rows) * cols + c) * modules
            wanted = jnp.full(shape, -1, jnp.int32)
            for k in range(modules):
                local = owned[first + k] - home
                here = (local >= 0) & (local < modules)
                wanted = jnp.where((i // 6 == k % capacity) & here, local, wanted)
            hit = (wanted == j // 6) & (i % 6 == j % 6)
            sends[c, d * size : (d + 1) * size, :] = jnp.where(hit, 1.0, 0.0)
        place = p % 6
        for k in range(modules):
            source = owned[home + k] // (cols * modules)
            d = source ^ row if rows & (rows - 1) == 0 else (row + rows - source) % rows
            place = place + jnp.where(p // 6 == k, d * size + k % capacity * 6, 0)
        take[c] = jnp.where(place == q, 1.0, 0.0)
        picked = jnp.dot(
            sends[c].astype(BF16), turned[c * slab : (c + 1) * slab, :], preferred_element_type=F32
        )
        for d in range(rows):
            held[d, c * size : (c + 1) * size, 0:lag_rows] = picked[d * size : (d + 1) * size, :]
    send[...] = sends[col]
    own_take[...] = take[col]
    for k in range(6):
        coef[pl.ds(k, modules, stride=6), :] = blocks[k]
    cuts = jnp.concatenate(split(dot_exact(send[...], coef[...]), 3), axis=1)
    for d in range(rows):
        held[d, 0:size, lag_rows : lag_rows + 18] = cuts[d * size : (d + 1) * size, :]
        riders[d][...] = held[d].astype(BF16)


def gap_map_kernel(links, arms, inverse, stiff, send, weights, early, late, table):
    modules = weights.shape[1] // 6
    points = links.shape[0] // modules
    row, col = lax.axis_index("row"), lax.axis_index("col")
    cols = lax.axis_size("col")
    slab = modules * 6
    count = modules * points
    table[:, 0:3] = arms[...]
    position = lax.broadcasted_iota(jnp.int32, (count, 1), 0)
    table[:, 3:4] = (position // points * 6).astype(F32)
    own = table[...]
    first_point = (row * cols + col) * count
    point = lax.broadcasted_iota(jnp.int32, (count, count), 1)
    meets = jnp.where(links[...] - first_point == point, 1.0, 0.0)
    partner = dot_exact(meets, own)
    deep = (count, slab)
    column = lax.broadcasted_iota(jnp.int32, deep, 1)
    total = [None] * 3
    for sign, side in ((1.0, own), (-1.0, partner)):
        mode = column - (side[:, 3:4] + 0.5).astype(jnp.int32)
        e = [jnp.broadcast_to(sign * side[:, c : c + 1], deep) for c in range(3)]
        for c in range(3):
            up, down = (c + 1) % 3, (c + 2) % 3
            value = jnp.where(mode == c, sign, 0.0)
            value = jnp.where(mode == 3 + up, e[down], value)
            value = jnp.where(mode == 3 + down, -e[up], value)
            total[c] = value if total[c] is None else total[c] + value
    for m in range(modules):
        for c in range(3):
            start = (m * 3 + c) * points
            weights[start : start + points, :] = total[c][m * points : (m + 1) * points, :]
    press = dot_exact(send[...], QUARTER * inverse[...])
    drift = send[...] - dot_exact(press, stiff[...])
    early[:, 0:slab] = drift
    early[:, slab:] = press
    late[:, 0:slab] = dot_exact((2 * QUARTER + 0.25 * DT) * drift, inverse[...])
    late[:, slab:] = -press


def gap_map(links, arms, inverse, stiff, send):
    modules, points = links.shape
    slab = 6 * modules
    wide = jax.ShapeDtypeStruct((send.shape[0], 2 * slab), F32)
    return call(
        gap_map_kernel,
        (jax.ShapeDtypeStruct((modules * 3 * points, slab), F32), wide, wide),
        [VMEM] * 5,
        (links.reshape(-1, 1), arms.transpose(0, 2, 1).reshape(-1, 3), inverse, stiff, send),
        12 * (modules * points) ** 2 * 4, 16 * modules * 3 * points * slab,
        [pltpu.VMEM((modules * points, 4), F32)],
    )


def plan(owned, lags, solve_inverse, rows, cols, lag_rows, reals):
    modules = solve_inverse.shape[0]
    slab, block = modules * 6, lags.shape[1]
    capacity = 2 * modules // rows
    size = -(-capacity * 6 // 8) * 8
    lines, lanes = cols * size, max(reals, lag_rows + 18)
    out = call(
        functools.partial(plan_kernel, rows, cols, capacity, size),
        (jax.ShapeDtypeStruct((lines, lanes), BF16),) * rows
        + (
            jax.ShapeDtypeStruct((rows * size, slab), F32),
            jax.ShapeDtypeStruct((cols, slab, rows * size), F32),
            jax.ShapeDtypeStruct((slab, rows * size), F32),
        ),
        [SMEM, VMEM, VMEM],
        (owned, lags, solve_inverse.transpose(1, 0, 2)),
        4 * rows * cols * size * slab * lag_rows, 16 * rows * lines * lanes,
        [
            pltpu.VMEM((cols, rows * size, slab), F32),
            pltpu.VMEM((slab, 6), F32),
            pltpu.VMEM((block, lag_rows), BF16),
            pltpu.VMEM((rows, lines, lanes), F32),
        ],
    )
    return out[:rows], *out[rows:]


def after(value, *others):
    return lax.optimization_barrier((value, *others))[0]


def body(
    kernel,
    history,
    displacement,
    velocity,
    acceleration,
    excitation,
    solve_inverse,
    stiffness,
    owned,
    links,
    arms,
):
    rows, cols = lax.axis_size("row"), lax.axis_size("col")
    steps = excitation.shape[0]
    slab, reals = velocity.shape
    modules, points = links.shape
    x, v, a = displacement, velocity, acceleration
    arrived = exchange([v] * rows, "row")
    lags, past, base = known_force(
        kernel.reshape(-1, kernel.shape[3]), history.reshape(-1, reals), rows * slab
    )
    inverse, stiff = diagonals(solve_inverse, stiffness)
    predicted, load = prepare(x, v, a, excitation[0], stiff)
    pieces, newest = first_force(lags, arrived, base, slab, cols)
    riders, send, take, own_take = plan(
        after(owned, pieces[0]), lags, solve_inverse, rows, cols, rows * slab, reals
    )
    parts = exchange(pieces, "col")
    x, v, a, messages = first_advance(parts, predicted, v, a, load, inverse, riders)
    arrived = exchange(messages, "row")
    predicted, load = prepare(x, v, a, excitation[1], stiff)
    weights, early, late = gap_map(after(links, v), arms, inverse, stiff, send)
    drifted = drift(predicted, v, a, excitation[2], early)
    bases = later_forces(lags, past, after(newest, v), steps - 1)
    pieces = force_pieces(lags, arrived, bases, slab, cols)
    parts = exchange(pieces, "col")
    listed, pull = listed_parts(arrived, take, own_take, weights, slab, rows * slab)
    v, a, rest, messages = last_advance(parts, v, a, load, inverse, drifted, late, rows)
    arrived = exchange(messages, "row")
    settled = settled_velocity(predicted, v, a, excitation[2], rest, inverse, stiff)
    pieces = last_force(lags, listed, arrived, slab, cols)
    parts = exchange(pieces, "col")
    known = settled_gaps(arrived, own_take, weights)
    v, out = end(parts, settled, inverse, known, pull, 4 if modules % 4 == 0 else 1)
    return v, out.reshape(modules, 3, points, reals).transpose(0, 2, 1, 3)


def solution(mesh):
    placed = (
        P(None, None, "col", "row"),
        P(None, None, "col", "sea"),
        P(("row", "col"), "sea"),
        P(("row", "col"), "sea"),
        P(("row", "col"), "sea"),
        P(None, ("row", "col"), "sea"),
        P(("row", "col"), None, None),
        P(("row", "col"), None, None),
        P(),
        P(("row", "col"), None),
        P(("row", "col"), None, None),
    )
    return jax.shard_map(
        body,
        mesh=mesh,
        in_specs=placed,
        out_specs=(P(("row", "col"), "sea"), P(("row", "col"), None, None, "sea")),
        check_vma=False,
    )
```

```python
import functools

import jax
import jax.numpy as jnp
from jax import lax
from jax.experimental import pallas as pl
from jax.experimental.pallas import tpu as pltpu
from jax.sharding import PartitionSpec as P


DT = 0.5
QUARTER = DT * DT / 4.0
F32 = jnp.float32
BF16 = jnp.bfloat16
HIGHEST = lax.Precision.HIGHEST
PAIRS = ((0, 0), (0, 1), (0, 2), (1, 0), (1, 1), (2, 0))
VMEM = pl.BlockSpec(memory_space=pltpu.VMEM)
SMEM = pl.BlockSpec(memory_space=pltpu.SMEM)


def sends_to(i, d, n):
    return i ^ d if n & (n - 1) == 0 else (i + d) % n


def comes_from(i, d, n):
    return i ^ d if n & (n - 1) == 0 else (i + n - d) % n


def exchange(pieces, axis):
    n = lax.axis_size(axis)
    out = [pieces[0]] + [None] * (n - 1)
    for d in range(n - 1, 0, -1):
        out[d] = lax.ppermute(pieces[d], axis, [(i, sends_to(i, d, n)) for i in range(n)])
    return out


def dot_rows(a, b):
    return lax.dot_general(a, b, (((0,), (0,)), ((), ())), preferred_element_type=F32)


def dot_exact(a, b):
    return jnp.dot(a, b, precision=HIGHEST, preferred_element_type=F32)


def padded_bytes(shape, dtype):
    size = jnp.dtype(dtype).itemsize
    dims = (1, 1, *shape)
    up = lambda n, m: -(-n // m) * m
    major = 1
    for n in dims[:-2]:
        major *= n
    return major * up(dims[-2], 32 // size) * up(dims[-1], 128) * size


def call(body, shapes, in_specs, args, flops, nbytes, scratch=()):
    arrays = list(args) + jax.tree.leaves(shapes)
    held = sum(padded_bytes(t.shape, t.dtype) for t in arrays)
    held += sum(padded_bytes(t.shape, t.dtype) for t in scratch if t.shape[1:])
    return pl.pallas_call(
        body,
        out_shape=shapes,
        in_specs=in_specs,
        out_specs=jax.tree.map(lambda _: VMEM, shapes),
        scratch_shapes=scratch,
        compiler_params=pltpu.CompilerParams(
            vmem_limit_bytes=min(2 * held + (2 << 20), 60 << 20)
        ),
        cost_estimate=pl.CostEstimate(flops=flops, bytes_accessed=nbytes, transcendentals=0),
    )(*args)


def known_kernel(lag_rows, pieces, k_hbm, h_hbm, k_ref, h_ref, out, k_sem, h_sem):
    copies = []
    for far, near, sems in ((k_hbm, k_ref, k_sem), (h_hbm, h_ref, h_sem)):
        size = far.shape[0] // pieces
        for i in range(pieces):
            at = pl.ds(i * size, size)
            copies.append(pltpu.make_async_copy(far.at[at], near.at[at], sems.at[i]))
            copies[-1].start()
    for copy in copies:
        copy.wait()
    total = k_ref.shape[0]
    out[...] = dot_rows(k_ref[lag_rows:, :], h_ref[: total - lag_rows, :])


def known_force(kernel_flat, history_flat, lag_rows):
    shapes = (
        jax.ShapeDtypeStruct(kernel_flat.shape, BF16),
        jax.ShapeDtypeStruct(history_flat.shape, BF16),
        jax.ShapeDtypeStruct((kernel_flat.shape[1], history_flat.shape[1]), F32),
    )
    pieces = 2 if kernel_flat.shape[0] % 32 == 0 and history_flat.shape[0] % 32 == 0 else 1
    return call(
        functools.partial(known_kernel, lag_rows, pieces),
        shapes,
        [pl.BlockSpec(memory_space=pltpu.MemorySpace.HBM)] * 2,
        tuple(
            pltpu.with_memory_space_constraint(t, pltpu.MemorySpace.HBM)
            for t in (kernel_flat, history_flat)
        ),
        2 * kernel_flat.size * history_flat.shape[1],
        2 * (kernel_flat.size + history_flat.size),
        [pltpu.SemaphoreType.DMA((pieces,)), pltpu.SemaphoreType.DMA((pieces,))],
    )


def later_kernel(k_ref, h_ref, newest, *outs):
    total, lag_rows = k_ref.shape[0], newest.shape[0]
    for n, out in enumerate(outs):
        first = (n + 1) * lag_rows
        out[...] = dot_rows(k_ref[first : first + lag_rows, :], newest[...]) + dot_rows(
            k_ref[first + lag_rows :, :], h_ref[: total - first - lag_rows, :]
        )


def later_forces(k, h, newest, count):
    shape = jax.ShapeDtypeStruct((k.shape[1], h.shape[1]), F32)
    return call(
        later_kernel, (shape,) * count, [VMEM] * 3, (k, h, newest),
        2 * count * k.size * h.shape[1], 2 * (k.size + h.size),
    )


def gather_newest(arrived, whole, slab, reals):
    row, rows = lax.axis_index("row"), len(arrived)
    for d in range(rows):
        start = pl.multiple_of(comes_from(row, d, rows) * slab, 16)
        whole[pl.ds(start, slab), :] = arrived[d][0:slab, 0:reals].astype(BF16)


def first_force_kernel(cols, rows, *refs):
    k_ref, arrived, base = refs[0], refs[1 : 1 + rows], refs[1 + rows]
    chunks, (whole, total) = refs[2 + rows : -2], refs[-2:]
    slab, reals = chunks[0].shape
    gather_newest(arrived, whole, slab, reals)
    total[...] = base[...] + dot_rows(k_ref[0 : rows * slab, :], whole[...])
    col = lax.axis_index("col")
    for d in range(cols):
        start = pl.multiple_of(sends_to(col, d, cols) * slab, 8)
        chunks[d][...] = total[pl.ds(start, slab), :]


def first_force(k, arrived, base, slab, cols):
    rows, (block, reals) = len(arrived), base.shape
    out = call(
        functools.partial(first_force_kernel, cols, rows),
        (jax.ShapeDtypeStruct((slab, reals), F32),) * cols
        + (jax.ShapeDtypeStruct((rows * slab, reals), BF16),),
        [VMEM] * (2 + rows),
        (k, *arrived, base),
        2 * rows * slab * block * reals, 8 * block * reals,
        [pltpu.VMEM((block, reals), F32)],
    )
    return out[:cols], out[cols]


def force_kernel(cols, rows, *refs):
    turned, arrived, bases = refs[0], refs[1 : 1 + rows], refs[1 + rows : 3 + rows]
    chunks, (whole, total) = refs[3 + rows : -2], refs[-2:]
    slab, reals = chunks[0].shape[0] // 2, chunks[0].shape[1]
    gather_newest(arrived, whole, slab, reals)
    col = lax.axis_index("col")
    for n in range(2):
        total[n] = bases[n][...] + jnp.dot(
            turned[n], whole[...], preferred_element_type=F32
        )
        for d in range(cols):
            start = pl.multiple_of(sends_to(col, d, cols) * slab, 8)
            chunks[d][n * slab : (n + 1) * slab, :] = total[n, pl.ds(start, slab), :]


def force_pieces(turned, arrived, bases, slab, cols):
    rows, (block, reals) = len(arrived), bases[0].shape
    return call(
        functools.partial(force_kernel, cols, rows),
        (jax.ShapeDtypeStruct((2 * slab, reals), F32),) * cols,
        [VMEM] * (3 + rows),
        (turned, *arrived, *bases),
        4 * rows * slab * block * reals, 16 * block * reals,
        [pltpu.VMEM((rows * slab, reals), BF16), pltpu.VMEM((2, block, reals), F32)],
    )


def prepare_kernel(x, v, a, e, stiff, predicted, load):
    p = x[...] + DT * v[...] + QUARTER * a[...]
    predicted[...] = p
    load[...] = e[...] - dot_exact(stiff[...], p)


def prepare(x, v, a, e, stiff):
    shape = jax.ShapeDtypeStruct(x.shape, F32)
    return call(
        prepare_kernel, (shape, shape), [VMEM] * 5, (x, v, a, e, stiff),
        12 * x.size * x.shape[0], 24 * x.size,
    )


def summed(parts, first, count):
    total = parts[0][first : first + count, :]
    for part in parts[1:]:
        total = total + part[first : first + count, :]
    return total


def split(value, count):
    out = []
    for _ in range(count):
        out.append(value.astype(BF16).astype(F32))
        value = value - out[-1]
    return out


def first_advance_kernel(cols, rows, *refs):
    parts = refs[:cols]
    predicted, v, a, load, inverse = refs[cols : cols + 5]
    riders = refs[cols + 5 : cols + 5 + rows]
    x_out, v_out, a_out, *messages = refs[cols + 5 + rows :]
    slab, reals = v.shape
    a_next = dot_exact(inverse[...], load[...] - summed(parts, 0, slab))
    v_next = v[...] + 0.5 * DT * (a[...] + a_next)
    v_half = v_next.astype(BF16)
    for message, rider in zip(messages, riders):
        message[0:slab, 0:reals] = v_half
        message[slab:, :] = rider[...]
    v_out[...] = v_next
    a_out[...] = a_next
    x_out[...] = predicted[...] + QUARTER * a_next


def first_advance(parts, predicted, v, a, load, inverse, riders):
    shape = jax.ShapeDtypeStruct(v.shape, F32)
    lines, lanes = riders[0].shape
    message = jax.ShapeDtypeStruct((v.shape[0] + lines, lanes), BF16)
    out = call(
        functools.partial(first_advance_kernel, len(parts), len(riders)),
        (shape,) * 3 + (message,) * len(riders),
        [VMEM] * (len(parts) + 5 + len(riders)),
        (*parts, predicted, v, a, load, inverse, *riders),
        12 * v.size * v.shape[0], 40 * v.size,
    )
    return out[0], out[1], out[2], out[3:]


def drift_kernel(predicted, v, a, e, early, moved, both):
    slab = v.shape[0]
    both[0:slab, :] = predicted[...] + DT * v[...] + 0.5 * DT * DT * a[...]
    both[slab:, :] = e[...]
    moved[...] = dot_exact(early[...], both[...])


def drift(predicted, v, a, e, early):
    lines, reals = early.shape[0], v.shape[1]
    return call(
        drift_kernel,
        jax.ShapeDtypeStruct((lines, reals), F32),
        [VMEM] * 5,
        (predicted, v, a, e, early),
        12 * early.size * reals, 24 * v.size,
        [pltpu.VMEM((2 * v.shape[0], reals), F32)],
    )


def last_advance_kernel(cols, rows, *refs):
    parts = refs[:cols]
    v, a, load, inverse, drifted, late = refs[cols : cols + 6]
    v_out, a_out, rest, *messages = refs[cols + 6 : -2]
    held, both = refs[-2:]
    slab, _ = v.shape
    size = late.shape[0] // rows
    turning = load[...] - summed(parts, 0, slab)
    known = summed(parts, slab, slab)
    both[0:slab, :] = turning
    both[slab:, :] = known
    moved = drifted[...] + dot_exact(late[...], both[...])
    a_next = dot_exact(inverse[...], turning)
    v_next = v[...] + 0.5 * DT * (a[...] + a_next)
    v_half = v_next.astype(BF16)
    cuts = split(moved, 2)
    for d in range(rows):
        for k in range(2):
            held[k * size : (k + 1) * size, :] = cuts[k][d * size : (d + 1) * size, :]
        messages[d][0:slab, :] = v_half
        messages[d][slab:, :] = held[...].astype(BF16)
    v_out[...] = v_next
    a_out[...] = a_next
    rest[...] = known


def last_advance(parts, v, a, load, inverse, drifted, late, rows):
    slab, reals = v.shape
    size = late.shape[0] // rows
    shape = jax.ShapeDtypeStruct(v.shape, F32)
    out = call(
        functools.partial(last_advance_kernel, len(parts), rows),
        (shape,) * 3 + (jax.ShapeDtypeStruct((slab + 2 * size, reals), BF16),) * rows,
        [VMEM] * (len(parts) + 6),
        (*parts, v, a, load, inverse, drifted, late),
        48 * v.size * slab, 40 * v.size,
        [pltpu.VMEM((2 * size, reals), F32), pltpu.VMEM((2 * slab, reals), F32)],
    )
    return out[0], out[1], out[2], out[3:]


def settled_kernel(predicted, v, a, e, rest, inverse, stiff, out):
    ahead = predicted[...] + DT * v[...] + 2 * QUARTER * a[...]
    push = dot_exact(inverse[...], e[...] - rest[...] - dot_exact(stiff[...], ahead))
    out[...] = v[...] + 0.5 * DT * (a[...] + push)


def settled_velocity(predicted, v, a, e, rest, inverse, stiff):
    return call(
        settled_kernel,
        jax.ShapeDtypeStruct(v.shape, F32),
        [VMEM] * 7,
        (predicted, v, a, e, rest, inverse, stiff),
        24 * v.size * v.shape[0], 32 * v.size,
    )


def last_force_kernel(cols, rows, *refs):
    turned, listed = refs[0], refs[1]
    arrived = refs[2 : 2 + rows]
    chunks, (whole, total) = refs[2 + rows : -2], refs[-2:]
    slab = chunks[0].shape[0] // 2
    row, col = lax.axis_index("row"), lax.axis_index("col")
    for d in range(rows):
        start = pl.multiple_of(comes_from(row, d, rows) * slab, 16)
        whole[pl.ds(start, slab), :] = arrived[d][0:slab, :]
    newest = whole[...]
    total[0] = jnp.dot(turned[0], newest, preferred_element_type=F32)
    total[1] = jnp.dot(listed[...], newest, preferred_element_type=F32)
    for d in range(cols):
        start = pl.multiple_of(sends_to(col, d, cols) * slab, 8)
        for k in range(2):
            chunks[d][k * slab : (k + 1) * slab, :] = total[k, pl.ds(start, slab), :]


def last_force(turned, listed, arrived, slab, cols):
    rows, block, reals = len(arrived), turned.shape[1], arrived[0].shape[1]
    return call(
        functools.partial(last_force_kernel, cols, rows),
        (jax.ShapeDtypeStruct((2 * slab, reals), F32),) * cols,
        [VMEM] * (2 + rows),
        (turned, listed, *arrived),
        4 * rows * slab * block * reals, 8 * block * reals,
        [pltpu.VMEM((rows * slab, reals), BF16), pltpu.VMEM((2, block, reals), F32)],
    )


def listed_kernel(rows, cols, slab, lag_rows, *refs):
    arrived, (own_rider, other, take, own_take, weights) = refs[:rows], refs[rows : rows + 5]
    listed, pull, held, stack, blocks = refs[rows + 5 :]
    size = own_take.shape[1] // rows
    modules = slab // 6
    part = arrived[0].shape[0] - slab
    shared = part < held.shape[0]
    for d in range(rows):
        if d == 0:
            held[...] = own_rider[...].astype(F32)
        else:
            mine = pl.multiple_of(lax.axis_index("sea") * part, 8) if shared else 0
            held[pl.ds(mine, part), :] = arrived[d][slab:, :].astype(F32)
            if shared:
                theirs = pl.multiple_of(part - mine, 8)
                held[pl.ds(theirs, part), :] = other[(d - 1) * part : d * part, :].astype(F32)
        for c in range(cols):
            stack[c, d * size : (d + 1) * size, :] = held[c * size : (c + 1) * size, 0:lag_rows]
        cuts = [held[0:size, lag_rows + 6 * k : lag_rows + 6 * k + 6] for k in range(3)]
        blocks[d * size : (d + 1) * size, :] = (cuts[2] + cuts[1]) + cuts[0]
    for c in range(cols):
        found = jnp.dot(take[c].astype(BF16), stack[c].astype(BF16), preferred_element_type=F32)
        listed[c * slab : (c + 1) * slab, :] = found.astype(BF16)
    block = dot_exact(own_take[...], blocks[...])
    lane = lax.broadcasted_iota(jnp.int32, (slab, slab), 1) // 6
    module = lax.broadcasted_iota(jnp.int32, (slab, slab), 0) // 6
    inverse = jnp.where(lane == module, jnp.concatenate([block] * modules, axis=1), 0.0)
    cuts = split(QUARTER * dot_exact(weights[...], inverse), 3)
    for k, (part, _) in enumerate(PAIRS):
        pull[:, k * slab : (k + 1) * slab] = cuts[part].astype(BF16)


def listed_parts(arrived, own_rider, other, take, own_take, weights, slab, lag_rows):
    rows, cols = len(arrived), take.shape[0]
    lines, lanes = own_rider.shape
    return call(
        functools.partial(listed_kernel, rows, cols, slab, lag_rows),
        (
            jax.ShapeDtypeStruct((cols * slab, lag_rows), BF16),
            jax.ShapeDtypeStruct((weights.shape[0], len(PAIRS) * slab), BF16),
        ),
        [VMEM] * (rows + 5),
        (*arrived, own_rider, other, take, own_take, weights),
        4 * take.size * lag_rows, 4 * take.size,
        [
            pltpu.VMEM((lines, lanes), F32),
            pltpu.VMEM((cols, own_take.shape[1], lag_rows), F32),
            pltpu.VMEM((own_take.shape[1], 6), F32),
        ],
    )


def settled_gaps_kernel(rows, *refs):
    arrived, (own_take, weights, out, held) = refs[:rows], refs[rows:]
    size = own_take.shape[1] // rows
    slab = own_take.shape[0]
    for d in range(rows):
        cuts = arrived[d][slab:, :].astype(F32)
        held[d * size : (d + 1) * size, :] = cuts[size : 2 * size, :] + cuts[0:size, :]
    out[...] = dot_exact(weights[...], dot_exact(own_take[...], held[...]))


def settled_gaps(arrived, own_take, weights):
    rows, reals = len(arrived), arrived[0].shape[1]
    return call(
        functools.partial(settled_gaps_kernel, rows),
        jax.ShapeDtypeStruct((weights.shape[0], reals), F32),
        [VMEM] * (rows + 2),
        (*arrived, own_take, weights),
        12 * weights.size * reals, 4 * weights.shape[0] * reals,
        [pltpu.VMEM((own_take.shape[1], reals), F32)],
    )


def end_kernel(cols, pieces, *refs):
    parts = refs[:cols]
    settled, inverse, known, pull, v_out, out, v_done, done, stack, sems = refs[cols:]
    slab = settled.shape[0]
    lines = known.shape[0] // pieces
    cuts = split(summed(parts, slab, slab), 3)
    for k, (_, part) in enumerate(PAIRS):
        stack[k * slab : (k + 1) * slab, :] = cuts[part].astype(BF16)
    copies = []
    for i in range(pieces):
        at = pl.ds(i * lines, lines)
        done[at, :] = known[at, :] - jnp.dot(
            pull[at, :], stack[...], preferred_element_type=F32
        )
        copies.append(pltpu.make_async_copy(done.at[at], out.at[at], sems.at[i]))
        copies[-1].start()
        if i == 0:
            push = dot_exact(inverse[...], summed(parts, 0, slab))
            v_done[...] = settled[...] - 0.5 * DT * push
            copies.append(pltpu.make_async_copy(v_done, v_out, sems.at[pieces]))
            copies[-1].start()
    for copy in copies:
        copy.wait()


def end(parts, settled, inverse, known, pull, pieces):
    hbm = pl.BlockSpec(memory_space=pltpu.MemorySpace.HBM)
    v_shape = jax.ShapeDtypeStruct(settled.shape, F32)
    shape = jax.ShapeDtypeStruct(known.shape, F32)
    return pl.pallas_call(
        functools.partial(end_kernel, len(parts), pieces),
        out_shape=(v_shape, shape),
        in_specs=[VMEM] * (len(parts) + 4),
        out_specs=(hbm, hbm),
        scratch_shapes=[
            pltpu.VMEM(settled.shape, F32),
            pltpu.VMEM(known.shape, F32),
            pltpu.VMEM((len(PAIRS) * settled.shape[0], settled.shape[1]), BF16),
            pltpu.SemaphoreType.DMA((pieces + 1,)),
        ],
        compiler_params=pltpu.CompilerParams(vmem_limit_bytes=16 << 20),
        cost_estimate=pl.CostEstimate(
            flops=12 * pull.size * settled.shape[1], bytes_accessed=8 * known.size, transcendentals=0
        ),
    )(*parts, settled, inverse, known, pull)


def diagonals_kernel(*refs):
    half = len(refs) // 2
    for blocks, out in zip(refs[:half], refs[half:]):
        modules = blocks.shape[1]
        width = 6 * modules
        lane = lax.broadcasted_iota(jnp.int32, (modules, width), 1) // 6
        module = lax.broadcasted_iota(jnp.int32, (modules, width), 0)
        for i in range(6):
            spread = jnp.concatenate([blocks[i]] * modules, axis=1)
            out[pl.ds(i, modules, stride=6), :] = jnp.where(lane == module, spread, 0.0)


def diagonals(*matrices):
    width = 6 * matrices[0].shape[0]
    shape = jax.ShapeDtypeStruct((width, width), F32)
    return call(
        diagonals_kernel, (shape,) * len(matrices), [VMEM] * len(matrices),
        tuple(m.transpose(1, 0, 2) for m in matrices), 100 * width * width, 16 * width * width,
    )


def plan_kernel(rows, cols, capacity, size, *refs):
    owned, lags, blocks = refs[:3]
    riders = refs[3 : 3 + rows]
    own_rider, send, take, own_take, turned, sends, coef, held = refs[3 + rows :]
    modules = send.shape[1] // 6
    row, col = lax.axis_index("row"), lax.axis_index("col")
    slab, lag_rows = modules * 6, turned.shape[2]
    for n in range(turned.shape[0]):
        turned[n] = lags[n * lag_rows : (n + 1) * lag_rows, :].T
    shape = (size, slab)
    i = lax.broadcasted_iota(jnp.int32, shape, 0)
    j = lax.broadcasted_iota(jnp.int32, shape, 1)
    wide = (slab, rows * size)
    p = lax.broadcasted_iota(jnp.int32, wide, 0)
    q = lax.broadcasted_iota(jnp.int32, wide, 1)
    for c in range(cols):
        home = (row * cols + c) * modules
        for d in range(rows):
            first = (sends_to(row, d, rows) * cols + c) * modules
            wanted = jnp.full(shape, -1, jnp.int32)
            for k in range(modules):
                local = owned[first + k] - home
                here = (local >= 0) & (local < modules)
                wanted = jnp.where((i // 6 == k % capacity) & here, local, wanted)
            hit = (wanted == j // 6) & (i % 6 == j % 6)
            sends[c, d * size : (d + 1) * size, :] = jnp.where(hit, 1.0, 0.0)
        place = p % 6
        for k in range(modules):
            source = owned[home + k] // (cols * modules)
            d = source ^ row if rows & (rows - 1) == 0 else (row + rows - source) % rows
            place = place + jnp.where(p // 6 == k, d * size + k % capacity * 6, 0)
        take[c] = jnp.where(place == q, 1.0, 0.0)
        picked = jnp.dot(
            sends[c].astype(BF16),
            turned[0, c * slab : (c + 1) * slab, :],
            preferred_element_type=F32,
        )
        for d in range(rows):
            held[d, c * size : (c + 1) * size, 0:lag_rows] = picked[d * size : (d + 1) * size, :]
    send[...] = sends[col]
    own_take[...] = take[col]
    for k in range(6):
        coef[pl.ds(k, modules, stride=6), :] = blocks[k]
    cuts = jnp.concatenate(split(dot_exact(send[...], coef[...]), 3), axis=1)
    part = riders[0].shape[0]
    first = 0
    if part < held.shape[1]:
        first = pl.multiple_of(lax.axis_index("sea") * part, 8)
    for d in range(rows):
        for at in range(0, held.shape[1], part):
            held[d, at : at + size, lag_rows : lag_rows + 18] = cuts[d * size : (d + 1) * size, :]
        riders[d][...] = held[d, pl.ds(first, part), :].astype(BF16)
    own_rider[...] = held[0].astype(BF16)


def gap_map_kernel(links, arms, inverse, stiff, send, weights, early, late, table):
    modules = weights.shape[1] // 6
    points = links.shape[0] // modules
    row, col = lax.axis_index("row"), lax.axis_index("col")
    cols = lax.axis_size("col")
    slab = modules * 6
    count = modules * points
    table[:, 0:3] = arms[...]
    position = lax.broadcasted_iota(jnp.int32, (count, 1), 0)
    table[:, 3:4] = (position // points * 6).astype(F32)
    own = table[...]
    first_point = (row * cols + col) * count
    point = lax.broadcasted_iota(jnp.int32, (count, count), 1)
    meets = jnp.where(links[...] - first_point == point, 1.0, 0.0)
    partner = dot_exact(meets, own)
    deep = (count, slab)
    column = lax.broadcasted_iota(jnp.int32, deep, 1)
    total = [None] * 3
    for sign, side in ((1.0, own), (-1.0, partner)):
        mode = column - (side[:, 3:4] + 0.5).astype(jnp.int32)
        e = [jnp.broadcast_to(sign * side[:, c : c + 1], deep) for c in range(3)]
        for c in range(3):
            up, down = (c + 1) % 3, (c + 2) % 3
            value = jnp.where(mode == c, sign, 0.0)
            value = jnp.where(mode == 3 + up, e[down], value)
            value = jnp.where(mode == 3 + down, -e[up], value)
            total[c] = value if total[c] is None else total[c] + value
    for m in range(modules):
        for c in range(3):
            start = (m * 3 + c) * points
            weights[start : start + points, :] = total[c][m * points : (m + 1) * points, :]
    press = dot_exact(send[...], QUARTER * inverse[...])
    drift = send[...] - dot_exact(press, stiff[...])
    early[:, 0:slab] = drift
    early[:, slab:] = press
    late[:, 0:slab] = dot_exact((2 * QUARTER + 0.25 * DT) * drift, inverse[...])
    late[:, slab:] = -press


def gap_map(links, arms, inverse, stiff, send):
    modules, points = links.shape
    slab = 6 * modules
    wide = jax.ShapeDtypeStruct((send.shape[0], 2 * slab), F32)
    return call(
        gap_map_kernel,
        (jax.ShapeDtypeStruct((modules * 3 * points, slab), F32), wide, wide),
        [VMEM] * 5,
        (links.reshape(-1, 1), arms.transpose(0, 2, 1).reshape(-1, 3), inverse, stiff, send),
        12 * (modules * points) ** 2 * 4, 16 * modules * 3 * points * slab,
        [pltpu.VMEM((modules * points, 4), F32)],
    )


def plan(owned, lags, solve_inverse, rows, cols, lag_rows, reals, shares):
    modules = solve_inverse.shape[0]
    slab, block = modules * 6, lags.shape[1]
    capacity = 2 * modules // rows
    size = -(-capacity * 6 // 8) * 8
    lines, lanes = cols * size, max(reals, lag_rows + 18)
    out = call(
        functools.partial(plan_kernel, rows, cols, capacity, size),
        (jax.ShapeDtypeStruct((lines // shares, lanes), BF16),) * rows
        + (
            jax.ShapeDtypeStruct((lines, lanes), BF16),
            jax.ShapeDtypeStruct((rows * size, slab), F32),
            jax.ShapeDtypeStruct((cols, slab, rows * size), F32),
            jax.ShapeDtypeStruct((slab, rows * size), F32),
            jax.ShapeDtypeStruct((2, block, lag_rows), BF16),
        ),
        [SMEM, VMEM, VMEM],
        (owned, lags, solve_inverse.transpose(1, 0, 2)),
        4 * rows * cols * size * slab * lag_rows, 16 * rows * lines * lanes,
        [
            pltpu.VMEM((cols, rows * size, slab), F32),
            pltpu.VMEM((slab, 6), F32),
            pltpu.VMEM((rows, lines, lanes), F32),
        ],
    )
    return out[:rows], *out[rows:]


def after(value, *others):
    return lax.optimization_barrier((value, *others))[0]


def body(
    kernel,
    history,
    displacement,
    velocity,
    acceleration,
    excitation,
    solve_inverse,
    stiffness,
    owned,
    links,
    arms,
):
    rows, cols = lax.axis_size("row"), lax.axis_size("col")
    steps = excitation.shape[0]
    slab, reals = velocity.shape
    modules, points = links.shape
    x, v, a = displacement, velocity, acceleration
    arrived = exchange([v] * rows, "row")
    lags, past, base = known_force(
        kernel.reshape(-1, kernel.shape[3]), history.reshape(-1, reals), rows * slab
    )
    inverse, stiff = diagonals(solve_inverse, stiffness)
    predicted, load = prepare(x, v, a, excitation[0], stiff)
    pieces, newest = first_force(lags, arrived, base, slab, cols)
    shares = 2 if lax.axis_size("sea") == 2 and cols % 2 == 0 else 1
    riders, own_rider, send, take, own_take, turned = plan(
        after(owned, pieces[0]), lags, solve_inverse, rows, cols, rows * slab, reals, shares
    )
    parts = exchange(pieces, "col")
    x, v, a, messages = first_advance(parts, predicted, v, a, load, inverse, riders)
    arrived = exchange(messages, "row")
    predicted, load = prepare(x, v, a, excitation[1], stiff)
    weights, early, late = gap_map(after(links, v), arms, inverse, stiff, send)
    drifted = drift(predicted, v, a, excitation[2], early)
    bases = later_forces(lags, past, after(newest, v), steps - 1)
    pieces = force_pieces(turned, arrived, bases, slab, cols)
    other = jnp.concatenate([after(t, pieces[0])[slab:] for t in arrived[1:]])
    if shares == 2:
        other = lax.ppermute(other, "sea", [(0, 1), (1, 0)])
    parts = exchange(pieces, "col")
    listed, pull = listed_parts(
        arrived, own_rider, other, take, own_take, weights, slab, rows * slab
    )
    v, a, rest, messages = last_advance(parts, v, a, load, inverse, drifted, late, rows)
    arrived = exchange(messages, "row")
    settled = settled_velocity(predicted, v, a, excitation[2], rest, inverse, stiff)
    pieces = last_force(turned, listed, arrived, slab, cols)
    parts = exchange(pieces, "col")
    known = settled_gaps(arrived, own_take, weights)
    v, out = end(parts, settled, inverse, known, pull, 2 if modules % 2 == 0 else 1)
    return v, out.reshape(modules, 3, points, reals).transpose(0, 2, 1, 3)


def solution(mesh):
    placed = (
        P(None, None, "col", "row"),
        P(None, None, "col", "sea"),
        P(("row", "col"), "sea"),
        P(("row", "col"), "sea"),
        P(("row", "col"), "sea"),
        P(None, ("row", "col"), "sea"),
        P(("row", "col"), None, None),
        P(("row", "col"), None, None),
        P(),
        P(("row", "col"), None),
        P(("row", "col"), None, None),
    )
    return jax.shard_map(
        body,
        mesh=mesh,
        in_specs=placed,
        out_specs=(P(("row", "col"), "sea"), P(("row", "col"), None, None, "sea")),
        check_vma=False,
    )
```
